128 devices in a mesh: gx: 16 (over x, z), gy: 8 (over y, core).
Axes of the slice: x: 4, y: 4, z: 4, core: 2. Of those that a mesh axis runs over, the one named last changes fastest.
Arguments:
- features: bfloat16 [262144, 128], P(('gx', 'gy')), may hold values from -6 to 6
- weights: bfloat16 [27, 128, 128], replicated, may hold values from -0.125 to 0.125
- rulebook: int32 [27, 262144], P(None, ('gx', 'gy')), may hold values from 0 to 2560, as said below
- owner_map: int32 [262144, 1], P(('gx', 'gy')), may hold values from 0 to 127, as said below
- coarse_slot: int32 [262144], P(('gx', 'gy')), may hold values from 0 to 255
- row_count: int32 [128], P(('gx', 'gy')), may hold values from 1 to 2048, 163840 in all
- coarse_grad: bfloat16 [32768, 128], P(('gx', 'gy')), may hold values from -6 to 6
Outputs:
- pooled: bfloat16 [32768, 128], P(('gx', 'gy'))
- weight_grad: float32 [27, 128, 128], replicated
- feature_grad: bfloat16 [262144, 128], P(('gx', 'gy'))
The draws below stay inside these ranges and needn't reach their ends.
Inputs may be any that keep to these rules, and one draw needn't show every extreme that they name: `rulebook`: entries below 2048 name a row of the same block, entries 2048 to 2559 a row of its cycle, and 2560 means that the offset has no neighbour. For each offset, the entries of an aligned block of 128 output rows that are not 2560 all lie in one aligned block of 128 table rows. `owner_map`: every row of block (bx, by) names block (bx + dx mod 16, by + dy mod 8) with dx and dy in -1, 0, 1; exactly 256 rows of each block name the block itself, and no owner is named by more than 256 rows of one block.
All inputs are finite; a program needn't handle non-finite values. No bound on the sum of `row_count` on one device may be relied on, other than what follows from the above.
Results may differ from the reference program's by a relative error of at most 0.0048.
Values may be sent and summed in bfloat16 or wider, within the bound.
No kernel may reach another device: no remote copies, remote signals or barrier semaphores. Data moves between devices by JAX's collectives and lax.ppermute only.
A program may use at most 64 MiB of HBM per device.

```python
import math
import jax
import jax.numpy as jnp
import numpy as np
from jax import lax

C = 128
KVOL = 27
VOX_DEV = 2048
RBLK = 128
FACE = 32
EXT = 2560
COARSE_DEV = 256
CAP = 256
VOXELS = 262144
COARSE = 32768
N_GX = 16
N_GY = 8
DEVICES = 128


def draw_rulebook(key, part):
    first_key, second_key, third_key = jax.random.split(key, 3)
    out_blocks = VOXELS // RBLK
    valid_blocks = (EXT + RBLK - 1) // RBLK
    source_block = jax.random.randint(first_key, (KVOL, out_blocks, 1), 0, valid_blocks)
    inside = jax.random.randint(second_key, (KVOL, out_blocks, RBLK), 0, RBLK)
    target = source_block * RBLK + inside
    missing = jax.random.randint(third_key, (KVOL, out_blocks, RBLK), 0, 5) < 2
    result = jnp.where(missing | (target >= EXT), EXT, target)
    return result.reshape(KVOL, VOXELS).astype(jnp.int32)


def draw_owner_map(key, part):
    block_keys = jax.random.split(jax.random.fold_in(key, 7), DEVICES)
    orders = jax.vmap(lambda block_key: jax.random.permutation(block_key, VOX_DEV))(block_keys)
    rows_index = jnp.arange(DEVICES, dtype=jnp.int32)[:, None]
    ranked = jnp.zeros((DEVICES, VOX_DEV), jnp.int32).at[rows_index, orders].set(jnp.arange(VOX_DEV, dtype=jnp.int32)[None, :])
    beside_all = (ranked - CAP) % 8
    beside_all = jnp.where(beside_all >= 4, beside_all + 1, beside_all)
    place = jnp.where(ranked < CAP, 4, beside_all)
    step_x = place // 3 - 1
    step_y = place % 3 - 1
    block_x = rows_index // N_GY
    block_y = rows_index % N_GY
    owner = (block_x + step_x) % N_GX * N_GY + (block_y + step_y) % N_GY
    return owner.reshape(VOXELS, 1).astype(jnp.int32)


def with_ends(entries, own_key, least, top_value):
    dims = entries.shape
    spot = [jax.random.randint(jax.random.fold_in(own_key, axis), (), 0, dims[axis]) for axis in range(len(dims))]
    entries = entries.at[tuple(spot)].set(least)
    longest = dims.index(max(dims))
    spot[longest] = (spot[longest] + 1) % dims[longest]
    return entries.at[tuple(spot)].set(top_value)


def block_levels(key, extent, shards, low, high):
    def one(position, parts):
        steps = jax.random.uniform(jax.random.fold_in(jax.random.fold_in(key, 6), position), (parts,), jnp.float32, low / len(shards), high / len(shards))
        return jnp.repeat(jnp.exp(steps), extent[position] // parts).reshape((-1,) + (1,) * (len(extent) - position - 1))

    level = one(*shards[0])
    for cut in shards[1:]:
        level = level * one(*cut)
    return level


def length_profile(count, total, limit, lean):
    portions = [(1 << 20) // math.isqrt(standing ** lean) + 1 for standing in range(2, count + 1)]
    spare, counts = total - limit - (count - 1), [1] * (count - 1)
    while spare > 0:
        movable = [i for i in range(count - 1) if counts[i] < limit]
        pool, budget = sum([portions[i] for i in movable]), spare
        for i in movable:
            extra = min(limit - counts[i], max(1, budget * portions[i] // pool), spare)
            counts[i] = counts[i] + extra
            spare = spare - extra
    return np.array([limit] + counts)


def uneven(own_key, count, total, reach, slope):
    if count == 2:
        one = jax.random.randint(own_key, (), max(1, total - reach), min(reach, total - 1) + 1)
        return jnp.stack([one, total - one])
    sizes = jnp.asarray(length_profile(count, total, reach, slope), jnp.int32)
    pairs = (count - 1) // 2
    source_of, taker = sizes[1:1 + 2 * pairs:2], sizes[2:2 + 2 * pairs:2]
    margin = jnp.minimum(source_of - 1, reach - taker)
    passed = jax.random.randint(jax.random.fold_in(own_key, 1), (pairs,), 0, 1 << 20) % (margin + 1)
    sizes = sizes.at[1:1 + 2 * pairs:2].set(source_of - passed).at[2:2 + 2 * pairs:2].set(taker + passed)
    return sizes[jax.random.permutation(jax.random.fold_in(own_key, 2), count)]


def scatter_about(rng, shape, deviation, bound, cuts=(), kind=jnp.bfloat16):
    drawn = jax.random.normal(rng, shape, jnp.float32) * deviation
    if len(cuts) > 0:
        drawn = block_levels(rng, shape, cuts, -0.22, 0.18) * drawn
    return jnp.clip(drawn, min=-bound, max=bound).astype(kind)


def setup_inputs(seed: int = 0) -> dict:
    seeds = jax.random.split(jax.random.key(seed), 8)
    return {
        "features": scatter_about(seeds[0], (VOXELS, C), 1.0, 6.0, ((0, 128),)),
        "weights": scatter_about(seeds[1], (KVOL, C, C), (16 * C) ** -0.5, 0.125),
        "rulebook": draw_rulebook(jax.random.fold_in(seeds[7], 71), 0),
        "owner_map": draw_owner_map(jax.random.fold_in(seeds[7], 71), 0),
        "coarse_slot": with_ends(jax.random.randint(seeds[4], (VOXELS,), 0, COARSE_DEV), jax.random.fold_in(seeds[4], 1), 0, COARSE_DEV - 1).astype(jnp.int32),
        "row_count": uneven(seeds[5], DEVICES, DEVICES * VOX_DEV * 5 // 8, VOX_DEV, 2).astype(jnp.int32),
        "coarse_grad": scatter_about(seeds[6], (COARSE, C), 1.0, 6.0, ((0, 128),)),
    }


def reference(features, weights, rulebook, owner_map, coarse_slot, row_count, coarse_grad):
    blocks_x = N_GX
    blocks_y = N_GY
    devices = blocks_x * blocks_y
    active = jnp.arange(VOX_DEV, dtype=jnp.int32)[None, :] < row_count[:, None]
    feats = features.reshape(devices, VOX_DEV, C)
    masked = jnp.where(active[:, :, None], feats, jnp.zeros((), jnp.bfloat16)).astype(jnp.bfloat16)
    faces = masked[:, :4 * FACE].reshape(blocks_x, blocks_y, 2, 2, FACE, C)
    faces = faces.transpose(0, 2, 1, 3, 4, 5).reshape(2 * blocks_x, 2 * blocks_y, FACE, C)
    grid = jnp.pad(faces, ((1, 1), (1, 1), (0, 0), (0, 0)))
    rules = rulebook.reshape(KVOL, devices, VOX_DEV).transpose(1, 0, 2)

    def table_of(device):
        place_x = (device // blocks_y).astype(jnp.int32)
        place_y = (device % blocks_y).astype(jnp.int32)
        zero = jnp.zeros((), jnp.int32)
        cycle = lax.dynamic_slice(grid, (2 * place_x, 2 * place_y, zero, zero), (4, 4, FACE, C))
        return jnp.concatenate([masked[device], cycle.reshape(16 * FACE, C), jnp.zeros((1, C), jnp.bfloat16)], 0)

    def forward_one(device):
        table = table_of(device)

        def offset_step(summed, offset_pair):
            offset_rows, offset_weight = offset_pair
            picked = jnp.take(table, offset_rows, axis=0)
            return (summed + jnp.dot(picked, offset_weight, preferred_element_type=jnp.float32), None)
        preact, _ = lax.scan(offset_step, jnp.zeros((VOX_DEV, C), jnp.float32), (rules[device], weights))
        return preact
    every = jnp.arange(devices, dtype=jnp.int32)
    preact = lax.map(forward_one, every)
    hidden = jnp.where(active[:, :, None], masked.astype(jnp.float32) + jax.nn.silu(preact), 0.0).astype(jnp.bfloat16)
    active_flat = active.reshape(VOXELS)
    target = jnp.where(active_flat, owner_map[:, 0] * COARSE_DEV + coarse_slot, COARSE).astype(jnp.int32)
    pooled = jax.ops.segment_sum(hidden.reshape(VOXELS, C).astype(jnp.float32), target, num_segments=COARSE + 1)[:COARSE].astype(jnp.bfloat16)
    grad_table = jnp.concatenate([coarse_grad, jnp.zeros((1, C), jnp.bfloat16)], 0)
    up_grad = jnp.take(grad_table, target, axis=0).reshape(devices, VOX_DEV, C)
    sigmoid_pre = jax.nn.sigmoid(preact)
    pre_grad = (up_grad.astype(jnp.float32) * (sigmoid_pre * (1.0 + preact * (1.0 - sigmoid_pre)))).astype(jnp.bfloat16)

    def backward_one(weight_total, device):
        table = table_of(device)
        block_grad = pre_grad[device]

        def offset_step(table_grad, offset_pair):
            offset_rows, offset_weight = offset_pair
            picked = jnp.take(table, offset_rows, axis=0)
            weight_term = lax.dot_general(picked, block_grad, (((0,), (0,)), ((), ())), preferred_element_type=jnp.float32)
            spread = jnp.dot(block_grad, offset_weight.T, preferred_element_type=jnp.float32)
            return (table_grad.at[offset_rows].add(spread), weight_term)
        table_grad, weight_terms = lax.scan(offset_step, jnp.zeros((EXT + 1, C), jnp.float32), (rules[device], weights))
        return (weight_total + weight_terms, (table_grad[:VOX_DEV], table_grad[VOX_DEV:EXT].reshape(4, 4, FACE, C)))
    weight_total, (local_grad, cycle_grad) = lax.scan(backward_one, jnp.zeros((KVOL, C, C), jnp.float32), every)
    cycle_grad = cycle_grad.reshape(blocks_x, blocks_y, 4, 4, FACE, C)
    grid_grad = jnp.zeros((2 * blocks_x + 2, 2 * blocks_y + 2, FACE, C), jnp.float32)
    for place_i in range(4):
        for place_j in range(4):
            grid_grad = grid_grad.at[place_i:place_i + 2 * blocks_x:2, place_j:place_j + 2 * blocks_y:2].add(cycle_grad[:, :, place_i, place_j])
    face_grad = grid_grad[1:-1, 1:-1].reshape(blocks_x, 2, blocks_y, 2, FACE, C).transpose(0, 2, 1, 3, 4, 5).reshape(devices, 4 * FACE, C)
    total_grad = local_grad + up_grad.astype(jnp.float32)
    total_grad = total_grad.at[:, :4 * FACE].add(face_grad)
    feature_grad = jnp.where(active[:, :, None], total_grad, 0.0).astype(jnp.bfloat16).reshape(VOXELS, C)
    weight_grad = weight_total * (1.0 / math.sqrt(VOXELS))
    return (pooled, weight_grad, feature_grad)
```

```python
import math

import jax
import jax.numpy as jnp
from jax import lax
from jax.experimental import pallas as pl
from jax.experimental.pallas import tpu as pltpu
from jax.sharding import PartitionSpec as P

BF = jnp.bfloat16
F32 = jnp.float32
AXES = ("gx", "gy")
C = 128
KV = 27
VOX = 2048
BLK = 128
NQ = VOX // BLK
FACE = 32
CYC = 16 * FACE
EXT = VOX + CYC
NLOC = VOX // BLK
NTAB = EXT // BLK
COARSE = 256
NT = 9 * COARSE
FAR = 1 << 14
GROUP = 8
VMEM_LIMIT = 56 << 20


def onehot(cond):
    return jnp.where(cond, 1.0, 0.0).astype(BF)


def params(**kw):
    return pltpu.CompilerParams(vmem_limit_bytes=VMEM_LIMIT, **kw)


def local_kernel(sb, rb, table, w, acc, pairs, count, picked):
    g = pl.program_id(0)
    lanes = lax.broadcasted_iota(jnp.int32, (BLK, BLK), 1)

    @pl.when(g == 0)
    def _():
        count[0] = 0

    def body(qq, n):
        q = g * 4 + qq
        r0 = pl.multiple_of(qq * BLK, BLK)
        cols = jnp.concatenate([rb[:, pl.ds(r0, BLK)], jnp.zeros((BLK - KV, BLK), jnp.int32)], 0).T
        for k in range(KV):
            s = sb[k, q]
            local = s < NLOC
            pairs[n] = k * NQ + q
            n = n + jnp.where(local, 0, 1)
            base = jnp.where(local, s * BLK, -FAR)
            t0 = pl.multiple_of(jnp.minimum(s, NLOC - 1) * BLK, BLK)
            col = jnp.broadcast_to(cols[:, k : k + 1], (BLK, BLK)) - base
            got = jnp.dot(onehot(col == lanes), table[pl.ds(t0, BLK), :], preferred_element_type=F32)
            picked[pl.ds(r0, BLK), k * C : (k + 1) * C] = got.astype(BF)
        return n

    count[0] = lax.fori_loop(0, 4, body, count[0])
    acc[...] = jnp.dot(picked[...], w[...], preferred_element_type=F32)


def local_call(sb, rb, table, w):
    smem = pl.BlockSpec(memory_space=pltpu.SMEM)
    return pl.pallas_call(
        local_kernel,
        grid=(NQ // 4,),
        in_specs=[
            smem,
            pl.BlockSpec((KV, 4 * BLK), lambda g: (0, g)),
            pl.BlockSpec((VOX, C), lambda g: (0, 0)),
            pl.BlockSpec((KV * C, C), lambda g: (0, 0)),
        ],
        out_specs=[pl.BlockSpec((4 * BLK, C), lambda g: (g, 0)), smem, smem],
        out_shape=[
            jax.ShapeDtypeStruct((VOX, C), F32),
            jax.ShapeDtypeStruct((KV * NQ + GROUP,), jnp.int32),
            jax.ShapeDtypeStruct((1,), jnp.int32),
        ],
        scratch_shapes=[pltpu.VMEM((4 * BLK, KV * C), BF)],
        compiler_params=params(),
        name="conv_local",
    )(sb, rb, table, w)


def remote_kernel(sb, pairs, count, rows, rb, cyc, w, acc_in, table, tgt, coarse, hidden, up, pre, acc):
    acc[...] = acc_in[...]
    n = count[0]
    subl = lax.broadcasted_iota(jnp.int32, (BLK, BLK), 0)
    lanes = lax.broadcasted_iota(jnp.int32, (BLK, BLK), 1)

    def group(i, carry):
        for j in range(GROUP):
            idx = i * GROUP + j
            valid = idx < n
            e = jnp.where(valid, pairs[jnp.minimum(idx, n - 1)], 0)
            k = e // NQ
            q = e % NQ
            s = jnp.where(valid, jnp.minimum(sb[k, q], NTAB - 1), NLOC)
            base = jnp.where(valid, s * BLK, -FAR)
            r0 = pl.multiple_of(q * BLK, BLK)
            t0 = pl.multiple_of((s - NLOC) * BLK, BLK)
            row = jnp.broadcast_to(rb[pl.ds(e, 1), :], (BLK, BLK)) - base
            got = lax.dot_general(
                onehot(row == subl), cyc[pl.ds(t0, BLK), :], (((0,), (0,)), ((), ())),
                preferred_element_type=F32,
            ).astype(BF)
            acc[pl.ds(r0, BLK), :] += jnp.dot(got, w[k], preferred_element_type=F32)
        return carry

    lax.fori_loop(0, (n + GROUP - 1) // GROUP, group, 0)

    def point(q, carry):
        r0 = pl.multiple_of(q * BLK, BLK)
        at = pl.ds(r0, BLK)
        col = jnp.broadcast_to(tgt[pl.ds(q, 1), :], (BLK, BLK)).T
        sel = jnp.concatenate([onehot(col - t * BLK == lanes) for t in range(NT // BLK)], 1)
        grad = jnp.dot(sel, coarse[...], preferred_element_type=F32)
        v = acc[at, :]
        sg = 1.0 / (1.0 + jnp.exp(-v))
        up[at, :] = grad.astype(BF)
        pre[at, :] = (grad * (sg * (1.0 + v * (1.0 - sg)))).astype(BF)
        out = table[at, :].astype(F32) + v * sg
        hidden[at, :] = jnp.where(subl + r0 < rows[0], out, 0.0).astype(BF)
        return carry

    lax.fori_loop(0, NQ, point, 0)


def remote_call(sb, pairs, count, rows, rb, cyc, w, acc, table, tgt, coarse):
    smem = pl.BlockSpec(memory_space=pltpu.SMEM)
    vmem = pl.BlockSpec(memory_space=pltpu.VMEM)
    return pl.pallas_call(
        remote_kernel,
        in_specs=[smem] * 4 + [vmem] * 7,
        out_specs=[vmem] * 3,
        out_shape=[jax.ShapeDtypeStruct((VOX, C), BF)] * 3,
        scratch_shapes=[pltpu.VMEM((VOX, C), F32)],
        compiler_params=params(),
        name="conv_remote",
    )(sb, pairs, count, rows, rb, cyc, w, acc, table, tgt, coarse)


def weight_kernel(sb, rb, pre, table, cyc, summed, wg, flipped):
    subl = lax.broadcasted_iota(jnp.int32, (BLK, BLK), 0)
    for b in range(NTAB):
        src = table[b * BLK : (b + 1) * BLK, :] if b < NLOC else cyc[(b - NLOC) * BLK : (b - NLOC + 1) * BLK, :]
        flipped[:, b * BLK : (b + 1) * BLK] = src.T

    def scatter(q, carry):
        r0 = pl.multiple_of(q * BLK, BLK)
        grads = pre[pl.ds(r0, BLK), :]
        for k in range(KV):
            base = jnp.minimum(sb[k, q], NTAB - 1) * BLK
            row = jnp.broadcast_to(rb[k : k + 1, pl.ds(r0, BLK)], (BLK, BLK)) - base
            got = jnp.dot(onehot(row == subl), grads, preferred_element_type=F32)
            summed[k, pl.ds(r0, BLK), :] = got.astype(BF)
        return carry

    lax.fori_loop(0, NQ, scatter, 0)

    def contract(k, carry):
        parts = []
        for q in range(NQ):
            t0 = pl.multiple_of(jnp.minimum(sb[k, q], NTAB - 1) * BLK, BLK)
            parts.append(flipped[:, pl.ds(t0, BLK)])
        got = jnp.dot(jnp.concatenate(parts, 1), summed[k], preferred_element_type=F32)
        wg[pl.ds(pl.multiple_of(k * C, C), C), :] = got.astype(BF)
        return carry

    lax.fori_loop(0, KV, contract, 0)
    wg[KV * C :, :] = jnp.zeros((wg.shape[0] - KV * C, C), BF)


def weight_call(sb, rb, pre, table, cyc):
    smem = pl.BlockSpec(memory_space=pltpu.SMEM)
    vmem = pl.BlockSpec(memory_space=pltpu.VMEM)
    return pl.pallas_call(
        weight_kernel,
        in_specs=[smem] + [vmem] * 4,
        out_specs=[vmem, vmem],
        out_shape=[
            jax.ShapeDtypeStruct((KV, VOX, C), BF),
            jax.ShapeDtypeStruct((32 * C, C), BF),
        ],
        scratch_shapes=[pltpu.VMEM((C, EXT), BF)],
        compiler_params=params(),
        name="weight_grad",
    )(sb, rb, pre, table, cyc)


def table_kernel(sb, summed, w, out):
    k = pl.program_id(0)

    @pl.when(k == 0)
    def _():
        out[...] = jnp.zeros(out.shape, F32)

    got = lax.dot_general(summed[0], w[0], (((1,), (1,)), ((), ())), preferred_element_type=F32)
    for q in range(NQ):
        t0 = pl.multiple_of(jnp.minimum(sb[k, q], NTAB - 1) * BLK, BLK)
        out[pl.ds(t0, BLK), :] += got[q * BLK : (q + 1) * BLK, :]


def table_call(sb, summed, w):
    return pl.pallas_call(
        table_kernel,
        grid=(KV,),
        in_specs=[
            pl.BlockSpec(memory_space=pltpu.SMEM),
            pl.BlockSpec((1, VOX, C), lambda k: (k, 0, 0)),
            pl.BlockSpec((1, C, C), lambda k: (k, 0, 0)),
        ],
        out_specs=pl.BlockSpec((EXT, C), lambda k: (0, 0)),
        out_shape=jax.ShapeDtypeStruct((EXT, C), F32),
        compiler_params=params(),
        name="table_grad",
    )(sb, summed, w)


def pool_kernel(tgt, hidden, own, out):
    t = pl.program_id(0)
    subl = lax.broadcasted_iota(jnp.int32, (COARSE, BLK), 0) + t * COARSE
    sel = jnp.concatenate(
        [onehot(jnp.broadcast_to(tgt[q : q + 1, :], (COARSE, BLK)) == subl) for q in range(NQ)], 1
    )
    got = jnp.dot(sel, hidden[...], preferred_element_type=F32)
    out[...] = got.astype(BF)

    @pl.when(t == 4)
    def _():
        own[...] = got


def pool_call(tgt, hidden):
    return pl.pallas_call(
        pool_kernel,
        grid=(9,),
        in_specs=[
            pl.BlockSpec((NQ, BLK), lambda t: (0, 0)),
            pl.BlockSpec((VOX, C), lambda t: (0, 0)),
        ],
        out_specs=[
            pl.BlockSpec((COARSE, C), lambda t: (0, 0)),
            pl.BlockSpec((COARSE, C), lambda t: (t, 0)),
        ],
        out_shape=[jax.ShapeDtypeStruct((COARSE, C), F32), jax.ShapeDtypeStruct((NT, C), BF)],
        compiler_params=params(),
        name="pool_partial",
    )(tgt, hidden)


def shift(array, axis, step):
    size = lax.axis_size(axis)
    return lax.ppermute(array, axis, [(i, (i + step) % size) for i in range(size)])


def shards(features, weights, rulebook, owner_map, coarse_slot, row_count, coarse_grad):
    size_x, size_y = lax.axis_size("gx"), lax.axis_size("gy")
    devices = size_x * size_y
    place_x, place_y = lax.axis_index("gx"), lax.axis_index("gy")
    active = lax.iota(jnp.int32, VOX) < row_count[0]
    masked = jnp.where(active[:, None], features, jnp.zeros((), BF))

    faces = jnp.where(active[: 4 * FACE, None], features[: 4 * FACE], jnp.zeros((), BF))
    half = 2 * FACE
    from_low = shift(jnp.concatenate([faces[half:], coarse_grad], 0), "gx", 1)
    from_high = shift(jnp.concatenate([faces[:half], coarse_grad], 0), "gx", -1)
    zero = jnp.zeros((), BF)
    low_faces = jnp.where(place_x > 0, from_low[:half], zero)
    high_faces = jnp.where(place_x < size_x - 1, from_high[:half], zero)
    strip = jnp.concatenate([low_faces, faces, high_faces], 0).reshape(4, 2, FACE, C)
    coarse_x = jnp.concatenate([from_low[half:], coarse_grad, from_high[half:]], 0)
    up_y = shift(jnp.concatenate([strip[:, 1].reshape(4 * FACE, C), coarse_x], 0), "gy", 1)
    down_y = shift(jnp.concatenate([strip[:, 0].reshape(4 * FACE, C), coarse_x], 0), "gy", -1)
    below = jnp.where(place_y > 0, up_y[: 4 * FACE], zero).reshape(4, 1, FACE, C)
    above = jnp.where(place_y < size_y - 1, down_y[: 4 * FACE], zero).reshape(4, 1, FACE, C)
    cyc = jnp.concatenate([below, strip, above], 1).reshape(CYC, C)
    near = jnp.stack(
        [
            up_y[4 * FACE :].reshape(3, COARSE, C),
            coarse_x.reshape(3, COARSE, C),
            down_y[4 * FACE :].reshape(3, COARSE, C),
        ],
        1,
    ).reshape(NT, C)

    sb = jnp.min(rulebook.reshape(KV, NQ, BLK), axis=2) // BLK
    owner = owner_map[:, 0]
    step_x = (owner // size_y - place_x + 1) % size_x
    step_y = (owner % size_y - place_y + 1) % size_y
    tgt = jnp.where(active, (step_x * 3 + step_y) * COARSE + coarse_slot, -1).reshape(NQ, BLK)

    acc, pairs, count = local_call(sb, rulebook, masked, weights.reshape(KV * C, C))
    hidden, up_grad, pre_grad = remote_call(
        sb, pairs, count, row_count, rulebook.reshape(KV * NQ, BLK), cyc, weights, acc, masked, tgt, near
    )
    summed, wg = weight_call(sb, rulebook, pre_grad, masked, cyc)

    share = 32 * C // devices
    parts = lax.all_to_all(wg.reshape(devices, share, C), AXES, 0, 0, tiled=True)
    total = jnp.sum(parts.astype(F32), axis=0).astype(BF)
    spread = jnp.broadcast_to(total[None], (devices, share, C))
    every = lax.all_to_all(spread, AXES, 0, 0, tiled=True).reshape(32 * C, C)
    weight_grad = every[: KV * C].reshape(KV, C, C).astype(F32) * (1.0 / math.sqrt(VOX * devices))

    own, partial = pool_call(tgt, hidden)
    partial = partial.reshape(3, 3, COARSE, C)
    sent_low = shift(partial[0], "gx", -1)
    sent_high = shift(partial[2], "gx", 1)
    to_low = shift(jnp.stack([sent_low[0], partial[1, 0], sent_high[0]]), "gy", -1)
    to_high = shift(jnp.stack([sent_low[2], partial[1, 2], sent_high[2]]), "gy", 1)
    pooled = own + sent_low[1].astype(F32) + sent_high[1].astype(F32)
    pooled = pooled + jnp.sum(to_low.astype(F32), 0) + jnp.sum(to_high.astype(F32), 0)

    table_grad = table_call(sb, summed, weights)
    cycle_grad = table_grad[VOX:].reshape(4, 4, FACE, C)
    to_left = lax.ppermute(cycle_grad[0].astype(BF), "gx", [(i + 1, i) for i in range(size_x - 1)])
    to_right = lax.ppermute(cycle_grad[3].astype(BF), "gx", [(i, i + 1) for i in range(size_x - 1)])
    wide = jnp.stack([cycle_grad[1] + to_right.astype(F32), cycle_grad[2] + to_left.astype(F32)])
    to_down = lax.ppermute(wide[:, 0].astype(BF), "gy", [(i + 1, i) for i in range(size_y - 1)])
    to_up = lax.ppermute(wide[:, 3].astype(BF), "gy", [(i, i + 1) for i in range(size_y - 1)])
    face_grad = jnp.stack([wide[:, 1] + to_up.astype(F32), wide[:, 2] + to_down.astype(F32)], 1)
    total_grad = table_grad[:VOX] + up_grad.astype(F32)
    total_grad = total_grad.at[: 4 * FACE].add(face_grad.reshape(4 * FACE, C))
    feature_grad = jnp.where(active[:, None], total_grad, 0.0).astype(BF)
    return (pooled.astype(BF), weight_grad, feature_grad)


def solution(mesh):
    return jax.shard_map(
        shards,
        mesh=mesh,
        in_specs=(
            P(AXES, None),
            P(),
            P(None, AXES),
            P(AXES, None),
            P(AXES),
            P(AXES),
            P(AXES, None),
        ),
        out_specs=(P(AXES, None), P(), P(AXES, None)),
        check_vma=False,
    )
```

```python
import functools
import math

import jax
import jax.numpy as jnp
from jax import lax
from jax.experimental import pallas as pl
from jax.experimental.pallas import tpu as pltpu
from jax.sharding import PartitionSpec as P

BF = jnp.bfloat16
F32 = jnp.float32
AXES = ("gx", "gy")
C = 128
KV = 27
VOX = 2048
BLK = 128
NQ = VOX // BLK
FACE = 32
CYC = 16 * FACE
EXT = VOX + CYC
NLOC = VOX // BLK
NTAB = EXT // BLK
COARSE = 256
NT = 9 * COARSE
FAR = 1 << 14
GROUP = 8
VMEM_LIMIT = 56 << 20


def onehot(cond):
    return jnp.where(cond, 1.0, 0.0).astype(BF)


def params(**kw):
    return pltpu.CompilerParams(vmem_limit_bytes=VMEM_LIMIT, **kw)


def cost(micros):
    return pl.CostEstimate(flops=0, transcendentals=0, bytes_accessed=int(micros * 3.6e6))


def local_kernel(first, sb, rb, table, w, acc, pairs, count, picked):
    g = pl.program_id(0)
    lanes = lax.broadcasted_iota(jnp.int32, (BLK, BLK), 1)

    @pl.when(g == 0)
    def _():
        count[0] = 0

    def body(qq, n):
        q = first + g * 4 + qq
        r0 = pl.multiple_of(qq * BLK, BLK)
        cols = jnp.concatenate([rb[:, pl.ds(r0, BLK)], jnp.zeros((BLK - KV, BLK), jnp.int32)], 0).T
        for k in range(KV):
            s = sb[k, q]
            local = s < NLOC
            pairs[n] = k * NQ + q
            n = n + jnp.where(local, 0, 1)
            base = jnp.where(local, s * BLK, -FAR)
            t0 = pl.multiple_of(jnp.minimum(s, NLOC - 1) * BLK, BLK)
            col = jnp.broadcast_to(cols[:, k : k + 1], (BLK, BLK)) - base
            got = jnp.dot(onehot(col == lanes), table[pl.ds(t0, BLK), :], preferred_element_type=F32)
            picked[pl.ds(r0, BLK), k * C : (k + 1) * C] = got.astype(BF)
        return n

    count[0] = lax.fori_loop(0, 4, body, count[0])
    acc[...] = jnp.dot(picked[...], w[...], preferred_element_type=F32)


def local_call(first, sb, rb, table, w):
    smem = pl.BlockSpec(memory_space=pltpu.SMEM)
    return pl.pallas_call(
        functools.partial(local_kernel, first),
        grid=(NQ // 8,),
        in_specs=[
            smem,
            pl.BlockSpec((KV, 4 * BLK), lambda g: (0, g + first // 4)),
            pl.BlockSpec((VOX, C), lambda g: (0, 0)),
            pl.BlockSpec((KV * C, C), lambda g: (0, 0)),
        ],
        out_specs=[pl.BlockSpec((4 * BLK, C), lambda g: (g, 0)), smem, smem],
        out_shape=[
            jax.ShapeDtypeStruct((VOX // 2, C), F32),
            jax.ShapeDtypeStruct((KV * NQ // 2 + GROUP,), jnp.int32),
            jax.ShapeDtypeStruct((1,), jnp.int32),
        ],
        scratch_shapes=[pltpu.VMEM((4 * BLK, KV * C), BF)],
        compiler_params=params(),
        cost_estimate=cost(10),
        name="conv_local",
    )(sb, rb, table, w)


def remote_kernel(
    sb, pairs_a, count_a, pairs_b, count_b, rows, rb, cyc, w, acc_a, acc_b, table, tgt, coarse,
    hidden, up, pre, acc,
):
    acc[: VOX // 2, :] = acc_a[...]
    acc[VOX // 2 :, :] = acc_b[...]
    subl = lax.broadcasted_iota(jnp.int32, (BLK, BLK), 0)
    lanes = lax.broadcasted_iota(jnp.int32, (BLK, BLK), 1)

    def group(pairs, n, i, carry):
        for j in range(GROUP):
            idx = i * GROUP + j
            valid = idx < n
            e = jnp.where(valid, pairs[jnp.minimum(idx, n - 1)], 0)
            k = e // NQ
            q = e % NQ
            s = jnp.where(valid, jnp.minimum(sb[k, q], NTAB - 1), NLOC)
            base = jnp.where(valid, s * BLK, -FAR)
            r0 = pl.multiple_of(q * BLK, BLK)
            t0 = pl.multiple_of((s - NLOC) * BLK, BLK)
            row = jnp.broadcast_to(rb[pl.ds(e, 1), :], (BLK, BLK)) - base
            got = lax.dot_general(
                onehot(row == subl), cyc[pl.ds(t0, BLK), :], (((0,), (0,)), ((), ())),
                preferred_element_type=F32,
            ).astype(BF)
            acc[pl.ds(r0, BLK), :] += jnp.dot(got, w[k], preferred_element_type=F32)
        return carry

    for pairs, count in ((pairs_a, count_a), (pairs_b, count_b)):
        n = count[0]
        lax.fori_loop(0, (n + GROUP - 1) // GROUP, functools.partial(group, pairs, n), 0)

    def point(q, carry):
        r0 = pl.multiple_of(q * BLK, BLK)
        at = pl.ds(r0, BLK)
        col = jnp.broadcast_to(tgt[pl.ds(q, 1), :], (BLK, BLK)).T
        sel = jnp.concatenate([onehot(col - t * BLK == lanes) for t in range(NT // BLK)], 1)
        grad = jnp.dot(sel, coarse[...], preferred_element_type=F32)
        v = acc[at, :]
        sg = 1.0 / (1.0 + jnp.exp(-v))
        up[at, :] = grad.astype(BF)
        pre[at, :] = (grad * (sg * (1.0 + v * (1.0 - sg)))).astype(BF)
        out = table[at, :].astype(F32) + v * sg
        hidden[at, :] = jnp.where(subl + r0 < rows[0], out, 0.0).astype(BF)
        return carry

    lax.fori_loop(0, NQ, point, 0)


def remote_call(*args):
    smem = pl.BlockSpec(memory_space=pltpu.SMEM)
    vmem = pl.BlockSpec(memory_space=pltpu.VMEM)
    return pl.pallas_call(
        remote_kernel,
        in_specs=[smem] * 6 + [vmem] * 8,
        out_specs=[vmem] * 3,
        out_shape=[jax.ShapeDtypeStruct((VOX, C), BF)] * 3,
        scratch_shapes=[pltpu.VMEM((VOX, C), F32)],
        compiler_params=params(),
        cost_estimate=cost(15),
        name="conv_remote",
    )(*args)


def weight_kernel(sb, rb, pre, table, cyc, summed, wg, flipped):
    subl = lax.broadcasted_iota(jnp.int32, (BLK, BLK), 0)
    for b in range(NTAB):
        src = table[b * BLK : (b + 1) * BLK, :] if b < NLOC else cyc[(b - NLOC) * BLK : (b - NLOC + 1) * BLK, :]
        flipped[:, b * BLK : (b + 1) * BLK] = src.T

    def scatter(q, carry):
        r0 = pl.multiple_of(q * BLK, BLK)
        grads = pre[pl.ds(r0, BLK), :]
        for k in range(KV):
            base = jnp.minimum(sb[k, q], NTAB - 1) * BLK
            row = jnp.broadcast_to(rb[k : k + 1, pl.ds(r0, BLK)], (BLK, BLK)) - base
            got = jnp.dot(onehot(row == subl), grads, preferred_element_type=F32)
            summed[k, pl.ds(r0, BLK), :] = got.astype(BF)
        return carry

    lax.fori_loop(0, NQ, scatter, 0)

    def contract(k, carry):
        parts = []
        for q in range(NQ):
            t0 = pl.multiple_of(jnp.minimum(sb[k, q], NTAB - 1) * BLK, BLK)
            parts.append(flipped[:, pl.ds(t0, BLK)])
        got = jnp.dot(jnp.concatenate(parts, 1), summed[k], preferred_element_type=F32)
        wg[pl.ds(pl.multiple_of(k * C, C), C), :] = got.astype(BF)
        return carry

    lax.fori_loop(0, KV, contract, 0)
    wg[KV * C :, :] = jnp.zeros((wg.shape[0] - KV * C, C), BF)


def weight_call(sb, rb, pre, table, cyc):
    smem = pl.BlockSpec(memory_space=pltpu.SMEM)
    vmem = pl.BlockSpec(memory_space=pltpu.VMEM)
    return pl.pallas_call(
        weight_kernel,
        in_specs=[smem] + [vmem] * 4,
        out_specs=[vmem, vmem],
        out_shape=[
            jax.ShapeDtypeStruct((KV, VOX, C), BF),
            jax.ShapeDtypeStruct((32 * C, C), BF),
        ],
        scratch_shapes=[pltpu.VMEM((C, EXT), BF)],
        compiler_params=params(),
        cost_estimate=cost(21),
        name="weight_grad",
    )(sb, rb, pre, table, cyc)


def table_kernel(sb, summed, w, out):
    k = pl.program_id(0)

    @pl.when(k == 0)
    def _():
        out[...] = jnp.zeros(out.shape, F32)

    got = lax.dot_general(summed[0], w[0], (((1,), (1,)), ((), ())), preferred_element_type=F32)
    for q in range(NQ):
        t0 = pl.multiple_of(jnp.minimum(sb[k, q], NTAB - 1) * BLK, BLK)
        out[pl.ds(t0, BLK), :] += got[q * BLK : (q + 1) * BLK, :]


def table_call(sb, summed, w):
    return pl.pallas_call(
        table_kernel,
        grid=(KV,),
        in_specs=[
            pl.BlockSpec(memory_space=pltpu.SMEM),
            pl.BlockSpec((1, VOX, C), lambda k: (k, 0, 0)),
            pl.BlockSpec((1, C, C), lambda k: (k, 0, 0)),
        ],
        out_specs=pl.BlockSpec((EXT, C), lambda k: (0, 0)),
        out_shape=jax.ShapeDtypeStruct((EXT, C), F32),
        compiler_params=params(),
        cost_estimate=cost(21),
        name="table_grad",
    )(sb, summed, w)


def pool_kernel(tgt, hidden, own, out):
    t = pl.program_id(0)
    subl = lax.broadcasted_iota(jnp.int32, (COARSE, BLK), 0) + t * COARSE
    sel = jnp.concatenate(
        [onehot(jnp.broadcast_to(tgt[q : q + 1, :], (COARSE, BLK)) == subl) for q in range(NQ)], 1
    )
    got = jnp.dot(sel, hidden[...], preferred_element_type=F32)
    out[...] = got.astype(BF)

    @pl.when(t == 4)
    def _():
        own[...] = got


def pool_call(tgt, hidden):
    return pl.pallas_call(
        pool_kernel,
        grid=(9,),
        in_specs=[
            pl.BlockSpec((NQ, BLK), lambda t: (0, 0)),
            pl.BlockSpec((VOX, C), lambda t: (0, 0)),
        ],
        out_specs=[
            pl.BlockSpec((COARSE, C), lambda t: (0, 0)),
            pl.BlockSpec((COARSE, C), lambda t: (t, 0)),
        ],
        out_shape=[jax.ShapeDtypeStruct((COARSE, C), F32), jax.ShapeDtypeStruct((NT, C), BF)],
        compiler_params=params(),
        cost_estimate=cost(6),
        name="pool_partial",
    )(tgt, hidden)


def shift(array, axis, step):
    size = lax.axis_size(axis)
    return lax.ppermute(array, axis, [(i, (i + step) % size) for i in range(size)])


def shards(features, weights, rulebook, owner_map, coarse_slot, row_count, coarse_grad):
    size_x, size_y = lax.axis_size("gx"), lax.axis_size("gy")
    devices = size_x * size_y
    place_x, place_y = lax.axis_index("gx"), lax.axis_index("gy")
    active = lax.iota(jnp.int32, VOX) < row_count[0]
    masked = jnp.where(active[:, None], features, jnp.zeros((), BF))

    sb = jnp.min(rulebook.reshape(KV, NQ, BLK), axis=2) // BLK
    flat_w = weights.reshape(KV * C, C)

    faces = jnp.where(active[: 4 * FACE, None], features[: 4 * FACE], jnp.zeros((), BF))
    half = 2 * FACE
    from_low = shift(jnp.concatenate([faces[half:], coarse_grad], 0), "gx", 1)
    from_high = shift(jnp.concatenate([faces[:half], coarse_grad], 0), "gx", -1)
    acc_a, pairs_a, count_a = local_call(0, sb, rulebook, masked, flat_w)
    from_low, from_high, acc_a = lax.optimization_barrier((from_low, from_high, acc_a))
    zero = jnp.zeros((), BF)
    low_faces = jnp.where(place_x > 0, from_low[:half], zero)
    high_faces = jnp.where(place_x < size_x - 1, from_high[:half], zero)
    strip = jnp.concatenate([low_faces, faces, high_faces], 0).reshape(4, 2, FACE, C)
    coarse_x = jnp.concatenate([from_low[half:], coarse_grad, from_high[half:]], 0)
    sent_up = jnp.concatenate([strip[:, 1].reshape(4 * FACE, C), coarse_x], 0)
    sent_down = jnp.concatenate([strip[:, 0].reshape(4 * FACE, C), coarse_x], 0)
    rulebook_b, sent_up, sent_down = lax.optimization_barrier((rulebook, sent_up, sent_down))
    up_y = shift(sent_up, "gy", 1)
    down_y = shift(sent_down, "gy", -1)
    acc_b, pairs_b, count_b = local_call(NQ // 2, sb, rulebook_b, masked, flat_w)
    below = jnp.where(place_y > 0, up_y[: 4 * FACE], zero).reshape(4, 1, FACE, C)
    above = jnp.where(place_y < size_y - 1, down_y[: 4 * FACE], zero).reshape(4, 1, FACE, C)
    cyc = jnp.concatenate([below, strip, above], 1).reshape(CYC, C)
    near = jnp.concatenate([up_y[4 * FACE :], coarse_x, down_y[4 * FACE :]], 0)

    owner = owner_map[:, 0]
    step_x = (owner // size_y - place_x + 1) % size_x
    step_y = (owner % size_y - place_y + 1) % size_y
    tgt = jnp.where(active, (step_y * 3 + step_x) * COARSE + coarse_slot, -1).reshape(NQ, BLK)

    hidden, up_grad, pre_grad = remote_call(
        sb, pairs_a, count_a, pairs_b, count_b, row_count,
        rulebook.reshape(KV * NQ, BLK), cyc, weights, acc_a, acc_b, masked, tgt, near,
    )
    summed, wg = weight_call(sb, rulebook, pre_grad, masked, cyc)

    share = 32 * C // devices
    parts = lax.all_to_all(wg.reshape(devices, share, C), AXES, 0, 0, tiled=True)
    table_grad = table_call(sb, summed, weights)
    parts, table_grad = lax.optimization_barrier((parts, table_grad))
    total = jnp.sum(parts.astype(F32), axis=0).astype(BF)
    spread = jnp.broadcast_to(total[None], (devices, share, C))
    every = lax.all_to_all(spread, AXES, 0, 0, tiled=True).reshape(32 * C, C)
    weight_grad = every[: KV * C].reshape(KV, C, C).astype(F32) * (1.0 / math.sqrt(VOX * devices))

    own, partial = pool_call(tgt, hidden)
    partial = partial.reshape(3, 3, COARSE, C)
    cycle_grad = table_grad[VOX:].reshape(4, 4, FACE, C)

    def packed(sums, grads):
        return jnp.concatenate([sums.reshape(3 * COARSE, C), grads.astype(BF).reshape(-1, C)], 0)

    from_high = shift(packed(partial[:, 0], cycle_grad[0]), "gx", -1)
    from_low = shift(packed(partial[:, 2], cycle_grad[3]), "gx", 1)
    cut = 3 * COARSE
    grad_high = jnp.where(place_x < size_x - 1, from_high[cut:], zero).reshape(4, FACE, C).astype(F32)
    grad_low = jnp.where(place_x > 0, from_low[cut:], zero).reshape(4, FACE, C).astype(F32)
    wide = jnp.stack([cycle_grad[1] + grad_low, cycle_grad[2] + grad_high])
    sums_high = from_high[:cut].reshape(3, COARSE, C)
    sums_low = from_low[:cut].reshape(3, COARSE, C)
    from_above = shift(
        packed(jnp.stack([sums_low[0], partial[0, 1], sums_high[0]]), wide[:, 0]), "gy", -1
    )
    from_below = shift(
        packed(jnp.stack([sums_low[2], partial[2, 1], sums_high[2]]), wide[:, 3]), "gy", 1
    )
    grad_above = jnp.where(place_y < size_y - 1, from_above[cut:], zero)
    grad_below = jnp.where(place_y > 0, from_below[cut:], zero)
    pooled = own + sums_low[1].astype(F32) + sums_high[1].astype(F32)
    for sums in (from_above, from_below):
        pooled = pooled + jnp.sum(sums[:cut].reshape(3, COARSE, C).astype(F32), 0)
    face_grad = jnp.stack(
        [
            wide[:, 1] + grad_below.reshape(2, FACE, C).astype(F32),
            wide[:, 2] + grad_above.reshape(2, FACE, C).astype(F32),
        ],
        1,
    )
    total_grad = table_grad[:VOX] + up_grad.astype(F32)
    total_grad = total_grad.at[: 4 * FACE].add(face_grad.reshape(4 * FACE, C))
    feature_grad = jnp.where(active[:, None], total_grad, 0.0).astype(BF)
    return (pooled.astype(BF), weight_grad, feature_grad)


def solution(mesh):
    return jax.shard_map(
        shards,
        mesh=mesh,
        in_specs=(
            P(AXES, None),
            P(),
            P(None, AXES),
            P(AXES, None),
            P(AXES),
            P(AXES),
            P(AXES, None),
        ),
        out_specs=(P(AXES, None), P(), P(AXES, None)),
        check_vma=False,
    )
```

```python
import functools
import math

import jax
import jax.numpy as jnp
from jax import lax
from jax.experimental import pallas as pl
from jax.experimental.pallas import tpu as pltpu
from jax.sharding import PartitionSpec as P

BF = jnp.bfloat16
F32 = jnp.float32
AXES = ("gx", "gy")
C = 128
KV = 27
VOX = 2048
BLK = 128
NQ = VOX // BLK
ROWS = 32
FACE = 32
CYC = 16 * FACE
EXT = VOX + CYC
NLOC = VOX // BLK
NTAB = EXT // BLK
COARSE = 256
NT = 9 * COARSE
GROUP = 16
WIDE = 512
SMEM = pl.BlockSpec(memory_space=pltpu.SMEM)
VMEM = pl.BlockSpec(memory_space=pltpu.VMEM)


def params():
    return pltpu.CompilerParams(vmem_limit_bytes=24 << 20)


def cost(micros):
    return pl.CostEstimate(flops=0, transcendentals=0, bytes_accessed=int(micros * 3.6e6))


def counting(axis):
    return lax.broadcasted_iota(jnp.int32, (BLK, BLK), axis).astype(F32).astype(BF)


def onehot(row, numbers):
    row = jnp.broadcast_to(row.astype(F32), (BLK, BLK)).astype(BF)
    return jnp.where(row == numbers, jnp.ones((), BF), jnp.zeros((), BF))


def prepare_kernel(rows, features, rb, table, listed, blocks):
    keep = lax.broadcasted_iota(jnp.int32, (VOX, C), 0) < rows[0]
    table[:VOX, :] = jnp.where(keep, features[...].astype(F32), 0.0).astype(BF)
    table[VOX:, :] = jnp.zeros((BLK, C), BF)
    cols = []
    for q in range(NQ):
        part = rb[:, q * BLK : (q + 1) * BLK]
        listed[q * ROWS : q * ROWS + KV, :] = part
        low = jnp.min(part.astype(F32), axis=1, keepdims=True).astype(jnp.int32)
        cols.append(jnp.minimum(low // BLK, NTAB - 1))
    blocks[...] = jnp.concatenate(cols, 1)


def prepare_call(rows, features, rb):
    return pl.pallas_call(
        prepare_kernel,
        in_specs=[SMEM, VMEM, VMEM],
        out_specs=[VMEM] * 3,
        out_shape=[
            pltpu.VMEM((VOX + BLK, C), BF),
            pltpu.VMEM((NQ * ROWS, BLK), jnp.int32),
            jax.ShapeDtypeStruct((KV, NQ), jnp.int32),
        ],
        compiler_params=params(),
        cost_estimate=cost(2),
        name="prepare",
    )(rows, features, rb)


def local_kernel(first, sb, listed, table, w, acc, pairs, count, picked):
    numbers = counting(0)

    def body(q, n):
        r0 = pl.multiple_of((q - first) * BLK, BLK)
        for k in range(KV):
            s = sb[k, q]
            pairs[n] = q * ROWS + k
            n = n + jnp.where(s < NLOC, 0, 1)
            t0 = pl.multiple_of(jnp.minimum(s, NLOC) * BLK, BLK)
            row = listed[pl.ds(q * ROWS + k, 1), :] - s * BLK
            got = lax.dot_general(
                onehot(row, numbers), table[pl.ds(t0, BLK), :], (((0,), (0,)), ((), ())),
                preferred_element_type=F32,
            )
            picked[pl.ds(r0, BLK), k * C : (k + 1) * C] = got.astype(BF)
        return n

    count[0] = lax.fori_loop(first, first + NQ // 2, body, 0)
    acc[...] = jnp.dot(picked[...], w[...], preferred_element_type=F32)


def local_call(first, sb, listed, table, w):
    return pl.pallas_call(
        functools.partial(local_kernel, first),
        in_specs=[SMEM, VMEM, VMEM, VMEM],
        out_specs=[VMEM, SMEM, SMEM],
        out_shape=[
            pltpu.VMEM((VOX // 2, C), F32),
            jax.ShapeDtypeStruct((KV * NQ // 2 + GROUP,), jnp.int32),
            jax.ShapeDtypeStruct((1,), jnp.int32),
        ],
        scratch_shapes=[pltpu.VMEM((VOX // 2, KV * C), BF)],
        compiler_params=params(),
        cost_estimate=cost(9),
        name="conv_local",
    )(sb, listed, table, w)


def remote_kernel(
    sb, pairs_a, count_a, pairs_b, count_b, rows, place, listed, w, acc_a, acc_b, table, tgt,
    sent_up, sent_down, got_up, got_down, hidden, up, pre, cyc, acc, sel,
):
    numbers = counting(0)
    lanes = counting(1)
    face = 4 * FACE
    zero = jnp.zeros((), BF)
    below = jnp.where(place[0] > 0, got_up[:face, :].astype(F32), 0.0).astype(BF)
    above = jnp.where(place[0] < place[1] - 1, got_down[:face, :].astype(F32), 0.0).astype(BF)
    four = (below, sent_down[:face, :], sent_up[:face, :], above)
    for i in range(4):
        for j in range(4):
            r = (4 * i + j) * FACE
            cyc[r : r + FACE, :] = four[j][i * FACE : (i + 1) * FACE, :]
    cyc[CYC:, :] = jnp.zeros((BLK, C), BF)
    acc[: VOX // 2, :] = acc_a[...]
    acc[VOX // 2 :, :] = acc_b[...]

    def group(pairs, n, i, carry):
        info, gots = [], []
        for j in range(GROUP):
            idx = i * GROUP + j
            e = pairs[jnp.minimum(idx, n - 1)]
            k, q = e % ROWS, e // ROWS
            s = sb[k, q]
            t0 = pl.multiple_of(jnp.where(idx < n, s - NLOC, NTAB - NLOC) * BLK, BLK)
            info.append((e, s, k, t0, pl.multiple_of(q * BLK, BLK)))
        for e, s, k, t0, r0 in info:
            row = listed[pl.ds(e, 1), :] - s * BLK
            got = lax.dot_general(
                onehot(row, numbers), cyc[pl.ds(t0, BLK), :], (((0,), (0,)), ((), ())),
                preferred_element_type=F32,
            )
            gots.append(got.astype(BF))
        outs = [
            jnp.dot(got, w[at[2]], preferred_element_type=F32)
            for got, at in zip(gots, info, strict=True)
        ]
        for out, at in zip(outs, info, strict=True):
            acc[pl.ds(at[4], BLK), :] += out
        return carry

    for pairs, count in ((pairs_a, count_a), (pairs_b, count_b)):
        n = count[0]
        lax.fori_loop(0, (n + GROUP - 1) // GROUP, functools.partial(group, pairs, n), 0)

    def point(p, carry):
        for h in range(WIDE // BLK):
            row = tgt[pl.ds(p * (WIDE // BLK) + h, 1), :]
            col = jnp.broadcast_to(row, (BLK, BLK)).T
            tile = jnp.floor(col * (1.0 / BLK))
            hit = jnp.where((col - tile * BLK).astype(BF) == lanes, jnp.ones((), BF), zero)
            tile = tile.astype(BF)
            for t in range(NT // BLK):
                here = tile == jnp.asarray(t, BF)
                sel[h * BLK : (h + 1) * BLK, t * BLK : (t + 1) * BLK] = jnp.where(here, hit, zero)
        at = pl.ds(pl.multiple_of(p * WIDE, WIDE), WIDE)
        third = 3 * COARSE
        grad = jnp.dot(sel[:, :third], got_up[face:, :], preferred_element_type=F32)
        grad += jnp.dot(sel[:, third : 2 * third], sent_up[face:, :], preferred_element_type=F32)
        grad += jnp.dot(sel[:, 2 * third :], got_down[face:, :], preferred_element_type=F32)
        v = acc[at, :]
        sg = 1.0 / (1.0 + jnp.exp(-v))
        up[at, :] = grad.astype(BF)
        pre[at, :] = (grad * (sg * (1.0 + v * (1.0 - sg)))).astype(BF)
        out = table[at, :].astype(F32) + v * sg
        number = lax.broadcasted_iota(jnp.int32, (WIDE, C), 0) + p * WIDE
        hidden[at, :] = jnp.where(number < rows[0], out, 0.0).astype(BF)
        return carry

    lax.fori_loop(0, VOX // WIDE, point, 0)


def remote_call(*args):
    return pl.pallas_call(
        remote_kernel,
        in_specs=[SMEM] * 7 + [VMEM] * 10,
        out_specs=[VMEM] * 4,
        out_shape=[pltpu.VMEM((VOX, C), BF)] * 3 + [pltpu.VMEM((CYC + BLK, C), BF)],
        scratch_shapes=[pltpu.VMEM((VOX, C), F32), pltpu.VMEM((WIDE, NT), BF)],
        compiler_params=params(),
        cost_estimate=cost(12),
        name="conv_remote",
    )(*args)


def scatter_rows(sb, listed, pre, summed):
    numbers = counting(0)

    def scatter(q, carry):
        r0 = pl.multiple_of(q * BLK, BLK)
        grads = pre[pl.ds(r0, BLK), :]
        for k in range(KV):
            row = listed[pl.ds(q * ROWS + k, 1), :] - sb[k, q] * BLK
            got = jnp.dot(onehot(row, numbers), grads, preferred_element_type=F32)
            summed[k, pl.ds(r0, BLK), :] = got.astype(BF)
        return carry

    lax.fori_loop(0, NQ, scatter, 0)


def weight_kernel(sb, listed, pre, table, cyc, wg, flipped, summed):
    for b in range(NTAB):
        src, r = (table, b * BLK) if b < NLOC else (cyc, (b - NLOC) * BLK)
        flipped[:, b * BLK : (b + 1) * BLK] = src[r : r + BLK, :].T
    scatter_rows(sb, listed, pre, summed)

    def contract(k, carry):
        parts = [flipped[:, pl.ds(pl.multiple_of(sb[k, q] * BLK, BLK), BLK)] for q in range(NQ)]
        got = jnp.dot(jnp.concatenate(parts, 1), summed[k], preferred_element_type=F32)
        wg[pl.ds(pl.multiple_of(k * C, C), C), :] = got.astype(BF)
        return carry

    lax.fori_loop(0, KV, contract, 0)
    wg[KV * C :, :] = jnp.zeros((wg.shape[0] - KV * C, C), BF)


def weight_call(*args):
    return pl.pallas_call(
        weight_kernel,
        in_specs=[SMEM] + [VMEM] * 4,
        out_specs=VMEM,
        out_shape=jax.ShapeDtypeStruct((32 * C, C), BF),
        scratch_shapes=[pltpu.VMEM((C, EXT), BF), pltpu.VMEM((KV, VOX, C), BF)],
        compiler_params=params(),
        cost_estimate=cost(15),
        name="weight_grad",
    )(*args)


def table_kernel(sb, listed, pre, w, out, summed):
    scatter_rows(sb, listed, pre, summed)
    out[...] = jnp.zeros(out.shape, F32)

    def body(i, carry):
        for j in range(3):
            k = 3 * i + j
            got = lax.dot_general(
                summed[k], w[k], (((1,), (1,)), ((), ())), preferred_element_type=F32
            )
            for q in range(NQ):
                t0 = pl.multiple_of(sb[k, q] * BLK, BLK)
                out[pl.ds(t0, BLK), :] += got[q * BLK : (q + 1) * BLK, :]
        return carry

    lax.fori_loop(0, KV // 3, body, 0)


def table_call(*args):
    return pl.pallas_call(
        table_kernel,
        in_specs=[SMEM] + [VMEM] * 3,
        out_specs=VMEM,
        out_shape=pltpu.VMEM((EXT, C), F32),
        scratch_shapes=[pltpu.VMEM((KV, VOX, C), BF)],
        compiler_params=params(),
        cost_estimate=cost(14),
        name="table_grad",
    )(*args)


def pool_kernel(tgt, hidden, own, out):
    t = pl.program_id(0)
    size = 3 * COARSE
    numbers = counting(0)
    parts = []
    for q in range(NQ):
        row = tgt[q : q + 1, :] - (t * size).astype(F32)
        parts.append(
            jnp.concatenate([onehot(row - float(j * BLK), numbers) for j in range(size // BLK)], 0)
        )
    got = jnp.dot(jnp.concatenate(parts, 1), hidden[...], preferred_element_type=F32)
    out[...] = got.astype(BF)

    @pl.when(t == 1)
    def _():
        own[...] = got[COARSE : 2 * COARSE]


def pool_call(tgt, hidden):
    return pl.pallas_call(
        pool_kernel,
        grid=(3,),
        in_specs=[
            pl.BlockSpec((NQ, BLK), lambda t: (0, 0)),
            pl.BlockSpec((VOX, C), lambda t: (0, 0)),
        ],
        out_specs=[
            pl.BlockSpec((COARSE, C), lambda t: (0, 0)),
            pl.BlockSpec((3 * COARSE, C), lambda t: (t, 0)),
        ],
        out_shape=[jax.ShapeDtypeStruct((COARSE, C), F32), jax.ShapeDtypeStruct((NT, C), BF)],
        compiler_params=params(),
        cost_estimate=cost(4),
        name="pool_partial",
    )(tgt, hidden)


def shift(array, axis, step):
    size = lax.axis_size(axis)
    return lax.ppermute(array, axis, [(i, (i + step) % size) for i in range(size)])


def shards(features, weights, rulebook, owner_map, coarse_slot, row_count, coarse_grad):
    size_x, size_y = lax.axis_size("gx"), lax.axis_size("gy")
    devices = size_x * size_y
    place_x, place_y = lax.axis_index("gx"), lax.axis_index("gy")
    active = lax.iota(jnp.int32, VOX) < row_count[0]
    flat_w = weights.reshape(KV * C, C)
    zero = jnp.zeros((), BF)

    faces = jnp.where(active[: 4 * FACE, None], features[: 4 * FACE], zero)
    half = 2 * FACE
    from_low = shift(jnp.concatenate([faces[half:], coarse_grad], 0), "gx", 1)
    from_high = shift(jnp.concatenate([faces[:half], coarse_grad], 0), "gx", -1)
    table, listed, sb = prepare_call(row_count, features, rulebook)
    acc_a, pairs_a, count_a = local_call(0, sb, listed, table, flat_w)
    from_low, from_high, acc_a = lax.optimization_barrier((from_low, from_high, acc_a))
    low_faces = jnp.where(place_x > 0, from_low[:half], zero)
    high_faces = jnp.where(place_x < size_x - 1, from_high[:half], zero)
    strip = jnp.concatenate([low_faces, faces, high_faces], 0).reshape(4, 2, FACE, C)
    coarse_x = jnp.concatenate([from_low[half:], coarse_grad, from_high[half:]], 0)
    sent_up = jnp.concatenate([strip[:, 1].reshape(4 * FACE, C), coarse_x], 0)
    sent_down = jnp.concatenate([strip[:, 0].reshape(4 * FACE, C), coarse_x], 0)
    sb_b, sent_up, sent_down = lax.optimization_barrier((sb, sent_up, sent_down))
    got_up = shift(sent_up, "gy", 1)
    got_down = shift(sent_down, "gy", -1)
    acc_b, pairs_b, count_b = local_call(NQ // 2, sb_b, listed, table, flat_w)

    owner = owner_map[:, 0]
    step_x = (owner // size_y - place_x + 1) % size_x
    step_y = (owner % size_y - place_y + 1) % size_y
    tgt = jnp.where(active, (step_y * 3 + step_x) * COARSE + coarse_slot, -1)
    tgt = tgt.reshape(NQ, BLK).astype(F32)
    place = jnp.stack([place_y, jnp.int32(size_y)])
    hidden, up_grad, pre_grad, cyc = remote_call(
        sb, pairs_a, count_a, pairs_b, count_b, row_count, place, listed, weights, acc_a, acc_b,
        table, tgt, sent_up, sent_down, got_up, got_down,
    )
    wg = weight_call(sb, listed, pre_grad, table, cyc)

    share = 32 * C // devices
    parts = lax.all_to_all(wg.reshape(devices, share, C), AXES, 0, 0, tiled=True)
    table_grad = table_call(sb, listed, pre_grad, weights)
    parts, table_grad = lax.optimization_barrier((parts, table_grad))
    total = jnp.sum(parts.astype(F32), axis=0).astype(BF)
    spread = jnp.broadcast_to(total[None], (devices, share, C))
    every = lax.all_to_all(spread, AXES, 0, 0, tiled=True).reshape(32 * C, C)
    weight_grad = every[: KV * C].reshape(KV, C, C).astype(F32) * (1.0 / math.sqrt(VOX * devices))

    own, partial = pool_call(tgt, hidden)
    partial = partial.reshape(3, 3, COARSE, C)
    cycle_grad = table_grad[VOX:].reshape(4, 4, FACE, C)

    def packed(sums, grads):
        return jnp.concatenate([sums.reshape(3 * COARSE, C), grads.astype(BF).reshape(-1, C)], 0)

    from_high = shift(packed(partial[:, 0], cycle_grad[0]), "gx", -1)
    from_low = shift(packed(partial[:, 2], cycle_grad[3]), "gx", 1)
    cut = 3 * COARSE
    grad_high = jnp.where(place_x < size_x - 1, from_high[cut:], zero).reshape(4, FACE, C).astype(F32)
    grad_low = jnp.where(place_x > 0, from_low[cut:], zero).reshape(4, FACE, C).astype(F32)
    wide = jnp.stack([cycle_grad[1] + grad_low, cycle_grad[2] + grad_high])
    sums_high = from_high[:cut].reshape(3, COARSE, C)
    sums_low = from_low[:cut].reshape(3, COARSE, C)
    from_above = shift(
        packed(jnp.stack([sums_low[0], partial[0, 1], sums_high[0]]), wide[:, 0]), "gy", -1
    )
    from_below = shift(
        packed(jnp.stack([sums_low[2], partial[2, 1], sums_high[2]]), wide[:, 3]), "gy", 1
    )
    grad_above = jnp.where(place_y < size_y - 1, from_above[cut:], zero)
    grad_below = jnp.where(place_y > 0, from_below[cut:], zero)
    pooled = own + sums_low[1].astype(F32) + sums_high[1].astype(F32)
    for sums in (from_above, from_below):
        pooled = pooled + jnp.sum(sums[:cut].reshape(3, COARSE, C).astype(F32), 0)
    face_grad = jnp.stack(
        [
            wide[:, 1] + grad_below.reshape(2, FACE, C).astype(F32),
            wide[:, 2] + grad_above.reshape(2, FACE, C).astype(F32),
        ],
        1,
    )
    total_grad = table_grad[:VOX] + up_grad.astype(F32)
    total_grad = total_grad.at[: 4 * FACE].add(face_grad.reshape(4 * FACE, C))
    feature_grad = jnp.where(active[:, None], total_grad, 0.0).astype(BF)
    return (pooled.astype(BF), weight_grad, feature_grad)


def solution(mesh):
    return jax.shard_map(
        shards,
        mesh=mesh,
        in_specs=(
            P(AXES, None),
            P(),
            P(None, AXES),
            P(AXES, None),
            P(AXES),
            P(AXES),
            P(AXES, None),
        ),
        out_specs=(P(AXES, None), P(), P(AXES, None)),
        check_vma=False,
    )
```

```python
import functools
import math

import jax
import jax.numpy as jnp
from jax import lax
from jax.experimental import pallas as pl
from jax.experimental.pallas import tpu as pltpu
from jax.sharding import PartitionSpec as P

BF = jnp.bfloat16
F32 = jnp.float32
AXES = ("gx", "gy")
C = 128
KV = 27
VOX = 2048
BLK = 128
NQ = VOX // BLK
ROWS = 32
FACE = 32
CYC = 16 * FACE
EXT = VOX + CYC
NLOC = VOX // BLK
NTAB = EXT // BLK
COARSE = 256
NT = 9 * COARSE
GROUP = 16
WIDE = 512
SMEM = pl.BlockSpec(memory_space=pltpu.SMEM)
VMEM = pl.BlockSpec(memory_space=pltpu.VMEM)


def params():
    return pltpu.CompilerParams(vmem_limit_bytes=24 << 20)


def cost(micros):
    return pl.CostEstimate(flops=0, transcendentals=0, bytes_accessed=int(micros * 3.6e6))


def counting(axis):
    return lax.broadcasted_iota(jnp.int32, (BLK, BLK), axis).astype(F32).astype(BF)


def onehot(row, numbers):
    row = jnp.broadcast_to(row.astype(F32), (BLK, BLK)).astype(BF)
    return jnp.where(row == numbers, jnp.ones((), BF), jnp.zeros((), BF))


def prepare_kernel(rows, features, rb, table, listed, blocks):
    number = lax.broadcasted_iota(jnp.int32, (BLK, C), 0)
    cols = []
    for q in range(NQ):
        at = slice(q * BLK, (q + 1) * BLK)
        kept = jnp.where(number + q * BLK < rows[0], features[at, :].astype(F32), 0.0)
        table[:, at] = kept.astype(BF).T
        part = rb[:, at]
        listed[q * ROWS : q * ROWS + KV, :] = part
        low = jnp.min(part.astype(F32), axis=1, keepdims=True).astype(jnp.int32)
        cols.append(jnp.minimum(low // BLK, NTAB - 1))
    blocks[...] = jnp.concatenate(cols, 1)


def prepare_call(rows, features, rb):
    return pl.pallas_call(
        prepare_kernel,
        in_specs=[SMEM, VMEM, VMEM],
        out_specs=[VMEM] * 3,
        out_shape=[
            pltpu.VMEM((C, VOX), BF),
            pltpu.VMEM((NQ * ROWS, BLK), jnp.int32),
            jax.ShapeDtypeStruct((KV, NQ), jnp.int32),
        ],
        compiler_params=params(),
        cost_estimate=cost(2),
        name="prepare",
    )(rows, features, rb)


def local_kernel(first, sb, listed, table, pick, pairs, count):
    numbers = counting(0)

    def body(q, n):
        r0 = pl.multiple_of((q - first) * BLK, BLK)
        for k in range(KV):
            s = sb[k, q]
            pairs[n] = q * ROWS + k
            n = n + jnp.where(s < NLOC, 0, 1)
            t0 = pl.multiple_of(jnp.minimum(s, NLOC - 1) * BLK, BLK)
            row = listed[pl.ds(q * ROWS + k, 1), :] - s * BLK
            got = jnp.dot(
                table[:, pl.ds(t0, BLK)], onehot(row, numbers), preferred_element_type=F32
            )
            pick[k * C : (k + 1) * C, pl.ds(r0, BLK)] = got.astype(BF)
        return n

    count[0] = lax.fori_loop(first, first + NQ // 2, body, 0)


def local_call(first, sb, listed, table):
    return pl.pallas_call(
        functools.partial(local_kernel, first),
        in_specs=[SMEM, VMEM, VMEM],
        out_specs=[VMEM, SMEM, SMEM],
        out_shape=[
            pltpu.VMEM((KV * C, VOX // 2), BF),
            jax.ShapeDtypeStruct((KV * NQ // 2 + GROUP,), jnp.int32),
            jax.ShapeDtypeStruct((1,), jnp.int32),
        ],
        compiler_params=params(),
        cost_estimate=cost(6),
        name="pick_local",
    )(sb, listed, table)


def main_kernel(
    sb, pairs_a, count_a, pairs_b, count_b, rows, place, listed, w, features, tgt,
    sent_up, sent_down, got_up, got_down, in_a, in_b, hidden, up, pre, wg, pick_a, pick_b,
    cyc, flipped, sel,
):
    numbers = counting(0)
    lanes = counting(1)
    face = 4 * FACE
    zero = jnp.zeros((), BF)
    below = jnp.where(place[0] > 0, got_up[:face, :].astype(F32), 0.0).astype(BF)
    above = jnp.where(place[0] < place[1] - 1, got_down[:face, :].astype(F32), 0.0).astype(BF)
    four = (below, sent_down[:face, :], sent_up[:face, :], above)
    for i in range(4):
        part = jnp.concatenate([side[i * FACE : (i + 1) * FACE, :] for side in four], 0)
        cyc[:, i * BLK : (i + 1) * BLK] = part.T
    for k in range(KV):
        flipped[:, k * C : (k + 1) * C] = w[k].T

    def group(first, pairs, n, pick, i, carry):
        info, gots = [], []
        for j in range(GROUP):
            e = pairs[jnp.minimum(i * GROUP + j, n - 1)]
            info.append((e, e % ROWS, e // ROWS))
        for e, k, q in info:
            s = sb[k, q]
            t0 = pl.multiple_of((s - NLOC) * BLK, BLK)
            row = listed[pl.ds(e, 1), :] - s * BLK
            got = jnp.dot(cyc[:, pl.ds(t0, BLK)], onehot(row, numbers), preferred_element_type=F32)
            gots.append(got.astype(BF))
        for got, (e, k, q) in zip(gots, info, strict=True):
            r0 = pl.multiple_of((q - first) * BLK, BLK)
            pick[pl.ds(pl.multiple_of(k * C, C), C), pl.ds(r0, BLK)] = got
        return carry

    for first, pairs, count, pick in (
        (0, pairs_a, count_a, pick_a), (NQ // 2, pairs_b, count_b, pick_b)
    ):
        n = count[0]
        fill = functools.partial(group, first, pairs, n, pick)
        lax.fori_loop(0, (n + GROUP - 1) // GROUP, fill, 0)

    def point(first, pick, p, carry):
        at = pl.ds(pl.multiple_of(first + p * WIDE, WIDE), WIDE)
        here = pl.ds(pl.multiple_of(p * WIDE, WIDE), WIDE)
        v = jnp.dot(flipped[...], pick[:, here], preferred_element_type=F32).T
        for h in range(WIDE // BLK):
            row = tgt[pl.ds(first // BLK + p * (WIDE // BLK) + h, 1), :]
            col = jnp.broadcast_to(row, (BLK, BLK)).T
            tile = jnp.floor(col * (1.0 / BLK))
            hit = jnp.where((col - tile * BLK).astype(BF) == lanes, jnp.ones((), BF), zero)
            tile = tile.astype(BF)
            for t in range(NT // BLK):
                meets = tile == jnp.asarray(t, BF)
                sel[h * BLK : (h + 1) * BLK, t * BLK : (t + 1) * BLK] = jnp.where(meets, hit, zero)
        third = 3 * COARSE
        grad = jnp.dot(sel[:, :third], got_up[face:, :], preferred_element_type=F32)
        grad += jnp.dot(sel[:, third : 2 * third], sent_up[face:, :], preferred_element_type=F32)
        grad += jnp.dot(sel[:, 2 * third :], got_down[face:, :], preferred_element_type=F32)
        sg = 1.0 / (1.0 + jnp.exp(-v))
        up[at, :] = grad.astype(BF)
        pre[at, :] = (grad * (sg * (1.0 + v * (1.0 - sg)))).astype(BF)
        out = features[at, :].astype(F32) + v * sg
        number = lax.broadcasted_iota(jnp.int32, (WIDE, C), 0) + first + p * WIDE
        hidden[at, :] = jnp.where(number < rows[0], out, 0.0).astype(BF)
        return carry

    for first, pick in ((0, pick_a), (VOX // 2, pick_b)):
        lax.fori_loop(0, VOX // 2 // WIDE, functools.partial(point, first, pick), 0)

    for k in range(0, KV, 9):
        at = slice(k * C, (k + 9) * C)
        got = jnp.dot(pick_a[at, :], pre[: VOX // 2, :], preferred_element_type=F32)
        got += jnp.dot(pick_b[at, :], pre[VOX // 2 :, :], preferred_element_type=F32)
        wg[at, :] = got.astype(BF)
    wg[KV * C :, :] = jnp.zeros((wg.shape[0] - KV * C, C), BF)


def main_call(*args):
    picks = pltpu.VMEM((KV * C, VOX // 2), BF)
    return pl.pallas_call(
        main_kernel,
        in_specs=[SMEM] * 7 + [VMEM] * 10,
        out_specs=[VMEM] * 6,
        out_shape=[pltpu.VMEM((VOX, C), BF)] * 3
        + [jax.ShapeDtypeStruct((32 * C, C), BF), picks, picks],
        input_output_aliases={15: 4, 16: 5},
        scratch_shapes=[
            pltpu.VMEM((C, CYC), BF),
            pltpu.VMEM((C, KV * C), BF),
            pltpu.VMEM((WIDE, NT), BF),
        ],
        compiler_params=params(),
        cost_estimate=cost(15),
        name="conv_main",
    )(*args)[:4]


def scatter_rows(sb, listed, pre, summed):
    numbers = counting(0)

    def scatter(q, carry):
        r0 = pl.multiple_of(q * BLK, BLK)
        grads = pre[pl.ds(r0, BLK), :]
        for k in range(KV):
            row = listed[pl.ds(q * ROWS + k, 1), :] - sb[k, q] * BLK
            got = jnp.dot(onehot(row, numbers), grads, preferred_element_type=F32)
            summed[k, pl.ds(r0, BLK), :] = got.astype(BF)
        return carry

    lax.fori_loop(0, NQ, scatter, 0)


def table_kernel(sb, listed, pre, w, out, summed):
    scatter_rows(sb, listed, pre, summed)
    out[...] = jnp.zeros(out.shape, F32)

    def body(i, carry):
        for j in range(3):
            k = 3 * i + j
            got = lax.dot_general(
                summed[k], w[k], (((1,), (1,)), ((), ())), preferred_element_type=F32
            )
            for q in range(NQ):
                t0 = pl.multiple_of(sb[k, q] * BLK, BLK)
                out[pl.ds(t0, BLK), :] += got[q * BLK : (q + 1) * BLK, :]
        return carry

    lax.fori_loop(0, KV // 3, body, 0)


def table_call(*args):
    return pl.pallas_call(
        table_kernel,
        in_specs=[SMEM] + [VMEM] * 3,
        out_specs=VMEM,
        out_shape=pltpu.VMEM((EXT, C), F32),
        scratch_shapes=[pltpu.VMEM((KV, VOX, C), BF)],
        compiler_params=params(),
        cost_estimate=cost(14),
        name="table_grad",
    )(*args)


def pool_kernel(tgt, hidden, own, out):
    t = pl.program_id(0)
    size = 3 * COARSE
    numbers = counting(0)
    parts = []
    for q in range(NQ):
        row = tgt[q : q + 1, :] - (t * size).astype(F32)
        parts.append(
            jnp.concatenate([onehot(row - float(j * BLK), numbers) for j in range(size // BLK)], 0)
        )
    got = jnp.dot(jnp.concatenate(parts, 1), hidden[...], preferred_element_type=F32)
    out[...] = got.astype(BF)

    @pl.when(t == 1)
    def _():
        own[...] = got[COARSE : 2 * COARSE]


def pool_call(tgt, hidden):
    return pl.pallas_call(
        pool_kernel,
        grid=(3,),
        in_specs=[
            pl.BlockSpec((NQ, BLK), lambda t: (0, 0)),
            pl.BlockSpec((VOX, C), lambda t: (0, 0)),
        ],
        out_specs=[
            pl.BlockSpec((COARSE, C), lambda t: (0, 0)),
            pl.BlockSpec((3 * COARSE, C), lambda t: (t, 0)),
        ],
        out_shape=[jax.ShapeDtypeStruct((COARSE, C), F32), jax.ShapeDtypeStruct((NT, C), BF)],
        compiler_params=params(),
        cost_estimate=cost(4),
        name="pool_partial",
    )(tgt, hidden)


def shift(array, axis, step):
    size = lax.axis_size(axis)
    return lax.ppermute(array, axis, [(i, (i + step) % size) for i in range(size)])


def shards(features, weights, rulebook, owner_map, coarse_slot, row_count, coarse_grad):
    size_x, size_y = lax.axis_size("gx"), lax.axis_size("gy")
    devices = size_x * size_y
    place_x, place_y = lax.axis_index("gx"), lax.axis_index("gy")
    active = lax.iota(jnp.int32, VOX) < row_count[0]
    zero = jnp.zeros((), BF)

    faces = jnp.where(active[: 4 * FACE, None], features[: 4 * FACE], zero)
    half = 2 * FACE
    from_low = shift(jnp.concatenate([faces[half:], coarse_grad], 0), "gx", 1)
    from_high = shift(jnp.concatenate([faces[:half], coarse_grad], 0), "gx", -1)
    table, listed, sb = prepare_call(row_count, features, rulebook)
    pick_a, pairs_a, count_a = local_call(0, sb, listed, table)
    from_low, from_high, pick_a = lax.optimization_barrier((from_low, from_high, pick_a))
    low_faces = jnp.where(place_x > 0, from_low[:half], zero)
    high_faces = jnp.where(place_x < size_x - 1, from_high[:half], zero)
    strip = jnp.concatenate([low_faces, faces, high_faces], 0).reshape(4, 2, FACE, C)
    coarse_x = jnp.concatenate([from_low[half:], coarse_grad, from_high[half:]], 0)
    sent_up = jnp.concatenate([strip[:, 1].reshape(4 * FACE, C), coarse_x], 0)
    sent_down = jnp.concatenate([strip[:, 0].reshape(4 * FACE, C), coarse_x], 0)
    sb_b, sent_up, sent_down = lax.optimization_barrier((sb, sent_up, sent_down))
    got_up = shift(sent_up, "gy", 1)
    got_down = shift(sent_down, "gy", -1)
    pick_b, pairs_b, count_b = local_call(NQ // 2, sb_b, listed, table)

    owner = owner_map[:, 0]
    step_x = (owner // size_y - place_x + 1) % size_x
    step_y = (owner % size_y - place_y + 1) % size_y
    tgt = jnp.where(active, (step_y * 3 + step_x) * COARSE + coarse_slot, -1)
    tgt = tgt.reshape(NQ, BLK).astype(F32)
    place = jnp.stack([place_y, jnp.int32(size_y)])
    hidden, up_grad, pre_grad, wg = main_call(
        sb, pairs_a, count_a, pairs_b, count_b, row_count, place, listed, weights, features,
        tgt, sent_up, sent_down, got_up, got_down, pick_a, pick_b,
    )

    share = 32 * C // devices
    parts = lax.all_to_all(wg.reshape(devices, share, C), AXES, 0, 0, tiled=True)
    table_grad = table_call(sb, listed, pre_grad, weights)
    parts, table_grad = lax.optimization_barrier((parts, table_grad))
    total = jnp.sum(parts.astype(F32), axis=0).astype(BF)
    spread = jnp.broadcast_to(total[None], (devices, share, C))
    every = lax.all_to_all(spread, AXES, 0, 0, tiled=True).reshape(32 * C, C)
    weight_grad = every[: KV * C].reshape(KV, C, C).astype(F32) * (1.0 / math.sqrt(VOX * devices))

    own, partial = pool_call(tgt, hidden)
    partial = partial.reshape(3, 3, COARSE, C)
    cycle_grad = table_grad[VOX:].reshape(4, 4, FACE, C)

    def packed(sums, grads):
        return jnp.concatenate([sums.astype(BF), grads.astype(BF).reshape(-1, C)], 0)

    from_high = shift(packed(partial[:, 0].reshape(3 * COARSE, C), cycle_grad[0]), "gx", -1)
    from_low = shift(packed(partial[:, 2].reshape(3 * COARSE, C), cycle_grad[3]), "gx", 1)
    cut = 3 * COARSE
    grad_high = jnp.where(place_x < size_x - 1, from_high[cut:], zero).reshape(4, FACE, C).astype(F32)
    grad_low = jnp.where(place_x > 0, from_low[cut:], zero).reshape(4, FACE, C).astype(F32)
    wide = jnp.stack([cycle_grad[1] + grad_low, cycle_grad[2] + grad_high])
    sums = from_high[:cut].astype(F32) + from_low[:cut].astype(F32)
    sums_down = sums[:COARSE] + partial[0, 1].astype(F32)
    sums_up = sums[2 * COARSE :] + partial[2, 1].astype(F32)
    from_above = shift(packed(sums_down, wide[:, 0]), "gy", -1)
    from_below = shift(packed(sums_up, wide[:, 3]), "gy", 1)
    grad_above = jnp.where(place_y < size_y - 1, from_above[COARSE:], zero)
    grad_below = jnp.where(place_y > 0, from_below[COARSE:], zero)
    pooled = own + sums[COARSE : 2 * COARSE]
    pooled = pooled + from_above[:COARSE].astype(F32) + from_below[:COARSE].astype(F32)
    face_grad = jnp.stack(
        [
            wide[:, 1] + grad_below.reshape(2, FACE, C).astype(F32),
            wide[:, 2] + grad_above.reshape(2, FACE, C).astype(F32),
        ],
        1,
    )
    total_grad = table_grad[:VOX] + up_grad.astype(F32)
    total_grad = total_grad.at[: 4 * FACE].add(face_grad.reshape(4 * FACE, C))
    feature_grad = jnp.where(active[:, None], total_grad, 0.0).astype(BF)
    return (pooled.astype(BF), weight_grad, feature_grad)


def solution(mesh):
    return jax.shard_map(
        shards,
        mesh=mesh,
        in_specs=(
            P(AXES, None),
            P(),
            P(None, AXES),
            P(AXES, None),
            P(AXES),
            P(AXES),
            P(AXES, None),
        ),
        out_specs=(P(AXES, None), P(), P(AXES, None)),
        check_vma=False,
    )
```

```python
import functools
import math

import jax
import jax.numpy as jnp
from jax import lax
from jax.experimental import pallas as pl
from jax.experimental.pallas import tpu as pltpu
from jax.sharding import PartitionSpec as P

BF = jnp.bfloat16
F32 = jnp.float32
AXES = ("gx", "gy")
C = 128
KV = 27
VOX = 2048
BLK = 128
NQ = VOX // BLK
ROWS = 32
FACE = 32
CYC = 16 * FACE
EXT = VOX + CYC
NLOC = VOX // BLK
NTAB = EXT // BLK
COARSE = 256
NT = 9 * COARSE
GROUP = 16
WIDE = 512
SMEM = pl.BlockSpec(memory_space=pltpu.SMEM)
VMEM = pl.BlockSpec(memory_space=pltpu.VMEM)


def params():
    return pltpu.CompilerParams(vmem_limit_bytes=24 << 20)


def cost(micros):
    return pl.CostEstimate(flops=0, transcendentals=0, bytes_accessed=int(micros * 3.6e6))


def counting(axis):
    return lax.broadcasted_iota(jnp.int32, (BLK, BLK), axis).astype(F32).astype(BF)


def onehot(row, numbers):
    row = jnp.broadcast_to(row.astype(F32), (BLK, BLK)).astype(BF)
    return jnp.where(row == numbers, jnp.ones((), BF), jnp.zeros((), BF))


def prepare_kernel(rows, features, rb, coarse, table, listed, blocks, to_low, to_high):
    number = lax.broadcasted_iota(jnp.int32, (BLK, C), 0)
    cols = []
    for q in range(NQ):
        at = slice(q * BLK, (q + 1) * BLK)
        kept = jnp.where(number + q * BLK < rows[0], features[at, :].astype(F32), 0.0).astype(BF)
        table[:, at] = kept.T
        if q == 0:
            to_low[: 2 * FACE, :] = kept[: 2 * FACE]
            to_high[: 2 * FACE, :] = kept[2 * FACE :]
        part = rb[:, at]
        listed[q * ROWS : q * ROWS + KV, :] = part
        low = jnp.min(part.astype(F32), axis=1, keepdims=True).astype(jnp.int32)
        cols.append(jnp.minimum(low // BLK, NTAB - 1))
    blocks[...] = jnp.concatenate(cols, 1)
    to_low[2 * FACE :, :] = coarse[...]
    to_high[2 * FACE :, :] = coarse[...]


def prepare_call(*args):
    return pl.pallas_call(
        prepare_kernel,
        in_specs=[SMEM, VMEM, VMEM, VMEM],
        out_specs=[VMEM] * 5,
        out_shape=[
            pltpu.VMEM((C, VOX), BF),
            pltpu.VMEM((NQ * ROWS, BLK), jnp.int32),
            jax.ShapeDtypeStruct((KV, NQ), jnp.int32),
            pltpu.VMEM((2 * FACE + COARSE, C), BF),
            pltpu.VMEM((2 * FACE + COARSE, C), BF),
        ],
        compiler_params=params(),
        cost_estimate=cost(1),
        name="prepare",
    )(*args)


def strip_kernel(place, to_low, to_high, from_low, from_high, down, up):
    half = 2 * FACE
    low = jnp.where(place[2] > 0, from_low[:half, :].astype(F32), 0.0).astype(BF)
    high = jnp.where(place[2] < place[3] - 1, from_high[:half, :].astype(F32), 0.0).astype(BF)
    for i, part in enumerate((low, to_low[:half, :], to_high[:half, :], high)):
        at = slice(i * FACE, (i + 1) * FACE)
        down[at, :] = part[:FACE]
        up[at, :] = part[FACE:]
    for i, src in enumerate((from_low, to_low, from_high)):
        at = slice(4 * FACE + i * COARSE, 4 * FACE + (i + 1) * COARSE)
        down[at, :] = src[half:, :]
        up[at, :] = src[half:, :]


def strip_call(*args):
    return pl.pallas_call(
        strip_kernel,
        in_specs=[SMEM] + [VMEM] * 4,
        out_specs=[VMEM] * 2,
        out_shape=[pltpu.VMEM((4 * FACE + 3 * COARSE, C), BF)] * 2,
        compiler_params=params(),
        cost_estimate=cost(1),
        name="strip",
    )(*args)


def local_kernel(first, sb, listed, table, pick, pairs, count):
    numbers = counting(0)

    def body(q, n):
        r0 = pl.multiple_of((q - first) * BLK, BLK)
        for k in range(KV):
            s = sb[k, q]
            pairs[n] = q * ROWS + k
            n = n + jnp.where(s < NLOC, 0, 1)
            t0 = pl.multiple_of(jnp.minimum(s, NLOC - 1) * BLK, BLK)
            row = listed[pl.ds(q * ROWS + k, 1), :] - s * BLK
            got = jnp.dot(
                table[:, pl.ds(t0, BLK)], onehot(row, numbers), preferred_element_type=F32
            )
            pick[k * C : (k + 1) * C, pl.ds(r0, BLK)] = got.astype(BF)
        return n

    count[0] = lax.fori_loop(first, first + NQ // 2, body, 0)


def local_call(first, sb, listed, table):
    return pl.pallas_call(
        functools.partial(local_kernel, first),
        in_specs=[SMEM, VMEM, VMEM],
        out_specs=[VMEM, SMEM, SMEM],
        out_shape=[
            pltpu.VMEM((KV * C, VOX // 2), BF),
            jax.ShapeDtypeStruct((KV * NQ // 2 + GROUP,), jnp.int32),
            jax.ShapeDtypeStruct((1,), jnp.int32),
        ],
        compiler_params=params(),
        cost_estimate=cost(6),
        name="pick_local",
    )(sb, listed, table)


def main_kernel(
    sb, pairs_a, count_a, pairs_b, count_b, rows, place, listed, w, features, tgt,
    sent_up, sent_down, got_up, got_down, in_a, in_b, hidden, up, pre, wg, pick_a, pick_b,
    cyc, flipped, sel,
):
    numbers = counting(0)
    lanes = counting(1)
    face = 4 * FACE
    zero = jnp.zeros((), BF)
    below = jnp.where(place[0] > 0, got_up[:face, :].astype(F32), 0.0).astype(BF)
    above = jnp.where(place[0] < place[1] - 1, got_down[:face, :].astype(F32), 0.0).astype(BF)
    four = (below, sent_down[:face, :], sent_up[:face, :], above)
    for i in range(4):
        part = jnp.concatenate([side[i * FACE : (i + 1) * FACE, :] for side in four], 0)
        cyc[:, i * BLK : (i + 1) * BLK] = part.T
    for k in range(KV):
        flipped[:, k * C : (k + 1) * C] = w[k].T

    def group(first, pairs, n, pick, i, carry):
        info, gots = [], []
        for j in range(GROUP):
            e = pairs[jnp.minimum(i * GROUP + j, n - 1)]
            info.append((e, e % ROWS, e // ROWS))
        for e, k, q in info:
            s = sb[k, q]
            t0 = pl.multiple_of((s - NLOC) * BLK, BLK)
            row = listed[pl.ds(e, 1), :] - s * BLK
            got = jnp.dot(cyc[:, pl.ds(t0, BLK)], onehot(row, numbers), preferred_element_type=F32)
            gots.append(got.astype(BF))
        for got, (e, k, q) in zip(gots, info, strict=True):
            r0 = pl.multiple_of((q - first) * BLK, BLK)
            pick[pl.ds(pl.multiple_of(k * C, C), C), pl.ds(r0, BLK)] = got
        return carry

    for first, pairs, count, pick in (
        (0, pairs_a, count_a, pick_a), (NQ // 2, pairs_b, count_b, pick_b)
    ):
        n = count[0]
        fill = functools.partial(group, first, pairs, n, pick)
        lax.fori_loop(0, (n + GROUP - 1) // GROUP, fill, 0)

    def point(first, pick, p, carry):
        at = pl.ds(pl.multiple_of(first + p * WIDE, WIDE), WIDE)
        here = pl.ds(pl.multiple_of(p * WIDE, WIDE), WIDE)
        v = jnp.dot(flipped[...], pick[:, here], preferred_element_type=F32).T
        for h in range(WIDE // BLK):
            row = tgt[pl.ds(first // BLK + p * (WIDE // BLK) + h, 1), :]
            col = jnp.broadcast_to(row, (BLK, BLK)).T
            tile = jnp.floor(col * (1.0 / BLK))
            hit = jnp.where((col - tile * BLK).astype(BF) == lanes, jnp.ones((), BF), zero)
            tile = tile.astype(BF)
            for t in range(NT // BLK):
                meets = tile == jnp.asarray(t, BF)
                sel[h * BLK : (h + 1) * BLK, t * BLK : (t + 1) * BLK] = jnp.where(meets, hit, zero)
        third = 3 * COARSE
        grad = jnp.dot(sel[:, :third], got_up[face:, :], preferred_element_type=F32)
        grad += jnp.dot(sel[:, third : 2 * third], sent_up[face:, :], preferred_element_type=F32)
        grad += jnp.dot(sel[:, 2 * third :], got_down[face:, :], preferred_element_type=F32)
        sg = 1.0 / (1.0 + jnp.exp(-v))
        up[at, :] = grad.astype(BF)
        pre[at, :] = (grad * (sg * (1.0 + v * (1.0 - sg)))).astype(BF)
        out = features[at, :].astype(F32) + v * sg
        number = lax.broadcasted_iota(jnp.int32, (WIDE, C), 0) + first + p * WIDE
        hidden[at, :] = jnp.where(number < rows[0], out, 0.0).astype(BF)
        return carry

    for first, pick in ((0, pick_a), (VOX // 2, pick_b)):
        lax.fori_loop(0, VOX // 2 // WIDE, functools.partial(point, first, pick), 0)

    for k in range(0, KV, 9):
        at = slice(k * C, (k + 9) * C)
        got = jnp.dot(pick_a[at, :], pre[: VOX // 2, :], preferred_element_type=F32)
        got += jnp.dot(pick_b[at, :], pre[VOX // 2 :, :], preferred_element_type=F32)
        wg[at, :] = got.astype(BF)
    wg[KV * C :, :] = jnp.zeros((wg.shape[0] - KV * C, C), BF)


def main_call(*args):
    picks = pltpu.VMEM((KV * C, VOX // 2), BF)
    return pl.pallas_call(
        main_kernel,
        in_specs=[SMEM] * 7 + [VMEM] * 10,
        out_specs=[VMEM] * 6,
        out_shape=[jax.ShapeDtypeStruct((VOX, C), BF)] * 3
        + [jax.ShapeDtypeStruct((32 * C, C), BF), picks, picks],
        input_output_aliases={15: 4, 16: 5},
        scratch_shapes=[
            pltpu.VMEM((C, CYC), BF),
            pltpu.VMEM((C, KV * C), BF),
            pltpu.VMEM((WIDE, NT), BF),
        ],
        compiler_params=params(),
        cost_estimate=cost(15),
        name="conv_main",
    )(*args)[:4]


def scatter_rows(sb, listed, pre, summed):
    numbers = counting(0)

    def scatter(q, carry):
        r0 = pl.multiple_of(q * BLK, BLK)
        grads = pre[pl.ds(r0, BLK), :]
        for k in range(KV):
            row = listed[pl.ds(q * ROWS + k, 1), :] - sb[k, q] * BLK
            got = jnp.dot(onehot(row, numbers), grads, preferred_element_type=F32)
            summed[k, pl.ds(r0, BLK), :] = got.astype(BF)
        return carry

    lax.fori_loop(0, NQ, scatter, 0)


def table_kernel(sb, listed, pre, w, out, summed):
    scatter_rows(sb, listed, pre, summed)
    out[...] = jnp.zeros(out.shape, F32)

    def body(i, carry):
        for j in range(3):
            k = 3 * i + j
            got = lax.dot_general(
                summed[k], w[k], (((1,), (1,)), ((), ())), preferred_element_type=F32
            )
            for q in range(NQ):
                t0 = pl.multiple_of(sb[k, q] * BLK, BLK)
                out[pl.ds(t0, BLK), :] += got[q * BLK : (q + 1) * BLK, :]
        return carry

    lax.fori_loop(0, KV // 3, body, 0)


def table_call(*args):
    return pl.pallas_call(
        table_kernel,
        in_specs=[SMEM] + [VMEM] * 3,
        out_specs=VMEM,
        out_shape=pltpu.VMEM((EXT, C), F32),
        scratch_shapes=[pltpu.VMEM((KV, VOX, C), BF)],
        compiler_params=params(),
        cost_estimate=cost(14),
        name="table_grad",
    )(*args)


def share_kernel(parts, out):
    total = jnp.sum(parts[...].astype(F32), axis=0, keepdims=True).astype(BF)
    out[...] = jnp.broadcast_to(total, out.shape)


def share_call(parts):
    return pl.pallas_call(
        share_kernel,
        in_specs=[VMEM],
        out_specs=VMEM,
        out_shape=jax.ShapeDtypeStruct(parts.shape, BF),
        compiler_params=params(),
        cost_estimate=cost(1),
        name="share_sum",
    )(parts)


def pool_kernel(tgt, hidden, grads, to_low, to_high, mid):
    size = 3 * COARSE
    numbers = counting(0)
    for t in range(3):
        parts = []
        for q in range(NQ):
            row = tgt[q : q + 1, :] - float(t * size)
            parts.append(
                jnp.concatenate(
                    [onehot(row - float(j * BLK), numbers) for j in range(size // BLK)], 0
                )
            )
        got = jnp.dot(jnp.concatenate(parts, 1), hidden[...], preferred_element_type=F32)
        at = slice(t * COARSE, (t + 1) * COARSE)
        to_low[at, :] = got[:COARSE].astype(BF)
        mid[at, :] = got[COARSE : 2 * COARSE]
        to_high[at, :] = got[2 * COARSE :].astype(BF)
    to_low[size:, :] = grads[VOX : VOX + BLK, :].astype(BF)
    to_high[size:, :] = grads[EXT - BLK :, :].astype(BF)


def pool_call(*args):
    return pl.pallas_call(
        pool_kernel,
        in_specs=[VMEM] * 3,
        out_specs=[VMEM] * 3,
        out_shape=[pltpu.VMEM((3 * COARSE + BLK, C), BF)] * 2
        + [pltpu.VMEM((3 * COARSE, C), F32)],
        compiler_params=params(),
        cost_estimate=cost(3),
        name="pool_partial",
    )(*args)


def middle_kernel(place, mid, grads, from_low, from_high, to_down, to_up, kept, faces):
    cut = 3 * COARSE
    sums = mid[...] + from_low[:cut, :].astype(F32) + from_high[:cut, :].astype(F32)
    kept[...] = sums[COARSE : 2 * COARSE]
    to_down[:COARSE, :] = sums[:COARSE].astype(BF)
    to_up[:COARSE, :] = sums[2 * COARSE :].astype(BF)
    low = jnp.where(place[2] > 0, from_low[cut:, :].astype(F32), 0.0)
    high = jnp.where(place[2] < place[3] - 1, from_high[cut:, :].astype(F32), 0.0)
    for i, add in ((0, low), (1, high)):
        r = VOX + (i + 1) * BLK
        wide = grads[r : r + BLK, :] + add
        at = slice(COARSE + i * FACE, COARSE + (i + 1) * FACE)
        to_down[at, :] = wide[:FACE].astype(BF)
        to_up[at, :] = wide[3 * FACE :].astype(BF)
        faces[i * 2 * FACE : (i + 1) * 2 * FACE, :] = wide[FACE : 3 * FACE]


def middle_call(*args):
    return pl.pallas_call(
        middle_kernel,
        in_specs=[SMEM] + [VMEM] * 4,
        out_specs=[VMEM] * 4,
        out_shape=[pltpu.VMEM((COARSE + 2 * FACE, C), BF)] * 2
        + [pltpu.VMEM((COARSE, C), F32), pltpu.VMEM((4 * FACE, C), F32)],
        compiler_params=params(),
        cost_estimate=cost(0.1),
        name="middle",
    )(*args)


def final_kernel(rows, place, grads, up, kept, faces, from_below, from_above, pooled, out):
    sums = kept[...] + from_below[:COARSE, :].astype(F32) + from_above[:COARSE, :].astype(F32)
    pooled[...] = sums.astype(BF)
    below = jnp.where(place[0] > 0, from_below[COARSE:, :].astype(F32), 0.0)
    above = jnp.where(place[0] < place[1] - 1, from_above[COARSE:, :].astype(F32), 0.0)
    add = jnp.concatenate([below[:FACE], above[:FACE], below[FACE:], above[FACE:]], 0) + faces[...]
    number = lax.broadcasted_iota(jnp.int32, (BLK, C), 0)
    for q in range(NQ):
        at = slice(q * BLK, (q + 1) * BLK)
        total = grads[at, :] + up[at, :].astype(F32)
        if q == 0:
            total += add
        out[at, :] = jnp.where(number + q * BLK < rows[0], total, 0.0).astype(BF)


def final_call(*args):
    return pl.pallas_call(
        final_kernel,
        in_specs=[SMEM] * 2 + [VMEM] * 6,
        out_specs=[VMEM] * 2,
        out_shape=[
            jax.ShapeDtypeStruct((COARSE, C), BF), jax.ShapeDtypeStruct((VOX, C), BF)
        ],
        compiler_params=params(),
        cost_estimate=cost(0.1),
        name="final",
    )(*args)


def shift(array, axis, step):
    size = lax.axis_size(axis)
    return lax.ppermute(array, axis, [(i, (i + step) % size) for i in range(size)])


def shards(features, weights, rulebook, owner_map, coarse_slot, row_count, coarse_grad):
    size_x, size_y = lax.axis_size("gx"), lax.axis_size("gy")
    devices = size_x * size_y
    place_x, place_y = lax.axis_index("gx"), lax.axis_index("gy")
    active = lax.iota(jnp.int32, VOX) < row_count[0]
    place = jnp.stack([place_y, jnp.int32(size_y), place_x, jnp.int32(size_x)])

    table, listed, sb, to_low, to_high = prepare_call(row_count, features, rulebook, coarse_grad)
    from_low = shift(to_high, "gx", 1)
    from_high = shift(to_low, "gx", -1)
    pick_a, pairs_a, count_a = local_call(0, sb, listed, table)
    from_low, from_high, pick_a = lax.optimization_barrier((from_low, from_high, pick_a))
    sent_down, sent_up = strip_call(place, to_low, to_high, from_low, from_high)
    sb_b, sent_up, sent_down = lax.optimization_barrier((sb, sent_up, sent_down))
    got_up = shift(sent_up, "gy", 1)
    got_down = shift(sent_down, "gy", -1)
    pick_b, pairs_b, count_b = local_call(NQ // 2, sb_b, listed, table)

    owner = owner_map[:, 0]
    step_x = (owner // size_y - place_x + 1) % size_x
    step_y = (owner % size_y - place_y + 1) % size_y
    tgt = jnp.where(active, (step_y * 3 + step_x) * COARSE + coarse_slot, -1)
    tgt = tgt.reshape(NQ, BLK).astype(F32)
    hidden, up_grad, pre_grad, wg = main_call(
        sb, pairs_a, count_a, pairs_b, count_b, row_count, place, listed, weights, features,
        tgt, sent_up, sent_down, got_up, got_down, pick_a, pick_b,
    )

    share = 32 * C // devices
    parts = lax.all_to_all(wg.reshape(devices, share, C), AXES, 0, 0, tiled=True)
    table_grad = table_call(sb, listed, pre_grad, weights)
    parts, table_grad = lax.optimization_barrier((parts, table_grad))
    spread = share_call(parts)
    every = lax.all_to_all(spread, AXES, 0, 0, tiled=True).reshape(32 * C, C)
    weight_grad = every[: KV * C].reshape(KV, C, C).astype(F32) * (1.0 / math.sqrt(VOX * devices))

    to_low, to_high, mid = pool_call(tgt, hidden, table_grad)
    from_high = shift(to_low, "gx", -1)
    from_low = shift(to_high, "gx", 1)
    to_down, to_up, kept, faces = middle_call(place, mid, table_grad, from_low, from_high)
    from_above = shift(to_down, "gy", -1)
    from_below = shift(to_up, "gy", 1)
    pooled, feature_grad = final_call(
        row_count, place, table_grad, up_grad, kept, faces, from_below, from_above
    )
    return (pooled, weight_grad, feature_grad)


def solution(mesh):
    return jax.shard_map(
        shards,
        mesh=mesh,
        in_specs=(
            P(AXES, None),
            P(),
            P(None, AXES),
            P(AXES, None),
            P(AXES),
            P(AXES),
            P(AXES, None),
        ),
        out_specs=(P(AXES, None), P(), P(AXES, None)),
        check_vma=False,
    )
```

```python
import functools
import math

import jax
import jax.numpy as jnp
from jax import lax
from jax.experimental import pallas as pl
from jax.experimental.pallas import tpu as pltpu
from jax.sharding import PartitionSpec as P

BF = jnp.bfloat16
F32 = jnp.float32
AXES = ("gx", "gy")
C = 128
KV = 27
VOX = 2048
BLK = 128
NQ = VOX // BLK
ROWS = 32
FACE = 32
CYC = 16 * FACE
EXT = VOX + CYC
NLOC = VOX // BLK
NTAB = EXT // BLK
COARSE = 256
NT = 9 * COARSE
GROUP = 16
WIDE = 512
SMEM = pl.BlockSpec(memory_space=pltpu.SMEM)
VMEM = pl.BlockSpec(memory_space=pltpu.VMEM)
HBM = pl.BlockSpec(memory_space=pltpu.HBM)
DMA = pltpu.SemaphoreType.DMA


def params():
    return pltpu.CompilerParams(vmem_limit_bytes=24 << 20)


def cost(micros):
    return pl.CostEstimate(flops=0, transcendentals=0, bytes_accessed=int(micros * 3.6e6))


def counting(axis):
    return lax.broadcasted_iota(jnp.int32, (BLK, BLK), axis).astype(F32).astype(BF)


def onehot(row, numbers):
    row = jnp.broadcast_to(row.astype(F32), (BLK, BLK)).astype(BF)
    return jnp.where(row == numbers, jnp.ones((), BF), jnp.zeros((), BF))


def prepare_kernel(
    rows, features_far, rb_far, coarse_far, w_far, table, listed, blocks, to_low, to_high, flipped,
    features, rb, w, sems,
):
    half = 2 * FACE
    copies = [
        pltpu.make_async_copy(features_far, features, sems.at[0]),
        pltpu.make_async_copy(coarse_far, to_low.at[pl.ds(half, COARSE), :], sems.at[1]),
        pltpu.make_async_copy(coarse_far, to_high.at[pl.ds(half, COARSE), :], sems.at[2]),
        pltpu.make_async_copy(rb_far, rb, sems.at[3]),
        pltpu.make_async_copy(w_far, w, sems.at[4]),
    ]
    for copy in copies:
        copy.start()
    for copy in copies:
        copy.wait()
    for k in range(KV):
        flipped[:, k * C : (k + 1) * C] = w[k].T
    number = lax.broadcasted_iota(jnp.int32, (BLK, C), 0)
    cols = []
    for q in range(NQ):
        at = slice(q * BLK, (q + 1) * BLK)
        kept = jnp.where(number + q * BLK < rows[0], features[at, :].astype(F32), 0.0).astype(BF)
        table[:, at] = kept.T
        if q == 0:
            to_low[: 2 * FACE, :] = kept[: 2 * FACE]
            to_high[: 2 * FACE, :] = kept[2 * FACE :]
        part = rb[:, at]
        listed[q * ROWS : q * ROWS + KV, :] = part
        low = jnp.min(part.astype(F32), axis=1, keepdims=True).astype(jnp.int32)
        cols.append(jnp.minimum(low // BLK, NTAB - 1))
    blocks[...] = jnp.concatenate(cols, 1)


def prepare_call(*args):
    return pl.pallas_call(
        prepare_kernel,
        in_specs=[SMEM] + [HBM] * 4,
        out_specs=[VMEM] * 6,
        out_shape=[
            pltpu.VMEM((C, VOX), BF),
            pltpu.VMEM((NQ * ROWS, BLK), jnp.int32),
            jax.ShapeDtypeStruct((KV, NQ), jnp.int32),
            pltpu.VMEM((2 * FACE + COARSE, C), BF),
            pltpu.VMEM((2 * FACE + COARSE, C), BF),
            pltpu.VMEM((C, KV * C), BF),
        ],
        scratch_shapes=[
            pltpu.VMEM((VOX, C), BF),
            pltpu.VMEM((KV, VOX), jnp.int32),
            pltpu.VMEM((KV, C, C), BF),
            DMA((5,)),
        ],
        compiler_params=params(),
        cost_estimate=cost(1),
        name="prepare",
    )(*args)


def strip_kernel(place, to_low, to_high, from_low, from_high, down, up):
    half = 2 * FACE
    low = jnp.where(place[2] > 0, from_low[:half, :].astype(F32), 0.0).astype(BF)
    high = jnp.where(place[2] < place[3] - 1, from_high[:half, :].astype(F32), 0.0).astype(BF)
    for i, part in enumerate((low, to_low[:half, :], to_high[:half, :], high)):
        at = slice(i * FACE, (i + 1) * FACE)
        down[at, :] = part[:FACE]
        up[at, :] = part[FACE:]
    for i, src in enumerate((from_low, to_low, from_high)):
        at = slice(4 * FACE + i * COARSE, 4 * FACE + (i + 1) * COARSE)
        down[at, :] = src[half:, :]
        up[at, :] = src[half:, :]


def strip_call(*args):
    return pl.pallas_call(
        strip_kernel,
        in_specs=[SMEM] + [VMEM] * 4,
        out_specs=[VMEM] * 2,
        out_shape=[pltpu.VMEM((4 * FACE + 3 * COARSE, C), BF)] * 2,
        compiler_params=params(),
        cost_estimate=cost(1),
        name="strip",
    )(*args)


def local_kernel(first, sb, listed, table, pick, pairs, count):
    numbers = counting(0)

    def body(q, n):
        r0 = pl.multiple_of((q - first) * BLK, BLK)
        for k in range(KV):
            s = sb[k, q]
            pairs[n] = q * ROWS + k
            n = n + jnp.where(s < NLOC, 0, 1)
            t0 = pl.multiple_of(jnp.minimum(s, NLOC - 1) * BLK, BLK)
            row = listed[pl.ds(q * ROWS + k, 1), :] - s * BLK
            got = jnp.dot(
                table[:, pl.ds(t0, BLK)], onehot(row, numbers), preferred_element_type=F32
            )
            pick[k * C : (k + 1) * C, pl.ds(r0, BLK)] = got.astype(BF)
        return n

    count[0] = lax.fori_loop(first, first + NQ // 2, body, 0)


def local_call(first, sb, listed, table):
    return pl.pallas_call(
        functools.partial(local_kernel, first),
        in_specs=[SMEM, VMEM, VMEM],
        out_specs=[VMEM, SMEM, SMEM],
        out_shape=[
            pltpu.VMEM((KV * C, VOX // 2), BF),
            jax.ShapeDtypeStruct((KV * NQ // 2 + GROUP,), jnp.int32),
            jax.ShapeDtypeStruct((1,), jnp.int32),
        ],
        compiler_params=params(),
        cost_estimate=cost(6),
        name="pick_local",
    )(sb, listed, table)


def main_kernel(
    sb, pairs_a, count_a, pairs_b, count_b, rows, place, listed, flipped, features_far, tgt,
    sent_up, sent_down, got_up, got_down, in_a, in_b, hidden_far, up_far, pre_far, wg_far,
    pick_a, pick_b, cyc, sel, features, hidden, up, pre, wg, sems,
):
    load = pltpu.make_async_copy(features_far, features, sems.at[0])
    load.start()
    numbers = counting(0)
    lanes = counting(1)
    face = 4 * FACE
    zero = jnp.zeros((), BF)
    below = jnp.where(place[0] > 0, got_up[:face, :].astype(F32), 0.0).astype(BF)
    above = jnp.where(place[0] < place[1] - 1, got_down[:face, :].astype(F32), 0.0).astype(BF)
    four = (below, sent_down[:face, :], sent_up[:face, :], above)
    for i in range(4):
        part = jnp.concatenate([side[i * FACE : (i + 1) * FACE, :] for side in four], 0)
        cyc[:, i * BLK : (i + 1) * BLK] = part.T

    def group(first, pairs, n, pick, i, carry):
        info, gots = [], []
        for j in range(GROUP):
            e = pairs[jnp.minimum(i * GROUP + j, n - 1)]
            info.append((e, e % ROWS, e // ROWS))
        for e, k, q in info:
            s = sb[k, q]
            t0 = pl.multiple_of((s - NLOC) * BLK, BLK)
            row = listed[pl.ds(e, 1), :] - s * BLK
            got = jnp.dot(cyc[:, pl.ds(t0, BLK)], onehot(row, numbers), preferred_element_type=F32)
            gots.append(got.astype(BF))
        for got, (e, k, q) in zip(gots, info, strict=True):
            r0 = pl.multiple_of((q - first) * BLK, BLK)
            pick[pl.ds(pl.multiple_of(k * C, C), C), pl.ds(r0, BLK)] = got
        return carry

    for first, pairs, count, pick in (
        (0, pairs_a, count_a, pick_a), (NQ // 2, pairs_b, count_b, pick_b)
    ):
        n = count[0]
        fill = functools.partial(group, first, pairs, n, pick)
        lax.fori_loop(0, (n + GROUP - 1) // GROUP, fill, 0)

    def point(first, pick, p, carry):
        at = pl.ds(pl.multiple_of(first + p * WIDE, WIDE), WIDE)
        here = pl.ds(pl.multiple_of(p * WIDE, WIDE), WIDE)
        v = jnp.dot(flipped[...], pick[:, here], preferred_element_type=F32).T
        for h in range(WIDE // BLK):
            row = tgt[pl.ds(first // BLK + p * (WIDE // BLK) + h, 1), :]
            col = jnp.broadcast_to(row, (BLK, BLK)).T
            tile = jnp.floor(col * (1.0 / BLK))
            hit = jnp.where((col - tile * BLK).astype(BF) == lanes, jnp.ones((), BF), zero)
            tile = tile.astype(BF)
            for t in range(NT // BLK):
                meets = tile == jnp.asarray(t, BF)
                sel[h * BLK : (h + 1) * BLK, t * BLK : (t + 1) * BLK] = jnp.where(meets, hit, zero)
        third = 3 * COARSE
        grad = jnp.dot(sel[:, :third], got_up[face:, :], preferred_element_type=F32)
        grad += jnp.dot(sel[:, third : 2 * third], sent_up[face:, :], preferred_element_type=F32)
        grad += jnp.dot(sel[:, 2 * third :], got_down[face:, :], preferred_element_type=F32)
        sg = 1.0 / (1.0 + jnp.exp(-v))
        up[at, :] = grad.astype(BF)
        pre[at, :] = (grad * (sg * (1.0 + v * (1.0 - sg)))).astype(BF)
        out = features[at, :].astype(F32) + v * sg
        number = lax.broadcasted_iota(jnp.int32, (WIDE, C), 0) + first + p * WIDE
        hidden[at, :] = jnp.where(number < rows[0], out, 0.0).astype(BF)
        return carry

    load.wait()
    for first, pick in ((0, pick_a), (VOX // 2, pick_b)):
        lax.fori_loop(0, VOX // 2 // WIDE, functools.partial(point, first, pick), 0)

    stores = [
        pltpu.make_async_copy(pre, pre_far, sems.at[1]),
        pltpu.make_async_copy(hidden, hidden_far, sems.at[2]),
        pltpu.make_async_copy(up, up_far, sems.at[3]),
    ]
    for store in stores:
        store.start()
    wg[KV * C :, :] = jnp.zeros((wg.shape[0] - KV * C, C), BF)
    for i, (low, high) in enumerate(((0, 9 * C), (9 * C, 18 * C), (18 * C, KV * C))):
        at = slice(low, high)
        got = jnp.dot(pick_a[at, :], pre[: VOX // 2, :], preferred_element_type=F32)
        got += jnp.dot(pick_b[at, :], pre[VOX // 2 :, :], preferred_element_type=F32)
        wg[at, :] = got.astype(BF)
        done = pl.ds(low, (high if i < 2 else wg.shape[0]) - low)
        stores.append(pltpu.make_async_copy(wg.at[done, :], wg_far.at[done, :], sems.at[4 + i]))
        stores[-1].start()
    for store in stores:
        store.wait()


def main_call(*args):
    picks = pltpu.VMEM((KV * C, VOX // 2), BF)
    return pl.pallas_call(
        main_kernel,
        in_specs=[SMEM] * 7 + [VMEM] * 2 + [HBM] + [VMEM] * 7,
        out_specs=[HBM] * 4 + [VMEM] * 2,
        out_shape=[pltpu.HBM((VOX, C), BF)] * 3 + [pltpu.HBM((32 * C, C), BF), picks, picks],
        input_output_aliases={15: 4, 16: 5},
        scratch_shapes=[
            pltpu.VMEM((C, CYC), BF),
            pltpu.VMEM((WIDE, NT), BF),
            pltpu.VMEM((VOX, C), BF),
            pltpu.VMEM((VOX, C), BF),
            pltpu.VMEM((VOX, C), BF),
            pltpu.VMEM((VOX, C), BF),
            pltpu.VMEM((32 * C, C), BF),
            DMA((7,)),
        ],
        compiler_params=params(),
        cost_estimate=cost(15),
        name="conv_main",
    )(*args)[:4]


def scatter_rows(sb, listed, pre, summed):
    numbers = counting(0)

    def scatter(q, carry):
        r0 = pl.multiple_of(q * BLK, BLK)
        grads = pre[pl.ds(r0, BLK), :]
        for k in range(KV):
            row = listed[pl.ds(q * ROWS + k, 1), :] - sb[k, q] * BLK
            got = jnp.dot(onehot(row, numbers), grads, preferred_element_type=F32)
            summed[k, pl.ds(r0, BLK), :] = got.astype(BF)
        return carry

    lax.fori_loop(0, NQ, scatter, 0)


def table_kernel(sb, listed, pre_far, w_far, out, summed, pre, w, sems):
    load = pltpu.make_async_copy(w_far, w, sems.at[0])
    load.start()
    first = pltpu.make_async_copy(pre_far, pre, sems.at[1])
    first.start()
    first.wait()
    scatter_rows(sb, listed, pre, summed)
    out[...] = jnp.zeros(out.shape, F32)
    load.wait()

    def body(i, carry):
        for j in range(3):
            k = 3 * i + j
            got = lax.dot_general(
                summed[k], w[k], (((1,), (1,)), ((), ())), preferred_element_type=F32
            )
            for q in range(NQ):
                t0 = pl.multiple_of(sb[k, q] * BLK, BLK)
                out[pl.ds(t0, BLK), :] += got[q * BLK : (q + 1) * BLK, :]
        return carry

    lax.fori_loop(0, KV // 3, body, 0)


def table_call(*args):
    return pl.pallas_call(
        table_kernel,
        in_specs=[SMEM, VMEM, HBM, HBM],
        out_specs=VMEM,
        out_shape=pltpu.VMEM((EXT, C), F32),
        scratch_shapes=[
            pltpu.VMEM((KV, VOX, C), BF),
            pltpu.VMEM((VOX, C), BF),
            pltpu.VMEM((KV, C, C), BF),
            DMA((2,)),
        ],
        compiler_params=params(),
        cost_estimate=cost(14),
        name="table_grad",
    )(*args)


def share_kernel(parts, out):
    total = jnp.sum(parts[...].astype(F32), axis=0, keepdims=True).astype(BF)
    out[...] = jnp.broadcast_to(total, out.shape)


def share_call(parts):
    return pl.pallas_call(
        share_kernel,
        in_specs=[VMEM],
        out_specs=VMEM,
        out_shape=jax.ShapeDtypeStruct(parts.shape, BF),
        compiler_params=params(),
        cost_estimate=cost(1),
        name="share_sum",
    )(parts)


def pool_kernel(tgt, hidden_far, grads, to_low, to_high, mid, hidden, sem):
    load = pltpu.make_async_copy(hidden_far, hidden, sem)
    load.start()
    load.wait()
    size = 3 * COARSE
    numbers = counting(0)
    for t in range(3):
        parts = []
        for q in range(NQ):
            row = tgt[q : q + 1, :] - float(t * size)
            parts.append(
                jnp.concatenate(
                    [onehot(row - float(j * BLK), numbers) for j in range(size // BLK)], 0
                )
            )
        got = jnp.dot(jnp.concatenate(parts, 1), hidden[...], preferred_element_type=F32)
        at = slice(t * COARSE, (t + 1) * COARSE)
        to_low[at, :] = got[:COARSE].astype(BF)
        mid[at, :] = got[COARSE : 2 * COARSE]
        to_high[at, :] = got[2 * COARSE :].astype(BF)
    to_low[size:, :] = grads[VOX : VOX + BLK, :].astype(BF)
    to_high[size:, :] = grads[EXT - BLK :, :].astype(BF)


def pool_call(*args):
    return pl.pallas_call(
        pool_kernel,
        in_specs=[VMEM, HBM, VMEM],
        out_specs=[VMEM] * 3,
        out_shape=[pltpu.VMEM((3 * COARSE + BLK, C), BF)] * 2
        + [pltpu.VMEM((3 * COARSE, C), F32)],
        scratch_shapes=[pltpu.VMEM((VOX, C), BF), DMA(())],
        compiler_params=params(),
        cost_estimate=cost(3),
        name="pool_partial",
    )(*args)


def middle_kernel(place, mid, grads, from_low, from_high, to_down, to_up, kept, faces):
    cut = 3 * COARSE
    sums = mid[...] + from_low[:cut, :].astype(F32) + from_high[:cut, :].astype(F32)
    kept[...] = sums[COARSE : 2 * COARSE]
    to_down[:COARSE, :] = sums[:COARSE].astype(BF)
    to_up[:COARSE, :] = sums[2 * COARSE :].astype(BF)
    low = jnp.where(place[2] > 0, from_low[cut:, :].astype(F32), 0.0)
    high = jnp.where(place[2] < place[3] - 1, from_high[cut:, :].astype(F32), 0.0)
    for i, add in ((0, low), (1, high)):
        r = VOX + (i + 1) * BLK
        wide = grads[r : r + BLK, :] + add
        at = slice(COARSE + i * FACE, COARSE + (i + 1) * FACE)
        to_down[at, :] = wide[:FACE].astype(BF)
        to_up[at, :] = wide[3 * FACE :].astype(BF)
        faces[i * 2 * FACE : (i + 1) * 2 * FACE, :] = wide[FACE : 3 * FACE]


def middle_call(*args):
    return pl.pallas_call(
        middle_kernel,
        in_specs=[SMEM] + [VMEM] * 4,
        out_specs=[VMEM] * 4,
        out_shape=[pltpu.VMEM((COARSE + 2 * FACE, C), BF)] * 2
        + [pltpu.VMEM((COARSE, C), F32), pltpu.VMEM((4 * FACE, C), F32)],
        compiler_params=params(),
        cost_estimate=cost(0.1),
        name="middle",
    )(*args)


def final_kernel(
    rows, place, grads, up_far, kept, faces, from_below, from_above, pooled, out, up, sem
):
    load = pltpu.make_async_copy(up_far, up, sem)
    load.start()
    sums = kept[...] + from_below[:COARSE, :].astype(F32) + from_above[:COARSE, :].astype(F32)
    pooled[...] = sums.astype(BF)
    below = jnp.where(place[0] > 0, from_below[COARSE:, :].astype(F32), 0.0)
    above = jnp.where(place[0] < place[1] - 1, from_above[COARSE:, :].astype(F32), 0.0)
    add = jnp.concatenate([below[:FACE], above[:FACE], below[FACE:], above[FACE:]], 0) + faces[...]
    number = lax.broadcasted_iota(jnp.int32, (BLK, C), 0)
    load.wait()
    for q in range(NQ):
        at = slice(q * BLK, (q + 1) * BLK)
        total = grads[at, :] + up[at, :].astype(F32)
        if q == 0:
            total += add
        out[at, :] = jnp.where(number + q * BLK < rows[0], total, 0.0).astype(BF)


def final_call(*args):
    return pl.pallas_call(
        final_kernel,
        in_specs=[SMEM] * 2 + [VMEM, HBM] + [VMEM] * 4,
        out_specs=[VMEM] * 2,
        scratch_shapes=[pltpu.VMEM((VOX, C), BF), DMA(())],
        out_shape=[
            jax.ShapeDtypeStruct((COARSE, C), BF), jax.ShapeDtypeStruct((VOX, C), BF)
        ],
        compiler_params=params(),
        cost_estimate=cost(0.1),
        name="final",
    )(*args)


def far(array):
    return pltpu.with_memory_space_constraint(array, pltpu.HBM)


def shift(array, axis, step):
    size = lax.axis_size(axis)
    return lax.ppermute(array, axis, [(i, (i + step) % size) for i in range(size)])


def shards(features, weights, rulebook, owner_map, coarse_slot, row_count, coarse_grad):
    size_x, size_y = lax.axis_size("gx"), lax.axis_size("gy")
    devices = size_x * size_y
    place_x, place_y = lax.axis_index("gx"), lax.axis_index("gy")
    active = lax.iota(jnp.int32, VOX) < row_count[0]
    place = jnp.stack([place_y, jnp.int32(size_y), place_x, jnp.int32(size_x)])

    table, listed, sb, to_low, to_high, flipped = prepare_call(
        row_count, far(features), far(rulebook), far(coarse_grad), far(weights)
    )
    from_low = shift(to_high, "gx", 1)
    from_high = shift(to_low, "gx", -1)
    pick_a, pairs_a, count_a = local_call(0, sb, listed, table)
    from_low, from_high, pick_a = lax.optimization_barrier((from_low, from_high, pick_a))
    sent_down, sent_up = strip_call(place, to_low, to_high, from_low, from_high)
    sb_b, sent_up, sent_down = lax.optimization_barrier((sb, sent_up, sent_down))
    got_up = shift(sent_up, "gy", 1)
    got_down = shift(sent_down, "gy", -1)
    pick_b, pairs_b, count_b = local_call(NQ // 2, sb_b, listed, table)

    owner = owner_map[:, 0]
    step_x = (owner // size_y - place_x + 1) % size_x
    step_y = (owner % size_y - place_y + 1) % size_y
    tgt = jnp.where(active, (step_y * 3 + step_x) * COARSE + coarse_slot, -1)
    tgt = tgt.reshape(NQ, BLK).astype(F32)
    hidden, up_grad, pre_grad, wg = main_call(
        sb, pairs_a, count_a, pairs_b, count_b, row_count, place, listed, flipped, far(features),
        tgt, sent_up, sent_down, got_up, got_down, pick_a, pick_b,
    )

    share = 32 * C // devices
    parts = lax.all_to_all(wg.reshape(devices, share, C), AXES, 0, 0, tiled=True)

    table_grad = table_call(sb, listed, far(pre_grad), far(weights))
    to_low, to_high, mid = pool_call(tgt, far(hidden), table_grad)
    from_high = shift(to_low, "gx", -1)
    from_low = shift(to_high, "gx", 1)
    parts, from_low, from_high = lax.optimization_barrier((parts, from_low, from_high))
    every = lax.all_to_all(share_call(parts), AXES, 0, 0, tiled=True).reshape(32 * C, C)
    weight_grad = every[: KV * C].reshape(KV, C, C).astype(F32) * (1.0 / math.sqrt(VOX * devices))
    to_down, to_up, kept, faces = middle_call(place, mid, table_grad, from_low, from_high)
    from_above = shift(to_down, "gy", -1)
    from_below = shift(to_up, "gy", 1)
    pooled, feature_grad = final_call(
        row_count, place, table_grad, far(up_grad), kept, faces, from_below, from_above
    )
    return (pooled, weight_grad, feature_grad)


def solution(mesh):
    return jax.shard_map(
        shards,
        mesh=mesh,
        in_specs=(
            P(AXES, None),
            P(),
            P(None, AXES),
            P(AXES, None),
            P(AXES),
            P(AXES),
            P(AXES, None),
        ),
        out_specs=(P(AXES, None), P(), P(AXES, None)),
        check_vma=False,
    )
```

```python
import functools
import math

import jax
import jax.numpy as jnp
from jax import lax
from jax.experimental import pallas as pl
from jax.experimental.pallas import tpu as pltpu
from jax.sharding import PartitionSpec as P

BF = jnp.bfloat16
F32 = jnp.float32
AXES = ("gx", "gy")
C = 128
KV = 27
VOX = 2048
BLK = 128
NQ = VOX // BLK
ROWS = 32
FACE = 32
CYC = 16 * FACE
EXT = VOX + CYC
NLOC = VOX // BLK
NTAB = EXT // BLK
COARSE = 256
NT = 9 * COARSE
GROUP = 16
WIDE = 512
SPLIT = 12
SMEM = pl.BlockSpec(memory_space=pltpu.SMEM)
VMEM = pl.BlockSpec(memory_space=pltpu.VMEM)
HBM = pl.BlockSpec(memory_space=pltpu.HBM)
DMA = pltpu.SemaphoreType.DMA


def params():
    return pltpu.CompilerParams(vmem_limit_bytes=24 << 20)


def cost(micros):
    return pl.CostEstimate(flops=0, transcendentals=0, bytes_accessed=int(micros * 3.6e6))


def counting(axis):
    return lax.broadcasted_iota(jnp.int32, (BLK, BLK), axis).astype(F32).astype(BF)


def onehot(row, numbers):
    row = jnp.broadcast_to(row.astype(F32), (BLK, BLK)).astype(BF)
    return jnp.where(row == numbers, jnp.ones((), BF), jnp.zeros((), BF))


def prepare_kernel(
    rows, features_far, rb_far, coarse_far, w_far, table, listed, blocks, to_low, to_high, flipped,
    features, rb, w, sems,
):
    half = 2 * FACE
    copies = [
        pltpu.make_async_copy(features_far, features, sems.at[0]),
        pltpu.make_async_copy(coarse_far, to_low.at[pl.ds(half, COARSE), :], sems.at[1]),
        pltpu.make_async_copy(coarse_far, to_high.at[pl.ds(half, COARSE), :], sems.at[2]),
        pltpu.make_async_copy(rb_far, rb, sems.at[3]),
        pltpu.make_async_copy(w_far, w, sems.at[4]),
    ]
    for copy in copies:
        copy.start()
    for copy in copies:
        copy.wait()
    for k in range(KV):
        flipped[:, k * C : (k + 1) * C] = w[k].T
    number = lax.broadcasted_iota(jnp.int32, (BLK, C), 0)
    cols = []
    for q in range(NQ):
        at = slice(q * BLK, (q + 1) * BLK)
        kept = jnp.where(number + q * BLK < rows[0], features[at, :].astype(F32), 0.0).astype(BF)
        table[:, at] = kept.T
        if q == 0:
            to_low[: 2 * FACE, :] = kept[: 2 * FACE]
            to_high[: 2 * FACE, :] = kept[2 * FACE :]
        part = rb[:, at]
        listed[q * ROWS : q * ROWS + KV, :] = part
        low = jnp.min(part.astype(F32), axis=1, keepdims=True).astype(jnp.int32)
        cols.append(jnp.minimum(low // BLK, NTAB - 1))
    blocks[...] = jnp.concatenate(cols, 1)


def prepare_call(*args):
    return pl.pallas_call(
        prepare_kernel,
        in_specs=[SMEM] + [HBM] * 4,
        out_specs=[VMEM] * 6,
        out_shape=[
            pltpu.VMEM((C, VOX), BF),
            pltpu.VMEM((NQ * ROWS, BLK), jnp.int32),
            jax.ShapeDtypeStruct((KV, NQ), jnp.int32),
            pltpu.VMEM((2 * FACE + COARSE, C), BF),
            pltpu.VMEM((2 * FACE + COARSE, C), BF),
            pltpu.VMEM((C, KV * C), BF),
        ],
        scratch_shapes=[
            pltpu.VMEM((VOX, C), BF),
            pltpu.VMEM((KV, VOX), jnp.int32),
            pltpu.VMEM((KV, C, C), BF),
            DMA((5,)),
        ],
        compiler_params=params(),
        cost_estimate=cost(1),
        name="prepare",
    )(*args)


def strip_kernel(place, to_low, to_high, from_low, from_high, down, up):
    half = 2 * FACE
    low = jnp.where(place[2] > 0, from_low[:half, :].astype(F32), 0.0).astype(BF)
    high = jnp.where(place[2] < place[3] - 1, from_high[:half, :].astype(F32), 0.0).astype(BF)
    for i, part in enumerate((low, to_low[:half, :], to_high[:half, :], high)):
        at = slice(i * FACE, (i + 1) * FACE)
        down[at, :] = part[:FACE]
        up[at, :] = part[FACE:]
    for i, src in enumerate((from_low, to_low, from_high)):
        at = slice(4 * FACE + i * COARSE, 4 * FACE + (i + 1) * COARSE)
        down[at, :] = src[half:, :]
        up[at, :] = src[half:, :]


def strip_call(*args):
    return pl.pallas_call(
        strip_kernel,
        in_specs=[SMEM] + [VMEM] * 4,
        out_specs=[VMEM] * 2,
        out_shape=[pltpu.VMEM((4 * FACE + 3 * COARSE, C), BF)] * 2,
        compiler_params=params(),
        cost_estimate=cost(1),
        name="strip",
    )(*args)


def local_kernel(first, sb, listed, table, tgt, pick, pairs, count, sel):
    numbers = counting(0)
    lanes = counting(1)
    zero = jnp.zeros((), BF)

    def body(q, n):
        r0 = pl.multiple_of((q - first) * BLK, BLK)
        for k in range(KV):
            s = sb[k, q]
            pairs[n] = q * ROWS + k
            n = n + jnp.where(s < NLOC, 0, 1)
            t0 = pl.multiple_of(jnp.minimum(s, NLOC - 1) * BLK, BLK)
            row = listed[pl.ds(q * ROWS + k, 1), :] - s * BLK
            got = jnp.dot(
                table[:, pl.ds(t0, BLK)], onehot(row, numbers), preferred_element_type=F32
            )
            pick[k * C : (k + 1) * C, pl.ds(r0, BLK)] = got.astype(BF)
        col = jnp.broadcast_to(tgt[pl.ds(q, 1), :], (BLK, BLK)).T
        tile = jnp.floor(col * (1.0 / BLK))
        hit = jnp.where((col - tile * BLK).astype(BF) == lanes, jnp.ones((), BF), zero)
        tile = tile.astype(BF)
        for t in range(NT // BLK):
            meets = tile == jnp.asarray(t, BF)
            sel[pl.ds(r0, BLK), t * BLK : (t + 1) * BLK] = jnp.where(meets, hit, zero)
        return n

    count[0] = lax.fori_loop(first, first + NQ // 2, body, 0)


def local_call(first, *args):
    return pl.pallas_call(
        functools.partial(local_kernel, first),
        in_specs=[SMEM, VMEM, VMEM, VMEM],
        out_specs=[VMEM, SMEM, SMEM, VMEM],
        out_shape=[
            pltpu.VMEM((KV * C, VOX // 2), BF),
            jax.ShapeDtypeStruct((KV * NQ // 2 + GROUP,), jnp.int32),
            jax.ShapeDtypeStruct((1,), jnp.int32),
            pltpu.VMEM((VOX // 2, NT), BF),
        ],
        compiler_params=params(),
        cost_estimate=cost(6),
        name="pick_local",
    )(*args)


def main_kernel(
    sb, pairs_a, count_a, pairs_b, count_b, rows, place, listed, flipped, features_far, sel_a,
    sel_b, sent_up, sent_down, got_up, got_down, in_a, in_b, hidden_far, up_far, pre_far, wg_far,
    pick_a, pick_b, cyc, features, hidden, up, pre, wg, sems,
):
    load = pltpu.make_async_copy(features_far, features, sems.at[0])
    load.start()
    numbers = counting(0)
    face = 4 * FACE
    below = jnp.where(place[0] > 0, got_up[:face, :].astype(F32), 0.0).astype(BF)
    above = jnp.where(place[0] < place[1] - 1, got_down[:face, :].astype(F32), 0.0).astype(BF)
    four = (below, sent_down[:face, :], sent_up[:face, :], above)
    for i in range(4):
        part = jnp.concatenate([side[i * FACE : (i + 1) * FACE, :] for side in four], 0)
        cyc[:, i * BLK : (i + 1) * BLK] = part.T

    def group(first, pairs, n, pick, i, carry):
        info, gots = [], []
        for j in range(GROUP):
            e = pairs[jnp.minimum(i * GROUP + j, n - 1)]
            info.append((e, e % ROWS, e // ROWS))
        for e, k, q in info:
            s = sb[k, q]
            t0 = pl.multiple_of((s - NLOC) * BLK, BLK)
            row = listed[pl.ds(e, 1), :] - s * BLK
            got = jnp.dot(cyc[:, pl.ds(t0, BLK)], onehot(row, numbers), preferred_element_type=F32)
            gots.append(got.astype(BF))
        for got, (e, k, q) in zip(gots, info, strict=True):
            r0 = pl.multiple_of((q - first) * BLK, BLK)
            pick[pl.ds(pl.multiple_of(k * C, C), C), pl.ds(r0, BLK)] = got
        return carry

    for first, pairs, count, pick in (
        (0, pairs_a, count_a, pick_a), (NQ // 2, pairs_b, count_b, pick_b)
    ):
        n = count[0]
        fill = functools.partial(group, first, pairs, n, pick)
        lax.fori_loop(0, (n + GROUP - 1) // GROUP, fill, 0)

    def point(first, pick, sel, p, carry):
        at = pl.ds(pl.multiple_of(first + p * WIDE, WIDE), WIDE)
        here = pl.ds(pl.multiple_of(p * WIDE, WIDE), WIDE)
        v = jnp.dot(flipped[...], pick[:, here], preferred_element_type=F32).T
        third = 3 * COARSE
        grad = jnp.zeros((WIDE, C), F32)
        for i, src in enumerate((got_up, sent_up, got_down)):
            part = sel[here, i * third : (i + 1) * third]
            grad += jnp.dot(part, src[face:, :], preferred_element_type=F32)
        sg = 1.0 / (1.0 + jnp.exp(-v))
        up[at, :] = grad.astype(BF)
        pre[at, :] = (grad * (sg * (1.0 + v * (1.0 - sg)))).astype(BF)
        out = features[at, :].astype(F32) + v * sg
        number = lax.broadcasted_iota(jnp.int32, (WIDE, C), 0) + first + p * WIDE
        hidden[at, :] = jnp.where(number < rows[0], out, 0.0).astype(BF)
        return carry

    load.wait()
    for at in ((0, pick_a, sel_a), (VOX // 2, pick_b, sel_b)):
        lax.fori_loop(0, VOX // 2 // WIDE, functools.partial(point, *at), 0)

    stores = [
        pltpu.make_async_copy(pre, pre_far, sems.at[1]),
        pltpu.make_async_copy(hidden, hidden_far, sems.at[2]),
        pltpu.make_async_copy(up, up_far, sems.at[3]),
    ]
    for store in stores:
        store.start()
    wg[KV * C :, :] = jnp.zeros((wg.shape[0] - KV * C, C), BF)
    for i, (low, high) in enumerate(((0, 9 * C), (9 * C, 18 * C), (18 * C, KV * C))):
        at = slice(low, high)
        got = jnp.dot(pick_a[at, :], pre[: VOX // 2, :], preferred_element_type=F32)
        got += jnp.dot(pick_b[at, :], pre[VOX // 2 :, :], preferred_element_type=F32)
        wg[at, :] = got.astype(BF)
        done = pl.ds(low, (high if i < 2 else wg.shape[0]) - low)
        stores.append(pltpu.make_async_copy(wg.at[done, :], wg_far.at[done, :], sems.at[4 + i]))
        stores[-1].start()
    for store in stores:
        store.wait()


def main_call(*args):
    picks = pltpu.VMEM((KV * C, VOX // 2), BF)
    return pl.pallas_call(
        main_kernel,
        in_specs=[SMEM] * 7 + [VMEM] * 2 + [HBM] + [VMEM] * 8,
        out_specs=[HBM] * 4 + [VMEM] * 2,
        out_shape=[pltpu.HBM((VOX, C), BF)] * 3 + [pltpu.HBM((32 * C, C), BF), picks, picks],
        input_output_aliases={16: 4, 17: 5},
        scratch_shapes=[
            pltpu.VMEM((C, CYC), BF),
            pltpu.VMEM((VOX, C), BF),
            pltpu.VMEM((VOX, C), BF),
            pltpu.VMEM((VOX, C), BF),
            pltpu.VMEM((VOX, C), BF),
            pltpu.VMEM((32 * C, C), BF),
            DMA((7,)),
        ],
        compiler_params=params(),
        cost_estimate=cost(15),
        name="conv_main",
    )(*args)[:4]


def table_kernel(first, sb, listed, pre_far, w_far, out, summed, pre, w, sems):
    size = w.shape[0]
    load = pltpu.make_async_copy(w_far.at[pl.ds(first, size)], w, sems.at[0])
    chunks = [
        pltpu.make_async_copy(pre_far.at[pl.ds(r, WIDE), :], pre.at[pl.ds(r, WIDE), :], sems.at[i])
        for i, r in enumerate(range(0, VOX, WIDE), 1)
    ]
    for copy in chunks:
        copy.start()
    load.start()
    numbers = counting(0)
    out[...] = jnp.zeros(out.shape, F32)

    def scatter(q, carry):
        r0 = pl.multiple_of(q * BLK, BLK)
        grads = pre[pl.ds(r0, BLK), :]
        for k in range(size):
            row = listed[pl.ds(q * ROWS + first + k, 1), :] - sb[first + k, q] * BLK
            got = jnp.dot(onehot(row, numbers), grads, preferred_element_type=F32)
            summed[k, pl.ds(r0, BLK), :] = got.astype(BF)
        return carry

    per = WIDE // BLK
    for i, copy in enumerate(chunks):
        copy.wait()
        lax.fori_loop(i * per, (i + 1) * per, scatter, 0)
    load.wait()

    def body(i, carry):
        for j in range(3):
            k = 3 * i + j
            got = lax.dot_general(
                summed[k], w[k], (((1,), (1,)), ((), ())), preferred_element_type=F32
            )
            for q in range(NQ):
                t0 = pl.multiple_of(jnp.minimum(sb[first + k, q], NLOC) * BLK, BLK)
                out[pl.ds(t0, BLK), :] += got[q * BLK : (q + 1) * BLK, :]
        return carry

    lax.fori_loop(0, size // 3, body, 0)


def table_call(first, last, *args):
    size = last - first
    return pl.pallas_call(
        functools.partial(table_kernel, first),
        in_specs=[SMEM, VMEM, HBM, HBM],
        out_specs=VMEM,
        out_shape=pltpu.VMEM((VOX + BLK, C), F32),
        scratch_shapes=[
            pltpu.VMEM((size, VOX, C), BF),
            pltpu.VMEM((VOX, C), BF),
            pltpu.VMEM((size, C, C), BF),
            DMA((5,)),
        ],
        compiler_params=params(),
        cost_estimate=cost(size / 2 if first == 0 else 0.1),
        name="table_grad",
    )(*args)


def share_kernel(parts, out):
    total = jnp.sum(parts[...].astype(F32), axis=0, keepdims=True).astype(BF)
    out[...] = jnp.broadcast_to(total, out.shape)


def share_call(parts):
    return pl.pallas_call(
        share_kernel,
        in_specs=[VMEM],
        out_specs=VMEM,
        out_shape=jax.ShapeDtypeStruct(parts.shape, BF),
        compiler_params=params(),
        cost_estimate=cost(1),
        name="share_sum",
    )(parts)


def cycle_kernel(
    sb, pairs_a, count_a, pairs_b, count_b, listed, tgt, pre_far, hidden_far, w_far,
    to_low, to_high, mid, inner, pre, hidden, w, grads, sems,
):
    loads = [
        pltpu.make_async_copy(src, dst, sems.at[i])
        for i, (src, dst) in enumerate(((hidden_far, hidden), (pre_far, pre), (w_far, w)))
    ]
    for load in loads:
        load.start()
    size = 3 * COARSE
    numbers = counting(0)
    grads[...] = jnp.zeros(grads.shape, F32)
    loads[0].wait()
    for t in range(3):
        parts = []
        for q in range(NQ):
            row = tgt[q : q + 1, :] - float(t * size)
            parts.append(
                jnp.concatenate(
                    [onehot(row - float(j * BLK), numbers) for j in range(size // BLK)], 0
                )
            )
        got = jnp.dot(jnp.concatenate(parts, 1), hidden[...], preferred_element_type=F32)
        at = slice(t * COARSE, (t + 1) * COARSE)
        to_low[at, :] = got[:COARSE].astype(BF)
        mid[at, :] = got[COARSE : 2 * COARSE]
        to_high[at, :] = got[2 * COARSE :].astype(BF)
    loads[1].wait()
    loads[2].wait()

    def group(pairs, n, i, carry):
        info, gots = [], []
        for j in range(GROUP):
            e = pairs[jnp.minimum(i * GROUP + j, n - 1)]
            k, q = e % ROWS, e // ROWS
            s = jnp.where(i * GROUP + j < n, sb[k, q] - NLOC, NTAB - NLOC)
            info.append((e, k, q, s))
        for e, k, q, s in info:
            row = listed[pl.ds(e, 1), :] - sb[k, q] * BLK
            rows = pre[pl.ds(pl.multiple_of(q * BLK, BLK), BLK), :]
            got = jnp.dot(onehot(row, numbers), rows, preferred_element_type=F32)
            gots.append(got.astype(BF))
        outs = [
            lax.dot_general(got, w[at[1]], (((1,), (1,)), ((), ())), preferred_element_type=F32)
            for got, at in zip(gots, info, strict=True)
        ]
        for out, at in zip(outs, info, strict=True):
            grads[pl.ds(pl.multiple_of(at[3] * BLK, BLK), BLK), :] += out
        return carry

    for pairs, count in ((pairs_a, count_a), (pairs_b, count_b)):
        n = count[0]
        lax.fori_loop(0, (n + GROUP - 1) // GROUP, functools.partial(group, pairs, n), 0)
    to_low[size:, :] = grads[:BLK, :].astype(BF)
    to_high[size:, :] = grads[CYC - BLK : CYC, :].astype(BF)
    inner[...] = grads[BLK : CYC - BLK, :]


def cycle_call(*args):
    return pl.pallas_call(
        cycle_kernel,
        in_specs=[SMEM] * 5 + [VMEM] * 2 + [HBM] * 3,
        out_specs=[VMEM] * 4,
        out_shape=[pltpu.VMEM((3 * COARSE + BLK, C), BF)] * 2
        + [pltpu.VMEM((3 * COARSE, C), F32), pltpu.VMEM((CYC - 2 * BLK, C), F32)],
        scratch_shapes=[
            pltpu.VMEM((VOX, C), BF),
            pltpu.VMEM((VOX, C), BF),
            pltpu.VMEM((KV, C, C), BF),
            pltpu.VMEM((CYC + BLK, C), F32),
            DMA((3,)),
        ],
        compiler_params=params(),
        cost_estimate=cost(7),
        name="cycle_grad",
    )(*args)


def middle_kernel(place, mid, inner, from_low, from_high, to_down, to_up, kept, faces):
    cut = 3 * COARSE
    sums = mid[...] + from_low[:cut, :].astype(F32) + from_high[:cut, :].astype(F32)
    kept[...] = sums[COARSE : 2 * COARSE]
    to_down[:COARSE, :] = sums[:COARSE].astype(BF)
    to_up[:COARSE, :] = sums[2 * COARSE :].astype(BF)
    low = jnp.where(place[2] > 0, from_low[cut:, :].astype(F32), 0.0)
    high = jnp.where(place[2] < place[3] - 1, from_high[cut:, :].astype(F32), 0.0)
    for i, add in ((0, low), (1, high)):
        wide = inner[i * BLK : (i + 1) * BLK, :] + add
        at = slice(COARSE + i * FACE, COARSE + (i + 1) * FACE)
        to_down[at, :] = wide[:FACE].astype(BF)
        to_up[at, :] = wide[3 * FACE :].astype(BF)
        faces[i * 2 * FACE : (i + 1) * 2 * FACE, :] = wide[FACE : 3 * FACE]


def middle_call(*args):
    return pl.pallas_call(
        middle_kernel,
        in_specs=[SMEM] + [VMEM] * 4,
        out_specs=[VMEM] * 4,
        out_shape=[pltpu.VMEM((COARSE + 2 * FACE, C), BF)] * 2
        + [pltpu.VMEM((COARSE, C), F32), pltpu.VMEM((4 * FACE, C), F32)],
        compiler_params=params(),
        cost_estimate=cost(0.1),
        name="middle",
    )(*args)


def final_kernel(
    rows, place, grads_a, grads_b, up_far, kept, faces, from_below, from_above, pooled, out,
    up, sem,
):
    load = pltpu.make_async_copy(up_far, up, sem)
    load.start()
    sums = kept[...] + from_below[:COARSE, :].astype(F32) + from_above[:COARSE, :].astype(F32)
    pooled[...] = sums.astype(BF)
    below = jnp.where(place[0] > 0, from_below[COARSE:, :].astype(F32), 0.0)
    above = jnp.where(place[0] < place[1] - 1, from_above[COARSE:, :].astype(F32), 0.0)
    add = jnp.concatenate([below[:FACE], above[:FACE], below[FACE:], above[FACE:]], 0) + faces[...]
    number = lax.broadcasted_iota(jnp.int32, (BLK, C), 0)
    load.wait()
    for q in range(NQ):
        at = slice(q * BLK, (q + 1) * BLK)
        total = grads_a[at, :] + grads_b[at, :] + up[at, :].astype(F32)
        if q == 0:
            total += add
        out[at, :] = jnp.where(number + q * BLK < rows[0], total, 0.0).astype(BF)


def final_call(*args):
    return pl.pallas_call(
        final_kernel,
        in_specs=[SMEM] * 2 + [VMEM] * 2 + [HBM] + [VMEM] * 4,
        out_specs=[VMEM] * 2,
        scratch_shapes=[pltpu.VMEM((VOX, C), BF), DMA(())],
        out_shape=[
            jax.ShapeDtypeStruct((COARSE, C), BF), jax.ShapeDtypeStruct((VOX, C), BF)
        ],
        compiler_params=params(),
        cost_estimate=cost(0.1),
        name="final",
    )(*args)


def far(array):
    return pltpu.with_memory_space_constraint(array, pltpu.HBM)


def shift(array, axis, step):
    size = lax.axis_size(axis)
    return lax.ppermute(array, axis, [(i, (i + step) % size) for i in range(size)])


def shards(features, weights, rulebook, owner_map, coarse_slot, row_count, coarse_grad):
    size_x, size_y = lax.axis_size("gx"), lax.axis_size("gy")
    devices = size_x * size_y
    place_x, place_y = lax.axis_index("gx"), lax.axis_index("gy")
    active = lax.iota(jnp.int32, VOX) < row_count[0]
    place = jnp.stack([place_y, jnp.int32(size_y), place_x, jnp.int32(size_x)])

    table, listed, sb, to_low, to_high, flipped = prepare_call(
        row_count, far(features), far(rulebook), far(coarse_grad), far(weights)
    )
    from_low = shift(to_high, "gx", 1)
    from_high = shift(to_low, "gx", -1)

    owner = owner_map[:, 0]
    step_x = (owner // size_y - place_x + 1) % size_x
    step_y = (owner % size_y - place_y + 1) % size_y
    tgt = jnp.where(active, (step_y * 3 + step_x) * COARSE + coarse_slot, -1)
    tgt = tgt.reshape(NQ, BLK).astype(F32)

    pick_a, pairs_a, count_a, sel_a = local_call(0, sb, listed, table, tgt)
    from_low, from_high, pick_a = lax.optimization_barrier((from_low, from_high, pick_a))
    sent_down, sent_up = strip_call(place, to_low, to_high, from_low, from_high)
    sb_b, sent_up, sent_down = lax.optimization_barrier((sb, sent_up, sent_down))
    got_up = shift(sent_up, "gy", 1)
    got_down = shift(sent_down, "gy", -1)
    pick_b, pairs_b, count_b, sel_b = local_call(NQ // 2, sb_b, listed, table, tgt)
    lists = (pairs_a, count_a, pairs_b, count_b)

    hidden, up_grad, pre_grad, wg = main_call(
        sb, *lists, row_count, place, listed, flipped, far(features), sel_a, sel_b, sent_up,
        sent_down, got_up, got_down, pick_a, pick_b,
    )
    hidden, up_grad, pre_grad = far(hidden), far(up_grad), far(pre_grad)

    share = 32 * C // devices
    parts = lax.all_to_all(wg.reshape(devices, share, C), AXES, 0, 0, tiled=True)

    to_low, to_high, mid, inner = cycle_call(
        sb, *lists, listed, tgt, pre_grad, hidden, far(weights)
    )
    from_high = shift(to_low, "gx", -1)
    from_low = shift(to_high, "gx", 1)
    sb_b, to_low = lax.optimization_barrier((sb, to_low))
    grads_a = table_call(0, SPLIT, sb_b, listed, pre_grad, far(weights))
    parts, grads_a, from_low, from_high = lax.optimization_barrier(
        (parts, grads_a, from_low, from_high)
    )
    spread = share_call(parts)
    every = lax.all_to_all(spread, AXES, 0, 0, tiled=True).reshape(32 * C, C)
    weight_grad = every[: KV * C].reshape(KV, C, C).astype(F32) * (1.0 / math.sqrt(VOX * devices))
    to_down, to_up, kept, faces = middle_call(place, mid, inner, from_low, from_high)
    sb_c, to_down, to_up, spread = lax.optimization_barrier((sb, to_down, to_up, spread))
    from_above = shift(to_down, "gy", -1)
    from_below = shift(to_up, "gy", 1)
    grads_b = table_call(SPLIT, KV, sb_c, listed, pre_grad, far(weights))
    pooled, feature_grad = final_call(
        row_count, place, grads_a, grads_b, up_grad, kept, faces, from_below, from_above
    )
    return (pooled, weight_grad, feature_grad)


def solution(mesh):
    return jax.shard_map(
        shards,
        mesh=mesh,
        in_specs=(
            P(AXES, None),
            P(),
            P(None, AXES),
            P(AXES, None),
            P(AXES),
            P(AXES),
            P(AXES, None),
        ),
        out_specs=(P(AXES, None), P(), P(AXES, None)),
        check_vma=False,
    )
```

```python
import functools
import math

import jax
import jax.numpy as jnp
from jax import lax
from jax.experimental import pallas as pl
from jax.experimental.pallas import tpu as pltpu
from jax.sharding import PartitionSpec as P

BF = jnp.bfloat16
F32 = jnp.float32
AXES = ("gx", "gy")
C = 128
KV = 27
VOX = 2048
BLK = 128
NQ = VOX // BLK
ROWS = 32
FACE = 32
CYC = 16 * FACE
EXT = VOX + CYC
NLOC = VOX // BLK
NTAB = EXT // BLK
COARSE = 256
NT = 9 * COARSE
GROUP = 16
WIDE = 512
SPLIT = 6
SMEM = pl.BlockSpec(memory_space=pltpu.SMEM)
VMEM = pl.BlockSpec(memory_space=pltpu.VMEM)
HBM = pl.BlockSpec(memory_space=pltpu.HBM)
DMA = pltpu.SemaphoreType.DMA


def params():
    return pltpu.CompilerParams(vmem_limit_bytes=24 << 20)


def cost(micros):
    return pl.CostEstimate(flops=0, transcendentals=0, bytes_accessed=int(micros * 3.6e6))


def counting(axis):
    return lax.broadcasted_iota(jnp.int32, (BLK, BLK), axis).astype(F32).astype(BF)


def onehot(row, numbers):
    row = jnp.broadcast_to(row.astype(F32), (BLK, BLK)).astype(BF)
    return jnp.where(row == numbers, jnp.ones((), BF), jnp.zeros((), BF))


def prepare_kernel(
    rows, features_far, rb_far, coarse_far, table, listed, blocks, to_low, to_high,
    features, rb, sems,
):
    half = 2 * FACE
    copies = [
        pltpu.make_async_copy(features_far, features, sems.at[0]),
        pltpu.make_async_copy(rb_far, rb, sems.at[1]),
        pltpu.make_async_copy(coarse_far, to_low.at[pl.ds(half, COARSE), :], sems.at[2]),
        pltpu.make_async_copy(coarse_far, to_high.at[pl.ds(half, COARSE), :], sems.at[3]),
    ]
    for copy in copies:
        copy.start()
    copies[0].wait()
    number = lax.broadcasted_iota(jnp.int32, (BLK, C), 0)
    for q in range(NQ):
        at = slice(q * BLK, (q + 1) * BLK)
        kept = jnp.where(number + q * BLK < rows[0], features[at, :].astype(F32), 0.0).astype(BF)
        table[:, at] = kept.T
        if q == 0:
            to_low[:half, :] = kept[:half]
            to_high[:half, :] = kept[half:]
    copies[1].wait()
    cols = []
    for q in range(NQ):
        part = rb[:, q * BLK : (q + 1) * BLK]
        listed[q * ROWS : q * ROWS + KV, :] = part
        low = jnp.min(part.astype(F32), axis=1, keepdims=True).astype(jnp.int32)
        cols.append(jnp.minimum(low // BLK, NTAB - 1))
    blocks[...] = jnp.concatenate(cols, 1)
    copies[2].wait()
    copies[3].wait()


def prepare_call(*args):
    return pl.pallas_call(
        prepare_kernel,
        in_specs=[SMEM] + [HBM] * 3,
        out_specs=[VMEM] * 5,
        out_shape=[
            pltpu.VMEM((C, VOX), BF),
            pltpu.VMEM((NQ * ROWS, BLK), jnp.int32),
            jax.ShapeDtypeStruct((KV, NQ), jnp.int32),
            pltpu.VMEM((2 * FACE + COARSE, C), BF),
            pltpu.VMEM((2 * FACE + COARSE, C), BF),
        ],
        scratch_shapes=[
            pltpu.VMEM((VOX, C), BF),
            pltpu.VMEM((KV, VOX), jnp.int32),
            DMA((4,)),
        ],
        compiler_params=params(),
        cost_estimate=cost(1),
        name="prepare",
    )(*args)


def strip_kernel(place, to_low, to_high, from_low, from_high, down, up):
    half = 2 * FACE
    low = jnp.where(place[2] > 0, from_low[:half, :].astype(F32), 0.0).astype(BF)
    high = jnp.where(place[2] < place[3] - 1, from_high[:half, :].astype(F32), 0.0).astype(BF)
    for i, part in enumerate((low, to_low[:half, :], to_high[:half, :], high)):
        at = slice(i * FACE, (i + 1) * FACE)
        down[at, :] = part[:FACE]
        up[at, :] = part[FACE:]
    for i, src in enumerate((from_low, to_low, from_high)):
        at = slice(4 * FACE + i * COARSE, 4 * FACE + (i + 1) * COARSE)
        down[at, :] = src[half:, :]
        up[at, :] = src[half:, :]


def strip_call(*args):
    return pl.pallas_call(
        strip_kernel,
        in_specs=[SMEM] + [VMEM] * 4,
        out_specs=[VMEM] * 2,
        out_shape=[pltpu.VMEM((4 * FACE + 3 * COARSE, C), BF)] * 2,
        compiler_params=params(),
        cost_estimate=cost(1),
        name="strip",
    )(*args)


def local_kernel(first, sb, listed, table, tgt, w_far, pick, pairs, count, sel, flipped, w, sem):
    load = pltpu.make_async_copy(w_far.at[pl.ds(0, w.shape[0])], w, sem)
    load.start()
    numbers = counting(0)
    lanes = counting(1)
    zero = jnp.zeros((), BF)

    def body(q, n):
        r0 = pl.multiple_of((q - first) * BLK, BLK)
        for k in range(KV):
            s = sb[k, q]
            pairs[n] = q * ROWS + k
            n = n + jnp.where(s < NLOC, 0, 1)
            t0 = pl.multiple_of(jnp.minimum(s, NLOC - 1) * BLK, BLK)
            row = listed[pl.ds(q * ROWS + k, 1), :] - s * BLK
            got = jnp.dot(
                table[:, pl.ds(t0, BLK)], onehot(row, numbers), preferred_element_type=F32
            )
            pick[k * C : (k + 1) * C, pl.ds(r0, BLK)] = got.astype(BF)
        col = jnp.broadcast_to(tgt[pl.ds(q, 1), :], (BLK, BLK)).T
        tile = jnp.floor(col * (1.0 / BLK))
        hit = jnp.where((col - tile * BLK).astype(BF) == lanes, jnp.ones((), BF), zero)
        tile = tile.astype(BF)
        for t in range(NT // BLK):
            meets = tile == jnp.asarray(t, BF)
            sel[pl.ds(r0, BLK), t * BLK : (t + 1) * BLK] = jnp.where(meets, hit, zero)
        return n

    count[0] = lax.fori_loop(first, first + NQ // 2, body, 0)
    load.wait()
    for k in range(w.shape[0]):
        flipped[:, k * C : (k + 1) * C] = w[k].T


def local_call(first, turned, *args):
    return pl.pallas_call(
        functools.partial(local_kernel, first),
        in_specs=[SMEM, VMEM, VMEM, VMEM, HBM],
        out_specs=[VMEM, SMEM, SMEM, VMEM, VMEM],
        out_shape=[
            pltpu.VMEM((KV * C, VOX // 2), BF),
            jax.ShapeDtypeStruct((KV * NQ // 2 + GROUP,), jnp.int32),
            jax.ShapeDtypeStruct((1,), jnp.int32),
            pltpu.VMEM((VOX // 2, NT), BF),
            pltpu.VMEM((C, turned * C), BF),
        ],
        scratch_shapes=[pltpu.VMEM((turned, C, C), BF), DMA(())],
        compiler_params=params(),
        cost_estimate=cost(6),
        name="pick_local",
    )(*args)


def main_kernel(
    sb, pairs_a, count_a, pairs_b, count_b, rows, place, listed, flipped, features_far, sel_a,
    sel_b, sent_up, sent_down, got_up, got_down, in_a, in_b, hidden_far, up_far, pre_far, wg_far,
    pick_a, pick_b, cyc, features, hidden, up, pre, wg, sems,
):
    load = pltpu.make_async_copy(features_far, features, sems.at[0])
    load.start()
    numbers = counting(0)
    face = 4 * FACE
    below = jnp.where(place[0] > 0, got_up[:face, :].astype(F32), 0.0).astype(BF)
    above = jnp.where(place[0] < place[1] - 1, got_down[:face, :].astype(F32), 0.0).astype(BF)
    four = (below, sent_down[:face, :], sent_up[:face, :], above)
    for i in range(4):
        part = jnp.concatenate([side[i * FACE : (i + 1) * FACE, :] for side in four], 0)
        cyc[:, i * BLK : (i + 1) * BLK] = part.T

    def group(first, pairs, n, pick, i, carry):
        info, gots = [], []
        for j in range(GROUP):
            e = pairs[jnp.minimum(i * GROUP + j, n - 1)]
            info.append((e, e % ROWS, e // ROWS))
        for e, k, q in info:
            s = sb[k, q]
            t0 = pl.multiple_of((s - NLOC) * BLK, BLK)
            row = listed[pl.ds(e, 1), :] - s * BLK
            got = jnp.dot(cyc[:, pl.ds(t0, BLK)], onehot(row, numbers), preferred_element_type=F32)
            gots.append(got.astype(BF))
        for got, (e, k, q) in zip(gots, info, strict=True):
            r0 = pl.multiple_of((q - first) * BLK, BLK)
            pick[pl.ds(pl.multiple_of(k * C, C), C), pl.ds(r0, BLK)] = got
        return carry

    for first, pairs, count, pick in (
        (0, pairs_a, count_a, pick_a), (NQ // 2, pairs_b, count_b, pick_b)
    ):
        n = count[0]
        fill = functools.partial(group, first, pairs, n, pick)
        lax.fori_loop(0, (n + GROUP - 1) // GROUP, fill, 0)

    def point(first, pick, sel, p, carry):
        at = pl.ds(pl.multiple_of(first + p * WIDE, WIDE), WIDE)
        here = pl.ds(pl.multiple_of(p * WIDE, WIDE), WIDE)
        v = jnp.dot(flipped[...], pick[:, here], preferred_element_type=F32).T
        third = 3 * COARSE
        grad = jnp.zeros((WIDE, C), F32)
        for i, src in enumerate((got_up, sent_up, got_down)):
            part = sel[here, i * third : (i + 1) * third]
            grad += jnp.dot(part, src[face:, :], preferred_element_type=F32)
        sg = 1.0 / (1.0 + jnp.exp(-v))
        up[at, :] = grad.astype(BF)
        pre[at, :] = (grad * (sg * (1.0 + v * (1.0 - sg)))).astype(BF)
        out = features[at, :].astype(F32) + v * sg
        number = lax.broadcasted_iota(jnp.int32, (WIDE, C), 0) + first + p * WIDE
        hidden[at, :] = jnp.where(number < rows[0], out, 0.0).astype(BF)
        return carry

    load.wait()
    for at in ((0, pick_a, sel_a), (VOX // 2, pick_b, sel_b)):
        lax.fori_loop(0, VOX // 2 // WIDE, functools.partial(point, *at), 0)

    stores = [
        pltpu.make_async_copy(pre, pre_far, sems.at[1]),
        pltpu.make_async_copy(hidden, hidden_far, sems.at[2]),
        pltpu.make_async_copy(up, up_far, sems.at[3]),
    ]
    for store in stores:
        store.start()
    wg[KV * C :, :] = jnp.zeros((wg.shape[0] - KV * C, C), BF)
    for i, (low, high) in enumerate(((0, 9 * C), (9 * C, 18 * C), (18 * C, KV * C))):
        at = slice(low, high)
        got = jnp.dot(pick_a[at, :], pre[: VOX // 2, :], preferred_element_type=F32)
        got += jnp.dot(pick_b[at, :], pre[VOX // 2 :, :], preferred_element_type=F32)
        wg[at, :] = got.astype(BF)
        done = pl.ds(low, (high if i < 2 else wg.shape[0]) - low)
        stores.append(pltpu.make_async_copy(wg.at[done, :], wg_far.at[done, :], sems.at[4 + i]))
        stores[-1].start()
    for store in stores:
        store.wait()


def main_call(*args):
    picks = pltpu.VMEM((KV * C, VOX // 2), BF)
    return pl.pallas_call(
        main_kernel,
        in_specs=[SMEM] * 7 + [VMEM] * 2 + [HBM] + [VMEM] * 8,
        out_specs=[HBM] * 4 + [VMEM] * 2,
        out_shape=[pltpu.HBM((VOX, C), BF)] * 3 + [pltpu.HBM((32 * C, C), BF), picks, picks],
        input_output_aliases={16: 4, 17: 5},
        scratch_shapes=[
            pltpu.VMEM((C, CYC), BF),
            pltpu.VMEM((VOX, C), BF),
            pltpu.VMEM((VOX, C), BF),
            pltpu.VMEM((VOX, C), BF),
            pltpu.VMEM((VOX, C), BF),
            pltpu.VMEM((32 * C, C), BF),
            DMA((7,)),
        ],
        compiler_params=params(),
        cost_estimate=cost(15),
        name="conv_main",
    )(*args)[:4]


def table_kernel(first, sb, listed, pre_far, w_far, out, summed, pre, w, sems):
    size = w.shape[0]
    load = pltpu.make_async_copy(w_far.at[pl.ds(first, size)], w, sems.at[0])
    chunks = [
        pltpu.make_async_copy(pre_far.at[pl.ds(r, WIDE), :], pre.at[pl.ds(r, WIDE), :], sems.at[i])
        for i, r in enumerate(range(0, VOX, WIDE), 1)
    ]
    for copy in chunks:
        copy.start()
    load.start()
    numbers = counting(0)
    out[...] = jnp.zeros(out.shape, F32)

    def scatter(q, carry):
        r0 = pl.multiple_of(q * BLK, BLK)
        grads = pre[pl.ds(r0, BLK), :]
        for k in range(size):
            row = listed[pl.ds(q * ROWS + first + k, 1), :] - sb[first + k, q] * BLK
            got = jnp.dot(onehot(row, numbers), grads, preferred_element_type=F32)
            summed[k, pl.ds(r0, BLK), :] = got.astype(BF)
        return carry

    per = WIDE // BLK
    for i, copy in enumerate(chunks):
        copy.wait()
        lax.fori_loop(i * per, (i + 1) * per, scatter, 0)
    load.wait()

    def body(i, carry):
        for j in range(3):
            k = 3 * i + j
            got = lax.dot_general(
                summed[k], w[k], (((1,), (1,)), ((), ())), preferred_element_type=F32
            )
            for q in range(NQ):
                t0 = pl.multiple_of(jnp.minimum(sb[first + k, q], NLOC) * BLK, BLK)
                out[pl.ds(t0, BLK), :] += got[q * BLK : (q + 1) * BLK, :]
        return carry

    lax.fori_loop(0, size // 3, body, 0)


def table_call(first, last, *args):
    size = last - first
    return pl.pallas_call(
        functools.partial(table_kernel, first),
        in_specs=[SMEM, VMEM, HBM, HBM],
        out_specs=VMEM,
        out_shape=pltpu.VMEM((VOX + BLK, C), F32),
        scratch_shapes=[
            pltpu.VMEM((size, VOX, C), BF),
            pltpu.VMEM((VOX, C), BF),
            pltpu.VMEM((size, C, C), BF),
            DMA((5,)),
        ],
        compiler_params=params(),
        cost_estimate=cost(size / 2 if first == 0 else 0.1),
        name="table_grad",
    )(*args)


def share_kernel(parts, out):
    total = jnp.sum(parts[...].astype(F32), axis=0, keepdims=True).astype(BF)
    out[...] = jnp.broadcast_to(total, out.shape)


def share_call(parts):
    return pl.pallas_call(
        share_kernel,
        in_specs=[VMEM],
        out_specs=VMEM,
        out_shape=jax.ShapeDtypeStruct(parts.shape, BF),
        compiler_params=params(),
        cost_estimate=cost(1),
        name="share_sum",
    )(parts)


def cycle_kernel(
    sb, pairs_a, count_a, pairs_b, count_b, listed, tgt, pre_far, hidden_far, w_far,
    to_low, to_high, mid, inner, pre, hidden, w, flipped, grads, sems,
):
    loads = [
        pltpu.make_async_copy(src, dst, sems.at[i])
        for i, (src, dst) in enumerate(((hidden_far, hidden), (pre_far, pre), (w_far, w)))
    ]
    for load in loads:
        load.start()
    size = 3 * COARSE
    numbers = counting(0)
    grads[...] = jnp.zeros(grads.shape, F32)
    loads[2].wait()
    for k in range(KV):
        flipped[:, k * C : (k + 1) * C] = w[k].T
    loads[0].wait()
    for t in range(3):
        parts = []
        for q in range(NQ):
            row = tgt[q : q + 1, :] - float(t * size)
            parts.append(
                jnp.concatenate(
                    [onehot(row - float(j * BLK), numbers) for j in range(size // BLK)], 0
                )
            )
        got = jnp.dot(jnp.concatenate(parts, 1), hidden[...], preferred_element_type=F32)
        at = slice(t * COARSE, (t + 1) * COARSE)
        to_low[at, :] = got[:COARSE].astype(BF)
        mid[at, :] = got[COARSE : 2 * COARSE]
        to_high[at, :] = got[2 * COARSE :].astype(BF)
    loads[1].wait()

    def group(pairs, n, i, carry):
        info, gots = [], []
        for j in range(GROUP):
            e = pairs[jnp.minimum(i * GROUP + j, n - 1)]
            k, q = e % ROWS, e // ROWS
            s = jnp.where(i * GROUP + j < n, sb[k, q] - NLOC, NTAB - NLOC)
            info.append((e, k, q, s))
        for e, k, q, s in info:
            row = listed[pl.ds(e, 1), :] - sb[k, q] * BLK
            rows = pre[pl.ds(pl.multiple_of(q * BLK, BLK), BLK), :]
            got = jnp.dot(onehot(row, numbers), rows, preferred_element_type=F32)
            gots.append(got.astype(BF))
        outs = []
        for got, at in zip(gots, info, strict=True):
            turned = flipped[:, pl.ds(pl.multiple_of(at[1] * C, C), C)]
            outs.append(jnp.dot(got, turned, preferred_element_type=F32))
        for out, at in zip(outs, info, strict=True):
            grads[pl.ds(pl.multiple_of(at[3] * BLK, BLK), BLK), :] += out
        return carry

    for pairs, count in ((pairs_a, count_a), (pairs_b, count_b)):
        n = count[0]
        lax.fori_loop(0, (n + GROUP - 1) // GROUP, functools.partial(group, pairs, n), 0)
    to_low[size:, :] = grads[:BLK, :].astype(BF)
    to_high[size:, :] = grads[CYC - BLK : CYC, :].astype(BF)
    inner[...] = grads[BLK : CYC - BLK, :]


def cycle_call(*args):
    return pl.pallas_call(
        cycle_kernel,
        in_specs=[SMEM] * 5 + [VMEM] * 2 + [HBM] * 3,
        out_specs=[VMEM] * 4,
        out_shape=[pltpu.VMEM((3 * COARSE + BLK, C), BF)] * 2
        + [pltpu.VMEM((3 * COARSE, C), F32), pltpu.VMEM((CYC - 2 * BLK, C), F32)],
        scratch_shapes=[
            pltpu.VMEM((VOX, C), BF),
            pltpu.VMEM((VOX, C), BF),
            pltpu.VMEM((KV, C, C), BF),
            pltpu.VMEM((C, KV * C), BF),
            pltpu.VMEM((CYC + BLK, C), F32),
            DMA((3,)),
        ],
        compiler_params=params(),
        cost_estimate=cost(7),
        name="cycle_grad",
    )(*args)


def middle_kernel(place, mid, inner, from_low, from_high, to_down, to_up, kept, faces):
    cut = 3 * COARSE
    sums = mid[...] + from_low[:cut, :].astype(F32) + from_high[:cut, :].astype(F32)
    kept[...] = sums[COARSE : 2 * COARSE]
    to_down[:COARSE, :] = sums[:COARSE].astype(BF)
    to_up[:COARSE, :] = sums[2 * COARSE :].astype(BF)
    low = jnp.where(place[2] > 0, from_low[cut:, :].astype(F32), 0.0)
    high = jnp.where(place[2] < place[3] - 1, from_high[cut:, :].astype(F32), 0.0)
    for i, add in ((0, low), (1, high)):
        wide = inner[i * BLK : (i + 1) * BLK, :] + add
        at = slice(COARSE + i * FACE, COARSE + (i + 1) * FACE)
        to_down[at, :] = wide[:FACE].astype(BF)
        to_up[at, :] = wide[3 * FACE :].astype(BF)
        faces[i * 2 * FACE : (i + 1) * 2 * FACE, :] = wide[FACE : 3 * FACE]


def middle_call(*args):
    return pl.pallas_call(
        middle_kernel,
        in_specs=[SMEM] + [VMEM] * 4,
        out_specs=[VMEM] * 4,
        out_shape=[pltpu.VMEM((COARSE + 2 * FACE, C), BF)] * 2
        + [pltpu.VMEM((COARSE, C), F32), pltpu.VMEM((4 * FACE, C), F32)],
        compiler_params=params(),
        cost_estimate=cost(0.1),
        name="middle",
    )(*args)


def final_kernel(
    rows, place, grads_a, grads_b, up_far, kept, faces, from_below, from_above, pooled, out,
    up, sem,
):
    load = pltpu.make_async_copy(up_far, up, sem)
    load.start()
    sums = kept[...] + from_below[:COARSE, :].astype(F32) + from_above[:COARSE, :].astype(F32)
    pooled[...] = sums.astype(BF)
    below = jnp.where(place[0] > 0, from_below[COARSE:, :].astype(F32), 0.0)
    above = jnp.where(place[0] < place[1] - 1, from_above[COARSE:, :].astype(F32), 0.0)
    add = jnp.concatenate([below[:FACE], above[:FACE], below[FACE:], above[FACE:]], 0) + faces[...]
    number = lax.broadcasted_iota(jnp.int32, (BLK, C), 0)
    load.wait()
    for q in range(NQ):
        at = slice(q * BLK, (q + 1) * BLK)
        total = grads_a[at, :] + grads_b[at, :] + up[at, :].astype(F32)
        if q == 0:
            total += add
        out[at, :] = jnp.where(number + q * BLK < rows[0], total, 0.0).astype(BF)


def final_call(*args):
    return pl.pallas_call(
        final_kernel,
        in_specs=[SMEM] * 2 + [VMEM] * 2 + [HBM] + [VMEM] * 4,
        out_specs=[VMEM] * 2,
        scratch_shapes=[pltpu.VMEM((VOX, C), BF), DMA(())],
        out_shape=[
            jax.ShapeDtypeStruct((COARSE, C), BF), jax.ShapeDtypeStruct((VOX, C), BF)
        ],
        compiler_params=params(),
        cost_estimate=cost(0.1),
        name="final",
    )(*args)


def far(array):
    return pltpu.with_memory_space_constraint(array, pltpu.HBM)


def shift(array, axis, step):
    size = lax.axis_size(axis)
    return lax.ppermute(array, axis, [(i, (i + step) % size) for i in range(size)])


def shards(features, weights, rulebook, owner_map, coarse_slot, row_count, coarse_grad):
    size_x, size_y = lax.axis_size("gx"), lax.axis_size("gy")
    devices = size_x * size_y
    place_x, place_y = lax.axis_index("gx"), lax.axis_index("gy")
    active = lax.iota(jnp.int32, VOX) < row_count[0]
    place = jnp.stack([place_y, jnp.int32(size_y), place_x, jnp.int32(size_x)])

    table, listed, sb, to_low, to_high = prepare_call(
        row_count, far(features), far(rulebook), far(coarse_grad)
    )
    from_low = shift(to_high, "gx", 1)
    from_high = shift(to_low, "gx", -1)

    owner = owner_map[:, 0]
    step_x = (owner // size_y - place_x + 1) % size_x
    step_y = (owner % size_y - place_y + 1) % size_y
    tgt = jnp.where(active, (step_y * 3 + step_x) * COARSE + coarse_slot, -1)
    tgt = tgt.reshape(NQ, BLK).astype(F32)

    w_far = far(weights)
    first = local_call(0, KV, sb, listed, table, tgt, w_far)
    pick_a, pairs_a, count_a, sel_a, flipped = first
    from_low, from_high, pick_a = lax.optimization_barrier((from_low, from_high, pick_a))
    sent_down, sent_up = strip_call(place, to_low, to_high, from_low, from_high)
    sb_b, sent_up, sent_down = lax.optimization_barrier((sb, sent_up, sent_down))
    got_up = shift(sent_up, "gy", 1)
    got_down = shift(sent_down, "gy", -1)
    second = local_call(NQ // 2, 1, sb_b, listed, table, tgt, w_far)
    pick_b, pairs_b, count_b, sel_b, _ = second
    lists = (pairs_a, count_a, pairs_b, count_b)

    hidden, up_grad, pre_grad, wg = main_call(
        sb, *lists, row_count, place, listed, flipped, far(features), sel_a, sel_b, sent_up,
        sent_down, got_up, got_down, pick_a, pick_b,
    )
    hidden, up_grad, pre_grad = far(hidden), far(up_grad), far(pre_grad)

    share = 32 * C // devices
    parts = lax.all_to_all(wg.reshape(devices, share, C), AXES, 0, 0, tiled=True)

    to_low, to_high, mid, inner = cycle_call(
        sb, *lists, listed, tgt, pre_grad, hidden, far(weights)
    )
    from_high = shift(to_low, "gx", -1)
    from_low = shift(to_high, "gx", 1)
    sb_b, to_low = lax.optimization_barrier((sb, to_low))
    grads_a = table_call(0, SPLIT, sb_b, listed, pre_grad, far(weights))
    parts, grads_a, from_low, from_high = lax.optimization_barrier(
        (parts, grads_a, from_low, from_high)
    )
    spread = share_call(parts)
    every = lax.all_to_all(spread, AXES, 0, 0, tiled=True).reshape(32 * C, C)
    weight_grad = every[: KV * C].reshape(KV, C, C).astype(F32) * (1.0 / math.sqrt(VOX * devices))
    to_down, to_up, kept, faces = middle_call(place, mid, inner, from_low, from_high)
    sb_c, to_down, to_up, spread = lax.optimization_barrier((sb, to_down, to_up, spread))
    from_above = shift(to_down, "gy", -1)
    from_below = shift(to_up, "gy", 1)
    grads_b = table_call(SPLIT, KV, sb_c, listed, pre_grad, far(weights))
    pooled, feature_grad = final_call(
        row_count, place, grads_a, grads_b, up_grad, kept, faces, from_below, from_above
    )
    return (pooled, weight_grad, feature_grad)


def solution(mesh):
    return jax.shard_map(
        shards,
        mesh=mesh,
        in_specs=(
            P(AXES, None),
            P(),
            P(None, AXES),
            P(AXES, None),
            P(AXES),
            P(AXES),
            P(AXES, None),
        ),
        out_specs=(P(AXES, None), P(), P(AXES, None)),
        check_vma=False,
    )
```

```python
import functools
import math

import jax
import jax.numpy as jnp
from jax import lax
from jax.experimental import pallas as pl
from jax.experimental.pallas import tpu as pltpu
from jax.sharding import PartitionSpec as P

BF = jnp.bfloat16
F32 = jnp.float32
AXES = ("gx", "gy")
C = 128
KV = 27
VOX = 2048
BLK = 128
NQ = VOX // BLK
ROWS = 32
FACE = 32
CYC = 16 * FACE
EXT = VOX + CYC
NLOC = VOX // BLK
NTAB = EXT // BLK
COARSE = 256
NT = 9 * COARSE
GROUP = 16
WIDE = 512
SPLIT = 3
SMEM = pl.BlockSpec(memory_space=pltpu.SMEM)
VMEM = pl.BlockSpec(memory_space=pltpu.VMEM)
HBM = pl.BlockSpec(memory_space=pltpu.HBM)
DMA = pltpu.SemaphoreType.DMA


def params():
    return pltpu.CompilerParams(vmem_limit_bytes=24 << 20)


def cost(micros):
    return pl.CostEstimate(flops=0, transcendentals=0, bytes_accessed=int(micros * 3.6e6))


def counting(axis):
    return lax.broadcasted_iota(jnp.int32, (BLK, BLK), axis).astype(F32).astype(BF)


def onehot(row, numbers):
    row = jnp.broadcast_to(row.astype(F32), (BLK, BLK)).astype(BF)
    return jnp.where(row == numbers, jnp.ones((), BF), jnp.zeros((), BF))


def prepare_kernel(
    rows, features_far, rb_far, coarse_far, table, listed, blocks, to_low, to_high,
    features, rb, sems,
):
    half = 2 * FACE
    copies = [
        pltpu.make_async_copy(features_far, features, sems.at[0]),
        pltpu.make_async_copy(rb_far, rb, sems.at[1]),
        pltpu.make_async_copy(coarse_far, to_low.at[pl.ds(half, COARSE), :], sems.at[2]),
        pltpu.make_async_copy(coarse_far, to_high.at[pl.ds(half, COARSE), :], sems.at[3]),
    ]
    for copy in copies:
        copy.start()
    copies[0].wait()
    number = lax.broadcasted_iota(jnp.int32, (BLK, C), 0)
    for q in range(NQ):
        at = slice(q * BLK, (q + 1) * BLK)
        kept = jnp.where(number + q * BLK < rows[0], features[at, :].astype(F32), 0.0).astype(BF)
        table[:, at] = kept.T
        if q == 0:
            to_low[:half, :] = kept[:half]
            to_high[:half, :] = kept[half:]
    copies[1].wait()
    cols = []
    for q in range(NQ):
        part = rb[:, q * BLK : (q + 1) * BLK]
        listed[q * ROWS : q * ROWS + KV, :] = part
        low = jnp.min(part.astype(F32), axis=1, keepdims=True).astype(jnp.int32)
        cols.append(jnp.minimum(low // BLK, NTAB - 1))
    blocks[...] = jnp.concatenate(cols, 1)
    copies[2].wait()
    copies[3].wait()


def prepare_call(*args):
    return pl.pallas_call(
        prepare_kernel,
        in_specs=[SMEM] + [HBM] * 3,
        out_specs=[VMEM] * 5,
        out_shape=[
            pltpu.VMEM((C, VOX), BF),
            pltpu.VMEM((NQ * ROWS, BLK), jnp.int32),
            jax.ShapeDtypeStruct((KV, NQ), jnp.int32),
            pltpu.VMEM((2 * FACE + COARSE, C), BF),
            pltpu.VMEM((2 * FACE + COARSE, C), BF),
        ],
        scratch_shapes=[
            pltpu.VMEM((VOX, C), BF),
            pltpu.VMEM((KV, VOX), jnp.int32),
            DMA((4,)),
        ],
        compiler_params=params(),
        cost_estimate=cost(1),
        name="prepare",
    )(*args)


def strip_kernel(place, to_low, to_high, from_low, from_high, down, up):
    half = 2 * FACE
    low = jnp.where(place[2] > 0, from_low[:half, :].astype(F32), 0.0).astype(BF)
    high = jnp.where(place[2] < place[3] - 1, from_high[:half, :].astype(F32), 0.0).astype(BF)
    for i, part in enumerate((low, to_low[:half, :], to_high[:half, :], high)):
        at = slice(i * FACE, (i + 1) * FACE)
        down[at, :] = part[:FACE]
        up[at, :] = part[FACE:]
    for i, src in enumerate((from_low, to_low, from_high)):
        at = slice(4 * FACE + i * COARSE, 4 * FACE + (i + 1) * COARSE)
        down[at, :] = src[half:, :]
        up[at, :] = src[half:, :]


def strip_call(*args):
    return pl.pallas_call(
        strip_kernel,
        in_specs=[SMEM] + [VMEM] * 4,
        out_specs=[VMEM] * 2,
        out_shape=[pltpu.VMEM((4 * FACE + 3 * COARSE, C), BF)] * 2,
        compiler_params=params(),
        cost_estimate=cost(1),
        name="strip",
    )(*args)


def local_kernel(
    first, sb, listed, table, tgt, w_far, pick, pairs, count, sel, flipped, flipped_far, w, sem
):
    load = pltpu.make_async_copy(w_far.at[pl.ds(0, w.shape[0])], w, sem)
    load.start()
    numbers = counting(0)
    lanes = counting(1)
    zero = jnp.zeros((), BF)

    def body(q, n):
        r0 = pl.multiple_of((q - first) * BLK, BLK)
        for k in range(KV):
            s = sb[k, q]
            pairs[n] = q * ROWS + k
            n = n + jnp.where(s < NLOC, 0, 1)
            t0 = pl.multiple_of(jnp.minimum(s, NLOC - 1) * BLK, BLK)
            row = listed[pl.ds(q * ROWS + k, 1), :] - s * BLK
            got = jnp.dot(
                table[:, pl.ds(t0, BLK)], onehot(row, numbers), preferred_element_type=F32
            )
            pick[k * C : (k + 1) * C, pl.ds(r0, BLK)] = got.astype(BF)
        col = jnp.broadcast_to(tgt[pl.ds(q, 1), :], (BLK, BLK)).T
        tile = jnp.floor(col * (1.0 / BLK))
        hit = jnp.where((col - tile * BLK).astype(BF) == lanes, jnp.ones((), BF), zero)
        tile = tile.astype(BF)
        for t in range(NT // BLK):
            meets = tile == jnp.asarray(t, BF)
            sel[pl.ds(r0, BLK), t * BLK : (t + 1) * BLK] = jnp.where(meets, hit, zero)
        return n

    count[0] = lax.fori_loop(first, first + NQ // 2, body, 0)
    load.wait()
    for k in range(w.shape[0]):
        flipped[:, k * C : (k + 1) * C] = w[k].T
    store = pltpu.make_async_copy(flipped, flipped_far, sem)
    store.start()
    store.wait()


def local_call(first, turned, *args):
    return pl.pallas_call(
        functools.partial(local_kernel, first),
        in_specs=[SMEM, VMEM, VMEM, VMEM, HBM],
        out_specs=[VMEM, SMEM, SMEM, VMEM, VMEM, HBM],
        out_shape=[
            pltpu.VMEM((KV * C, VOX // 2), BF),
            jax.ShapeDtypeStruct((KV * NQ // 2 + GROUP,), jnp.int32),
            jax.ShapeDtypeStruct((1,), jnp.int32),
            pltpu.VMEM((VOX // 2, NT), BF),
            pltpu.VMEM((C, turned * C), BF),
            pltpu.HBM((C, turned * C), BF),
        ],
        scratch_shapes=[pltpu.VMEM((turned, C, C), BF), DMA(())],
        compiler_params=params(),
        cost_estimate=cost(6),
        name="pick_local",
    )(*args)


def main_kernel(
    sb, pairs_a, count_a, pairs_b, count_b, rows, place, listed, flipped, features_far, sel_a,
    sel_b, sent_up, sent_down, got_up, got_down, in_a, in_b, hidden_far, up_far, pre_far, wg_far,
    pick_a, pick_b, cyc, features, hidden, up, pre, wg, sems,
):
    load = pltpu.make_async_copy(features_far, features, sems.at[0])
    load.start()
    numbers = counting(0)
    face = 4 * FACE
    below = jnp.where(place[0] > 0, got_up[:face, :].astype(F32), 0.0).astype(BF)
    above = jnp.where(place[0] < place[1] - 1, got_down[:face, :].astype(F32), 0.0).astype(BF)
    four = (below, sent_down[:face, :], sent_up[:face, :], above)
    for i in range(4):
        part = jnp.concatenate([side[i * FACE : (i + 1) * FACE, :] for side in four], 0)
        cyc[:, i * BLK : (i + 1) * BLK] = part.T

    def group(first, pairs, n, pick, i, carry):
        info, gots = [], []
        for j in range(GROUP):
            e = pairs[jnp.minimum(i * GROUP + j, n - 1)]
            info.append((e, e % ROWS, e // ROWS))
        for e, k, q in info:
            s = sb[k, q]
            t0 = pl.multiple_of((s - NLOC) * BLK, BLK)
            row = listed[pl.ds(e, 1), :] - s * BLK
            got = jnp.dot(cyc[:, pl.ds(t0, BLK)], onehot(row, numbers), preferred_element_type=F32)
            gots.append(got.astype(BF))
        for got, (e, k, q) in zip(gots, info, strict=True):
            r0 = pl.multiple_of((q - first) * BLK, BLK)
            pick[pl.ds(pl.multiple_of(k * C, C), C), pl.ds(r0, BLK)] = got
        return carry

    for first, pairs, count, pick in (
        (0, pairs_a, count_a, pick_a), (NQ // 2, pairs_b, count_b, pick_b)
    ):
        n = count[0]
        fill = functools.partial(group, first, pairs, n, pick)
        lax.fori_loop(0, (n + GROUP - 1) // GROUP, fill, 0)

    def point(first, pick, sel, p, carry):
        at = pl.ds(pl.multiple_of(first + p * WIDE, WIDE), WIDE)
        here = pl.ds(pl.multiple_of(p * WIDE, WIDE), WIDE)
        v = jnp.dot(flipped[...], pick[:, here], preferred_element_type=F32).T
        third = 3 * COARSE
        grad = jnp.zeros((WIDE, C), F32)
        for i, src in enumerate((got_up, sent_up, got_down)):
            part = sel[here, i * third : (i + 1) * third]
            grad += jnp.dot(part, src[face:, :], preferred_element_type=F32)
        sg = 1.0 / (1.0 + jnp.exp(-v))
        up[at, :] = grad.astype(BF)
        pre[at, :] = (grad * (sg * (1.0 + v * (1.0 - sg)))).astype(BF)
        out = features[at, :].astype(F32) + v * sg
        number = lax.broadcasted_iota(jnp.int32, (WIDE, C), 0) + first + p * WIDE
        hidden[at, :] = jnp.where(number < rows[0], out, 0.0).astype(BF)
        return carry

    load.wait()
    for at in ((0, pick_a, sel_a), (VOX // 2, pick_b, sel_b)):
        lax.fori_loop(0, VOX // 2 // WIDE, functools.partial(point, *at), 0)

    stores = [
        pltpu.make_async_copy(pre, pre_far, sems.at[1]),
        pltpu.make_async_copy(hidden, hidden_far, sems.at[2]),
        pltpu.make_async_copy(up, up_far, sems.at[3]),
    ]
    for store in stores:
        store.start()
    wg[KV * C :, :] = jnp.zeros((wg.shape[0] - KV * C, C), BF)
    for i, (low, high) in enumerate(((0, 9 * C), (9 * C, 18 * C), (18 * C, KV * C))):
        at = slice(low, high)
        got = jnp.dot(pick_a[at, :], pre[: VOX // 2, :], preferred_element_type=F32)
        got += jnp.dot(pick_b[at, :], pre[VOX // 2 :, :], preferred_element_type=F32)
        wg[at, :] = got.astype(BF)
        done = pl.ds(low, (high if i < 2 else wg.shape[0]) - low)
        stores.append(pltpu.make_async_copy(wg.at[done, :], wg_far.at[done, :], sems.at[4 + i]))
        stores[-1].start()
    for store in stores:
        store.wait()


def main_call(*args):
    picks = pltpu.VMEM((KV * C, VOX // 2), BF)
    return pl.pallas_call(
        main_kernel,
        in_specs=[SMEM] * 7 + [VMEM] * 2 + [HBM] + [VMEM] * 8,
        out_specs=[HBM] * 4 + [VMEM] * 2,
        out_shape=[pltpu.HBM((VOX, C), BF)] * 3 + [pltpu.HBM((32 * C, C), BF), picks, picks],
        input_output_aliases={16: 4, 17: 5},
        scratch_shapes=[
            pltpu.VMEM((C, CYC), BF),
            pltpu.VMEM((VOX, C), BF),
            pltpu.VMEM((VOX, C), BF),
            pltpu.VMEM((VOX, C), BF),
            pltpu.VMEM((VOX, C), BF),
            pltpu.VMEM((32 * C, C), BF),
            DMA((7,)),
        ],
        compiler_params=params(),
        cost_estimate=cost(15),
        name="conv_main",
    )(*args)[:4]


def table_kernel(first, size, sb, listed, pre_far, flipped_far, *refs):
    starts, (out, summed, pre, flipped, up, sems) = refs[:-6], refs[-6:]
    load = pltpu.make_async_copy(
        flipped_far.at[:, pl.ds(first * C, size * C)], flipped, sems.at[0]
    )
    chunks = [
        pltpu.make_async_copy(pre_far.at[pl.ds(r, WIDE), :], pre.at[pl.ds(r, WIDE), :], sems.at[i])
        for i, r in enumerate(range(0, VOX, WIDE), 1)
    ]
    for copy in chunks:
        copy.start()
    load.start()
    if starts:
        begin = pltpu.make_async_copy(starts[1], up, sems.at[5])
        begin.start()
    numbers = counting(0)

    def scatter(q, carry):
        r0 = pl.multiple_of(q * BLK, BLK)
        grads = pre[pl.ds(r0, BLK), :]
        for k in range(size):
            row = listed[pl.ds(q * ROWS + first + k, 1), :] - sb[first + k, q] * BLK
            got = jnp.dot(onehot(row, numbers), grads, preferred_element_type=F32)
            summed[k, pl.ds(r0, BLK), :] = got.astype(BF)
        return carry

    per = WIDE // BLK
    for i, copy in enumerate(chunks):
        copy.wait()
        lax.fori_loop(i * per, (i + 1) * per, scatter, 0)
    load.wait()
    if starts:
        begin.wait()
        out[:VOX, :] = starts[0][:VOX, :] + up[...].astype(F32)
    else:
        out[...] = jnp.zeros(out.shape, F32)

    def body(i, carry):
        for j in range(3):
            k = 3 * i + j
            turned = flipped[:, pl.ds(pl.multiple_of(k * C, C), C)]
            got = jnp.dot(summed[k], turned, preferred_element_type=F32)
            for q in range(NQ):
                t0 = pl.multiple_of(jnp.minimum(sb[first + k, q], NLOC) * BLK, BLK)
                out[pl.ds(t0, BLK), :] += got[q * BLK : (q + 1) * BLK, :]
        return carry

    lax.fori_loop(0, size // 3, body, 0)


def table_call(first, last, *args):
    size = last - first
    return pl.pallas_call(
        functools.partial(table_kernel, first, size),
        in_specs=[SMEM, VMEM, HBM, HBM] + [VMEM, HBM][: len(args) - 4],
        out_specs=VMEM,
        out_shape=pltpu.VMEM((VOX + BLK, C), F32),
        scratch_shapes=[
            pltpu.VMEM((size, VOX, C), BF),
            pltpu.VMEM((VOX, C), BF),
            pltpu.VMEM((C, size * C), BF),
            pltpu.VMEM((VOX, C), BF),
            DMA((6,)),
        ],
        compiler_params=params(),
        cost_estimate=cost(size / 2 if first == 0 else 0.1),
        name="table_grad",
    )(*args)


def share_kernel(parts, out):
    total = jnp.sum(parts[...].astype(F32), axis=0, keepdims=True).astype(BF)
    out[...] = jnp.broadcast_to(total, out.shape)


def share_call(parts):
    return pl.pallas_call(
        share_kernel,
        in_specs=[VMEM],
        out_specs=VMEM,
        out_shape=jax.ShapeDtypeStruct(parts.shape, BF),
        compiler_params=params(),
        cost_estimate=cost(1),
        name="share_sum",
    )(parts)


def cycle_kernel(
    sb, pairs_a, count_a, pairs_b, count_b, listed, tgt, pre_far, hidden_far, flipped_far,
    to_low, to_high, mid, inner, pre, hidden, flipped, grads, sems,
):
    loads = [
        pltpu.make_async_copy(src, dst, sems.at[i])
        for i, (src, dst) in enumerate(
            ((hidden_far, hidden), (pre_far, pre), (flipped_far, flipped))
        )
    ]
    for load in loads:
        load.start()
    size = 3 * COARSE
    numbers = counting(0)
    grads[...] = jnp.zeros(grads.shape, F32)
    loads[0].wait()
    for t in range(3):
        parts = []
        for q in range(NQ):
            row = tgt[q : q + 1, :] - float(t * size)
            parts.append(
                jnp.concatenate(
                    [onehot(row - float(j * BLK), numbers) for j in range(size // BLK)], 0
                )
            )
        got = jnp.dot(jnp.concatenate(parts, 1), hidden[...], preferred_element_type=F32)
        at = slice(t * COARSE, (t + 1) * COARSE)
        to_low[at, :] = got[:COARSE].astype(BF)
        mid[at, :] = got[COARSE : 2 * COARSE]
        to_high[at, :] = got[2 * COARSE :].astype(BF)
    loads[1].wait()
    loads[2].wait()

    def group(pairs, n, i, carry):
        info, gots = [], []
        for j in range(GROUP):
            e = pairs[jnp.minimum(i * GROUP + j, n - 1)]
            k, q = e % ROWS, e // ROWS
            s = jnp.where(i * GROUP + j < n, sb[k, q] - NLOC, NTAB - NLOC)
            info.append((e, k, q, s))
        for e, k, q, s in info:
            row = listed[pl.ds(e, 1), :] - sb[k, q] * BLK
            rows = pre[pl.ds(pl.multiple_of(q * BLK, BLK), BLK), :]
            got = jnp.dot(onehot(row, numbers), rows, preferred_element_type=F32)
            gots.append(got.astype(BF))
        outs = []
        for got, at in zip(gots, info, strict=True):
            turned = flipped[:, pl.ds(pl.multiple_of(at[1] * C, C), C)]
            outs.append(jnp.dot(got, turned, preferred_element_type=F32))
        for out, at in zip(outs, info, strict=True):
            grads[pl.ds(pl.multiple_of(at[3] * BLK, BLK), BLK), :] += out
        return carry

    for pairs, count in ((pairs_a, count_a), (pairs_b, count_b)):
        n = count[0]
        lax.fori_loop(0, (n + GROUP - 1) // GROUP, functools.partial(group, pairs, n), 0)
    to_low[size:, :] = grads[:BLK, :].astype(BF)
    to_high[size:, :] = grads[CYC - BLK : CYC, :].astype(BF)
    inner[...] = grads[BLK : CYC - BLK, :]


def cycle_call(*args):
    return pl.pallas_call(
        cycle_kernel,
        in_specs=[SMEM] * 5 + [VMEM] * 2 + [HBM] * 3,
        out_specs=[VMEM] * 4,
        out_shape=[pltpu.VMEM((3 * COARSE + BLK, C), BF)] * 2
        + [pltpu.VMEM((3 * COARSE, C), F32), pltpu.VMEM((CYC - 2 * BLK, C), F32)],
        scratch_shapes=[
            pltpu.VMEM((VOX, C), BF),
            pltpu.VMEM((VOX, C), BF),
            pltpu.VMEM((C, KV * C), BF),
            pltpu.VMEM((CYC + BLK, C), F32),
            DMA((3,)),
        ],
        compiler_params=params(),
        cost_estimate=cost(7),
        name="cycle_grad",
    )(*args)


def middle_kernel(place, mid, inner, from_low, from_high, to_down, to_up, kept, faces):
    cut = 3 * COARSE
    sums = mid[...] + from_low[:cut, :].astype(F32) + from_high[:cut, :].astype(F32)
    kept[...] = sums[COARSE : 2 * COARSE]
    to_down[:COARSE, :] = sums[:COARSE].astype(BF)
    to_up[:COARSE, :] = sums[2 * COARSE :].astype(BF)
    low = jnp.where(place[2] > 0, from_low[cut:, :].astype(F32), 0.0)
    high = jnp.where(place[2] < place[3] - 1, from_high[cut:, :].astype(F32), 0.0)
    for i, add in ((0, low), (1, high)):
        wide = inner[i * BLK : (i + 1) * BLK, :] + add
        at = slice(COARSE + i * FACE, COARSE + (i + 1) * FACE)
        to_down[at, :] = wide[:FACE].astype(BF)
        to_up[at, :] = wide[3 * FACE :].astype(BF)
        faces[i * 2 * FACE : (i + 1) * 2 * FACE, :] = wide[FACE : 3 * FACE]


def middle_call(*args):
    return pl.pallas_call(
        middle_kernel,
        in_specs=[SMEM] + [VMEM] * 4,
        out_specs=[VMEM] * 4,
        out_shape=[pltpu.VMEM((COARSE + 2 * FACE, C), BF)] * 2
        + [pltpu.VMEM((COARSE, C), F32), pltpu.VMEM((4 * FACE, C), F32)],
        compiler_params=params(),
        cost_estimate=cost(0.1),
        name="middle",
    )(*args)


def final_kernel(
    rows, place, grads, kept, faces, from_below, from_above, pooled, out
):
    sums = kept[...] + from_below[:COARSE, :].astype(F32) + from_above[:COARSE, :].astype(F32)
    pooled[...] = sums.astype(BF)
    below = jnp.where(place[0] > 0, from_below[COARSE:, :].astype(F32), 0.0)
    above = jnp.where(place[0] < place[1] - 1, from_above[COARSE:, :].astype(F32), 0.0)
    add = jnp.concatenate([below[:FACE], above[:FACE], below[FACE:], above[FACE:]], 0) + faces[...]
    number = lax.broadcasted_iota(jnp.int32, (BLK, C), 0)
    for q in range(NQ):
        at = slice(q * BLK, (q + 1) * BLK)
        total = grads[at, :]
        if q == 0:
            total += add
        out[at, :] = jnp.where(number + q * BLK < rows[0], total, 0.0).astype(BF)


def final_call(*args):
    return pl.pallas_call(
        final_kernel,
        in_specs=[SMEM] * 2 + [VMEM] * 5,
        out_specs=[VMEM] * 2,
        out_shape=[
            jax.ShapeDtypeStruct((COARSE, C), BF), jax.ShapeDtypeStruct((VOX, C), BF)
        ],
        compiler_params=params(),
        cost_estimate=cost(0.1),
        name="final",
    )(*args)


def far(array):
    return pltpu.with_memory_space_constraint(array, pltpu.HBM)


def shift(array, axis, step):
    size = lax.axis_size(axis)
    return lax.ppermute(array, axis, [(i, (i + step) % size) for i in range(size)])


def shards(features, weights, rulebook, owner_map, coarse_slot, row_count, coarse_grad):
    size_x, size_y = lax.axis_size("gx"), lax.axis_size("gy")
    devices = size_x * size_y
    place_x, place_y = lax.axis_index("gx"), lax.axis_index("gy")
    active = lax.iota(jnp.int32, VOX) < row_count[0]
    place = jnp.stack([place_y, jnp.int32(size_y), place_x, jnp.int32(size_x)])

    table, listed, sb, to_low, to_high = prepare_call(
        row_count, far(features), far(rulebook), far(coarse_grad)
    )
    from_low = shift(to_high, "gx", 1)
    from_high = shift(to_low, "gx", -1)

    owner = owner_map[:, 0]
    step_x = (owner // size_y - place_x + 1) % size_x
    step_y = (owner % size_y - place_y + 1) % size_y
    tgt = jnp.where(active, (step_y * 3 + step_x) * COARSE + coarse_slot, -1)
    tgt = tgt.reshape(NQ, BLK).astype(F32)

    w_far = far(weights)
    first = local_call(0, KV, sb, listed, table, tgt, w_far)
    pick_a, pairs_a, count_a, sel_a, flipped, flipped_far = first
    flipped_far = far(flipped_far)
    from_low, from_high, pick_a = lax.optimization_barrier((from_low, from_high, pick_a))
    sent_down, sent_up = strip_call(place, to_low, to_high, from_low, from_high)
    sb_b, sent_up, sent_down = lax.optimization_barrier((sb, sent_up, sent_down))
    got_up = shift(sent_up, "gy", 1)
    got_down = shift(sent_down, "gy", -1)
    second = local_call(NQ // 2, 1, sb_b, listed, table, tgt, w_far)
    pick_b, pairs_b, count_b, sel_b = second[:4]
    lists = (pairs_a, count_a, pairs_b, count_b)

    hidden, up_grad, pre_grad, wg = main_call(
        sb, *lists, row_count, place, listed, flipped, far(features), sel_a, sel_b, sent_up,
        sent_down, got_up, got_down, pick_a, pick_b,
    )
    hidden, up_grad, pre_grad = far(hidden), far(up_grad), far(pre_grad)

    share = 32 * C // devices
    parts = lax.all_to_all(wg.reshape(devices, share, C), AXES, 0, 0, tiled=True)

    to_low, to_high, mid, inner = cycle_call(
        sb, *lists, listed, tgt, pre_grad, hidden, flipped_far
    )
    from_high = shift(to_low, "gx", -1)
    from_low = shift(to_high, "gx", 1)
    sb_b, to_low = lax.optimization_barrier((sb, to_low))
    grads_a = table_call(0, SPLIT, sb_b, listed, pre_grad, flipped_far)
    parts, grads_a, from_low, from_high = lax.optimization_barrier(
        (parts, grads_a, from_low, from_high)
    )
    spread = share_call(parts)
    every = lax.all_to_all(spread, AXES, 0, 0, tiled=True).reshape(32 * C, C)
    weight_grad = every[: KV * C].reshape(KV, C, C).astype(F32) * (1.0 / math.sqrt(VOX * devices))
    to_down, to_up, kept, faces = middle_call(place, mid, inner, from_low, from_high)
    sb_c, to_down, to_up, spread = lax.optimization_barrier((sb, to_down, to_up, spread))
    from_above = shift(to_down, "gy", -1)
    from_below = shift(to_up, "gy", 1)
    grads = table_call(SPLIT, KV, sb_c, listed, pre_grad, flipped_far, grads_a, up_grad)
    pooled, feature_grad = final_call(
        row_count, place, grads, kept, faces, from_below, from_above
    )
    return (pooled, weight_grad, feature_grad)


def solution(mesh):
    return jax.shard_map(
        shards,
        mesh=mesh,
        in_specs=(
            P(AXES, None),
            P(),
            P(None, AXES),
            P(AXES, None),
            P(AXES),
            P(AXES),
            P(AXES, None),
        ),
        out_specs=(P(AXES, None), P(), P(AXES, None)),
        check_vma=False,
    )
```

```python
import functools
import math

import jax
import jax.numpy as jnp
from jax import lax
from jax.experimental import pallas as pl
from jax.experimental.pallas import tpu as pltpu
from jax.sharding import PartitionSpec as P

BF = jnp.bfloat16
F32 = jnp.float32
AXES = ("gx", "gy")
C = 128
KV = 27
VOX = 2048
BLK = 128
NQ = VOX // BLK
ROWS = 32
FACE = 32
CYC = 16 * FACE
EXT = VOX + CYC
NLOC = VOX // BLK
NTAB = EXT // BLK
COARSE = 256
NT = 9 * COARSE
GROUP = 16
WIDE = 512
SMEM = pl.BlockSpec(memory_space=pltpu.SMEM)
VMEM = pl.BlockSpec(memory_space=pltpu.VMEM)
HBM = pl.BlockSpec(memory_space=pltpu.HBM)
DMA = pltpu.SemaphoreType.DMA


def params():
    return pltpu.CompilerParams(vmem_limit_bytes=24 << 20)


def cost(micros):
    return pl.CostEstimate(flops=0, transcendentals=0, bytes_accessed=int(micros * 3.6e6))


def counting(axis):
    return lax.broadcasted_iota(jnp.int32, (BLK, BLK), axis).astype(F32).astype(BF)


def onehot(row, numbers):
    row = jnp.broadcast_to(row.astype(F32), (BLK, BLK)).astype(BF)
    return jnp.where(row == numbers, jnp.ones((), BF), jnp.zeros((), BF))


def prepare_kernel(
    rows, features_far, rb_far, coarse_far, table, listed, blocks, to_low, to_high,
    features, rb, sems,
):
    half = 2 * FACE
    copies = [
        pltpu.make_async_copy(features_far, features, sems.at[0]),
        pltpu.make_async_copy(rb_far, rb, sems.at[1]),
        pltpu.make_async_copy(coarse_far, to_low.at[pl.ds(half, COARSE), :], sems.at[2]),
        pltpu.make_async_copy(coarse_far, to_high.at[pl.ds(half, COARSE), :], sems.at[3]),
    ]
    for copy in copies:
        copy.start()
    copies[0].wait()
    number = lax.broadcasted_iota(jnp.int32, (BLK, C), 0)
    for q in range(NQ):
        at = slice(q * BLK, (q + 1) * BLK)
        kept = jnp.where(number + q * BLK < rows[0], features[at, :].astype(F32), 0.0).astype(BF)
        table[:, at] = kept.T
        if q == 0:
            to_low[:half, :] = kept[:half]
            to_high[:half, :] = kept[half:]
    copies[1].wait()
    cols = []
    for q in range(NQ):
        part = rb[:, q * BLK : (q + 1) * BLK]
        listed[q * ROWS : q * ROWS + KV, :] = part
        low = jnp.min(part.astype(F32), axis=1, keepdims=True).astype(jnp.int32)
        cols.append(jnp.minimum(low // BLK, NTAB - 1))
    blocks[...] = jnp.concatenate(cols, 1)
    copies[2].wait()
    copies[3].wait()


def prepare_call(*args):
    return pl.pallas_call(
        prepare_kernel,
        in_specs=[SMEM] + [HBM] * 3,
        out_specs=[VMEM] * 5,
        out_shape=[
            pltpu.VMEM((C, VOX), BF),
            pltpu.VMEM((NQ * ROWS, BLK), jnp.int32),
            jax.ShapeDtypeStruct((KV, NQ), jnp.int32),
            pltpu.VMEM((2 * FACE + COARSE, C), BF),
            pltpu.VMEM((2 * FACE + COARSE, C), BF),
        ],
        scratch_shapes=[
            pltpu.VMEM((VOX, C), BF),
            pltpu.VMEM((KV, VOX), jnp.int32),
            DMA((4,)),
        ],
        compiler_params=params(),
        cost_estimate=cost(1),
        name="prepare",
    )(*args)


def strip_kernel(place, to_low, to_high, from_low, from_high, down, up):
    half = 2 * FACE
    low = jnp.where(place[2] > 0, from_low[:half, :].astype(F32), 0.0).astype(BF)
    high = jnp.where(place[2] < place[3] - 1, from_high[:half, :].astype(F32), 0.0).astype(BF)
    for i, part in enumerate((low, to_low[:half, :], to_high[:half, :], high)):
        at = slice(i * FACE, (i + 1) * FACE)
        down[at, :] = part[:FACE]
        up[at, :] = part[FACE:]
    for i, src in enumerate((from_low, to_low, from_high)):
        at = slice(4 * FACE + i * COARSE, 4 * FACE + (i + 1) * COARSE)
        down[at, :] = src[half:, :]
        up[at, :] = src[half:, :]


def strip_call(*args):
    return pl.pallas_call(
        strip_kernel,
        in_specs=[SMEM] + [VMEM] * 4,
        out_specs=[VMEM] * 2,
        out_shape=[pltpu.VMEM((4 * FACE + 3 * COARSE, C), BF)] * 2,
        compiler_params=params(),
        cost_estimate=cost(1),
        name="strip",
    )(*args)


def local_kernel(first, sb, listed, table, tgt, *refs):
    if first:
        pick, pairs, count, sel = refs
    else:
        w_far, pick, pairs, count, sel, flipped, flipped_far, w, sem = refs
        load = pltpu.make_async_copy(w_far, w, sem)
        load.start()
    numbers = counting(0)
    lanes = counting(1)
    zero = jnp.zeros((), BF)

    def body(q, n):
        r0 = pl.multiple_of((q - first) * BLK, BLK)
        for k in range(KV):
            s = sb[k, q]
            pairs[n] = q * ROWS + k
            n = n + jnp.where(s < NLOC, 0, 1)
            t0 = pl.multiple_of(jnp.minimum(s, NLOC - 1) * BLK, BLK)
            row = listed[pl.ds(q * ROWS + k, 1), :] - s * BLK
            got = jnp.dot(
                table[:, pl.ds(t0, BLK)], onehot(row, numbers), preferred_element_type=F32
            )
            pick[k * C : (k + 1) * C, pl.ds(r0, BLK)] = got.astype(BF)
        col = jnp.broadcast_to(tgt[pl.ds(q, 1), :], (BLK, BLK)).T
        tile = jnp.floor(col * (1.0 / BLK))
        hit = jnp.where((col - tile * BLK).astype(BF) == lanes, jnp.ones((), BF), zero)
        tile = tile.astype(BF)
        for t in range(NT // BLK):
            meets = tile == jnp.asarray(t, BF)
            sel[pl.ds(r0, BLK), t * BLK : (t + 1) * BLK] = jnp.where(meets, hit, zero)
        return n

    count[0] = lax.fori_loop(first, first + NQ // 2, body, 0)
    if not first:
        load.wait()
        for k in range(KV):
            flipped[:, k * C : (k + 1) * C] = w[k].T
        store = pltpu.make_async_copy(flipped, flipped_far, sem)
        store.start()
        store.wait()


def local_call(first, *args):
    turns = [pltpu.VMEM((C, KV * C), BF), pltpu.HBM((C, KV * C), BF)]
    return pl.pallas_call(
        functools.partial(local_kernel, first),
        in_specs=[SMEM, VMEM, VMEM, VMEM] + ([] if first else [HBM]),
        out_specs=[VMEM, SMEM, SMEM, VMEM] + ([] if first else [VMEM, HBM]),
        out_shape=[
            pltpu.VMEM((KV * C, VOX // 2), BF),
            jax.ShapeDtypeStruct((KV * NQ // 2 + GROUP,), jnp.int32),
            jax.ShapeDtypeStruct((1,), jnp.int32),
            pltpu.VMEM((VOX // 2, NT), BF),
        ]
        + ([] if first else turns),
        scratch_shapes=[] if first else [pltpu.VMEM((KV, C, C), BF), DMA(())],
        compiler_params=params(),
        cost_estimate=cost(6),
        name="pick_local",
    )(*args)


def main_kernel(
    sb, pairs_a, count_a, pairs_b, count_b, rows, place, listed, flipped, features_far, sel_a,
    sel_b, sent_up, sent_down, got_up, got_down, in_a, in_b, hidden_far, up_far, pre_far, wg_far,
    pick_a, pick_b, cyc, features, hidden, up, pre, wg, sems,
):
    load = pltpu.make_async_copy(features_far, features, sems.at[0])
    load.start()
    numbers = counting(0)
    face = 4 * FACE
    below = jnp.where(place[0] > 0, got_up[:face, :].astype(F32), 0.0).astype(BF)
    above = jnp.where(place[0] < place[1] - 1, got_down[:face, :].astype(F32), 0.0).astype(BF)
    four = (below, sent_down[:face, :], sent_up[:face, :], above)
    for i in range(4):
        part = jnp.concatenate([side[i * FACE : (i + 1) * FACE, :] for side in four], 0)
        cyc[:, i * BLK : (i + 1) * BLK] = part.T

    def group(first, pairs, n, pick, i, carry):
        info, gots = [], []
        for j in range(GROUP):
            e = pairs[jnp.minimum(i * GROUP + j, n - 1)]
            info.append((e, e % ROWS, e // ROWS))
        for e, k, q in info:
            s = sb[k, q]
            t0 = pl.multiple_of((s - NLOC) * BLK, BLK)
            row = listed[pl.ds(e, 1), :] - s * BLK
            got = jnp.dot(cyc[:, pl.ds(t0, BLK)], onehot(row, numbers), preferred_element_type=F32)
            gots.append(got.astype(BF))
        for got, (e, k, q) in zip(gots, info, strict=True):
            r0 = pl.multiple_of((q - first) * BLK, BLK)
            pick[pl.ds(pl.multiple_of(k * C, C), C), pl.ds(r0, BLK)] = got
        return carry

    for first, pairs, count, pick in (
        (0, pairs_a, count_a, pick_a), (NQ // 2, pairs_b, count_b, pick_b)
    ):
        n = count[0]
        fill = functools.partial(group, first, pairs, n, pick)
        lax.fori_loop(0, (n + GROUP - 1) // GROUP, fill, 0)

    def point(first, pick, sel, p, carry):
        at = pl.ds(pl.multiple_of(first + p * WIDE, WIDE), WIDE)
        here = pl.ds(pl.multiple_of(p * WIDE, WIDE), WIDE)
        v = jnp.dot(flipped[...], pick[:, here], preferred_element_type=F32).T
        third = 3 * COARSE
        grad = jnp.zeros((WIDE, C), F32)
        for i, src in enumerate((got_up, sent_up, got_down)):
            part = sel[here, i * third : (i + 1) * third]
            grad += jnp.dot(part, src[face:, :], preferred_element_type=F32)
        sg = 1.0 / (1.0 + jnp.exp(-v))
        up[at, :] = grad.astype(BF)
        pre[at, :] = (grad * (sg * (1.0 + v * (1.0 - sg)))).astype(BF)
        out = features[at, :].astype(F32) + v * sg
        number = lax.broadcasted_iota(jnp.int32, (WIDE, C), 0) + first + p * WIDE
        hidden[at, :] = jnp.where(number < rows[0], out, 0.0).astype(BF)
        return carry

    load.wait()
    for at in ((0, pick_a, sel_a), (VOX // 2, pick_b, sel_b)):
        lax.fori_loop(0, VOX // 2 // WIDE, functools.partial(point, *at), 0)

    stores = [
        pltpu.make_async_copy(pre, pre_far, sems.at[1]),
        pltpu.make_async_copy(hidden, hidden_far, sems.at[2]),
        pltpu.make_async_copy(up, up_far, sems.at[3]),
    ]
    for store in stores:
        store.start()
    wg[KV * C :, :] = jnp.zeros((wg.shape[0] - KV * C, C), BF)
    for i, (low, high) in enumerate(((0, 9 * C), (9 * C, 18 * C), (18 * C, KV * C))):
        at = slice(low, high)
        got = jnp.dot(pick_a[at, :], pre[: VOX // 2, :], preferred_element_type=F32)
        got += jnp.dot(pick_b[at, :], pre[VOX // 2 :, :], preferred_element_type=F32)
        wg[at, :] = got.astype(BF)
        done = pl.ds(low, (high if i < 2 else wg.shape[0]) - low)
        stores.append(pltpu.make_async_copy(wg.at[done, :], wg_far.at[done, :], sems.at[4 + i]))
        stores[-1].start()
    for store in stores:
        store.wait()


def main_call(*args):
    picks = pltpu.VMEM((KV * C, VOX // 2), BF)
    return pl.pallas_call(
        main_kernel,
        in_specs=[SMEM] * 7 + [VMEM] * 2 + [HBM] + [VMEM] * 8,
        out_specs=[HBM] * 4 + [VMEM] * 2,
        out_shape=[pltpu.HBM((VOX, C), BF)] * 3 + [pltpu.HBM((32 * C, C), BF), picks, picks],
        input_output_aliases={16: 4, 17: 5},
        scratch_shapes=[
            pltpu.VMEM((C, CYC), BF),
            pltpu.VMEM((VOX, C), BF),
            pltpu.VMEM((VOX, C), BF),
            pltpu.VMEM((VOX, C), BF),
            pltpu.VMEM((VOX, C), BF),
            pltpu.VMEM((32 * C, C), BF),
            DMA((7,)),
        ],
        compiler_params=params(),
        cost_estimate=cost(15),
        name="conv_main",
    )(*args)[:4]


def table_kernel(sb, listed, pre_far, flipped_far, up_far, out, summed, pre, flipped, up, sems):
    load = pltpu.make_async_copy(flipped_far, flipped, sems.at[0])
    begin = pltpu.make_async_copy(up_far, up, sems.at[5])
    chunks = [
        pltpu.make_async_copy(pre_far.at[pl.ds(r, WIDE), :], pre.at[pl.ds(r, WIDE), :], sems.at[i])
        for i, r in enumerate(range(0, VOX, WIDE), 1)
    ]
    for copy in chunks:
        copy.start()
    load.start()
    begin.start()
    numbers = counting(0)

    def scatter(q, carry):
        r0 = pl.multiple_of(q * BLK, BLK)
        grads = pre[pl.ds(r0, BLK), :]
        for k in range(KV):
            row = listed[pl.ds(q * ROWS + k, 1), :] - sb[k, q] * BLK
            got = jnp.dot(onehot(row, numbers), grads, preferred_element_type=F32)
            summed[k, pl.ds(r0, BLK), :] = got.astype(BF)
        return carry

    per = WIDE // BLK
    for i, copy in enumerate(chunks):
        copy.wait()
        lax.fori_loop(i * per, (i + 1) * per, scatter, 0)
    load.wait()
    begin.wait()
    out[:VOX, :] = up[...].astype(F32)
    out[VOX:, :] = jnp.zeros((BLK, C), F32)

    def body(i, carry):
        for j in range(3):
            k = 3 * i + j
            turned = flipped[:, pl.ds(pl.multiple_of(k * C, C), C)]
            got = jnp.dot(summed[k], turned, preferred_element_type=F32)
            for q in range(NQ):
                t0 = pl.multiple_of(jnp.minimum(sb[k, q], NLOC) * BLK, BLK)
                out[pl.ds(t0, BLK), :] += got[q * BLK : (q + 1) * BLK, :]
        return carry

    lax.fori_loop(0, KV // 3, body, 0)


def table_call(*args):
    return pl.pallas_call(
        table_kernel,
        in_specs=[SMEM, VMEM] + [HBM] * 3,
        out_specs=VMEM,
        out_shape=pltpu.VMEM((VOX + BLK, C), F32),
        scratch_shapes=[
            pltpu.VMEM((KV, VOX, C), BF),
            pltpu.VMEM((VOX, C), BF),
            pltpu.VMEM((C, KV * C), BF),
            pltpu.VMEM((VOX, C), BF),
            DMA((6,)),
        ],
        compiler_params=params(),
        cost_estimate=cost(0.1),
        name="table_grad",
    )(*args)


def share_kernel(parts, out):
    total = jnp.sum(parts[...].astype(F32), axis=0, keepdims=True).astype(BF)
    out[...] = jnp.broadcast_to(total, out.shape)


def share_call(parts):
    return pl.pallas_call(
        share_kernel,
        in_specs=[VMEM],
        out_specs=VMEM,
        out_shape=jax.ShapeDtypeStruct(parts.shape, BF),
        compiler_params=params(),
        cost_estimate=cost(1),
        name="share_sum",
    )(parts)


def cycle_kernel(
    sb, pairs_a, count_a, pairs_b, count_b, listed, tgt, pre_far, hidden_far, flipped_far,
    to_low, to_high, mid, inner, pre, hidden, flipped, grads, sems,
):
    loads = [
        pltpu.make_async_copy(src, dst, sems.at[i])
        for i, (src, dst) in enumerate(
            ((hidden_far, hidden), (pre_far, pre), (flipped_far, flipped))
        )
    ]
    for load in loads:
        load.start()
    size = 3 * COARSE
    numbers = counting(0)
    grads[...] = jnp.zeros(grads.shape, F32)
    loads[0].wait()
    for t in range(3):
        parts = []
        for q in range(NQ):
            row = tgt[q : q + 1, :] - float(t * size)
            parts.append(
                jnp.concatenate(
                    [onehot(row - float(j * BLK), numbers) for j in range(size // BLK)], 0
                )
            )
        got = jnp.dot(jnp.concatenate(parts, 1), hidden[...], preferred_element_type=F32)
        at = slice(t * COARSE, (t + 1) * COARSE)
        to_low[at, :] = got[:COARSE].astype(BF)
        mid[at, :] = got[COARSE : 2 * COARSE]
        to_high[at, :] = got[2 * COARSE :].astype(BF)
    loads[1].wait()
    loads[2].wait()

    def group(pairs, n, i, carry):
        info, gots = [], []
        for j in range(GROUP):
            e = pairs[jnp.minimum(i * GROUP + j, n - 1)]
            k, q = e % ROWS, e // ROWS
            s = jnp.where(i * GROUP + j < n, sb[k, q] - NLOC, NTAB - NLOC)
            info.append((e, k, q, s))
        for e, k, q, s in info:
            row = listed[pl.ds(e, 1), :] - sb[k, q] * BLK
            rows = pre[pl.ds(pl.multiple_of(q * BLK, BLK), BLK), :]
            got = jnp.dot(onehot(row, numbers), rows, preferred_element_type=F32)
            gots.append(got.astype(BF))
        outs = []
        for got, at in zip(gots, info, strict=True):
            turned = flipped[:, pl.ds(pl.multiple_of(at[1] * C, C), C)]
            outs.append(jnp.dot(got, turned, preferred_element_type=F32))
        for out, at in zip(outs, info, strict=True):
            grads[pl.ds(pl.multiple_of(at[3] * BLK, BLK), BLK), :] += out
        return carry

    for pairs, count in ((pairs_a, count_a), (pairs_b, count_b)):
        n = count[0]
        lax.fori_loop(0, (n + GROUP - 1) // GROUP, functools.partial(group, pairs, n), 0)
    to_low[size:, :] = grads[:BLK, :].astype(BF)
    to_high[size:, :] = grads[CYC - BLK : CYC, :].astype(BF)
    inner[...] = grads[BLK : CYC - BLK, :]


def cycle_call(*args):
    return pl.pallas_call(
        cycle_kernel,
        in_specs=[SMEM] * 5 + [VMEM] * 2 + [HBM] * 3,
        out_specs=[VMEM] * 4,
        out_shape=[pltpu.VMEM((3 * COARSE + BLK, C), BF)] * 2
        + [pltpu.VMEM((3 * COARSE, C), F32), pltpu.VMEM((CYC - 2 * BLK, C), F32)],
        scratch_shapes=[
            pltpu.VMEM((VOX, C), BF),
            pltpu.VMEM((VOX, C), BF),
            pltpu.VMEM((C, KV * C), BF),
            pltpu.VMEM((CYC + BLK, C), F32),
            DMA((3,)),
        ],
        compiler_params=params(),
        cost_estimate=cost(7),
        name="cycle_grad",
    )(*args)


def middle_kernel(place, mid, inner, from_low, from_high, to_down, to_up, kept, faces):
    cut = 3 * COARSE
    sums = mid[...] + from_low[:cut, :].astype(F32) + from_high[:cut, :].astype(F32)
    kept[...] = sums[COARSE : 2 * COARSE]
    to_down[:COARSE, :] = sums[:COARSE].astype(BF)
    to_up[:COARSE, :] = sums[2 * COARSE :].astype(BF)
    low = jnp.where(place[2] > 0, from_low[cut:, :].astype(F32), 0.0)
    high = jnp.where(place[2] < place[3] - 1, from_high[cut:, :].astype(F32), 0.0)
    for i, add in ((0, low), (1, high)):
        wide = inner[i * BLK : (i + 1) * BLK, :] + add
        at = slice(COARSE + i * FACE, COARSE + (i + 1) * FACE)
        to_down[at, :] = wide[:FACE].astype(BF)
        to_up[at, :] = wide[3 * FACE :].astype(BF)
        faces[i * 2 * FACE : (i + 1) * 2 * FACE, :] = wide[FACE : 3 * FACE]


def middle_call(*args):
    return pl.pallas_call(
        middle_kernel,
        in_specs=[SMEM] + [VMEM] * 4,
        out_specs=[VMEM] * 4,
        out_shape=[pltpu.VMEM((COARSE + 2 * FACE, C), BF)] * 2
        + [pltpu.VMEM((COARSE, C), F32), pltpu.VMEM((4 * FACE, C), F32)],
        compiler_params=params(),
        cost_estimate=cost(0.1),
        name="middle",
    )(*args)


def final_kernel(
    rows, place, grads, kept, faces, from_below, from_above, pooled, out
):
    sums = kept[...] + from_below[:COARSE, :].astype(F32) + from_above[:COARSE, :].astype(F32)
    pooled[...] = sums.astype(BF)
    below = jnp.where(place[0] > 0, from_below[COARSE:, :].astype(F32), 0.0)
    above = jnp.where(place[0] < place[1] - 1, from_above[COARSE:, :].astype(F32), 0.0)
    add = jnp.concatenate([below[:FACE], above[:FACE], below[FACE:], above[FACE:]], 0) + faces[...]
    number = lax.broadcasted_iota(jnp.int32, (BLK, C), 0)
    for q in range(NQ):
        at = slice(q * BLK, (q + 1) * BLK)
        total = grads[at, :]
        if q == 0:
            total += add
        out[at, :] = jnp.where(number + q * BLK < rows[0], total, 0.0).astype(BF)


def final_call(*args):
    return pl.pallas_call(
        final_kernel,
        in_specs=[SMEM] * 2 + [VMEM] * 5,
        out_specs=[VMEM] * 2,
        out_shape=[
            jax.ShapeDtypeStruct((COARSE, C), BF), jax.ShapeDtypeStruct((VOX, C), BF)
        ],
        compiler_params=params(),
        cost_estimate=cost(0.1),
        name="final",
    )(*args)


def far(array):
    return pltpu.with_memory_space_constraint(array, pltpu.HBM)


def shift(array, axis, step):
    size = lax.axis_size(axis)
    return lax.ppermute(array, axis, [(i, (i + step) % size) for i in range(size)])


def shards(features, weights, rulebook, owner_map, coarse_slot, row_count, coarse_grad):
    size_x, size_y = lax.axis_size("gx"), lax.axis_size("gy")
    devices = size_x * size_y
    place_x, place_y = lax.axis_index("gx"), lax.axis_index("gy")
    active = lax.iota(jnp.int32, VOX) < row_count[0]
    place = jnp.stack([place_y, jnp.int32(size_y), place_x, jnp.int32(size_x)])

    table, listed, sb, to_low, to_high = prepare_call(
        row_count, far(features), far(rulebook), far(coarse_grad)
    )
    from_low = shift(to_high, "gx", 1)
    from_high = shift(to_low, "gx", -1)

    owner = owner_map[:, 0]
    step_x = (owner // size_y - place_x + 1) % size_x
    step_y = (owner % size_y - place_y + 1) % size_y
    tgt = jnp.where(active, (step_y * 3 + step_x) * COARSE + coarse_slot, -1)
    tgt = tgt.reshape(NQ, BLK).astype(F32)

    first = local_call(0, sb, listed, table, tgt, far(weights))
    pick_a, pairs_a, count_a, sel_a, flipped, flipped_far = first
    flipped_far = far(flipped_far)
    from_low, from_high, pick_a = lax.optimization_barrier((from_low, from_high, pick_a))
    sent_down, sent_up = strip_call(place, to_low, to_high, from_low, from_high)
    sb_b, sent_up, sent_down = lax.optimization_barrier((sb, sent_up, sent_down))
    got_up = shift(sent_up, "gy", 1)
    got_down = shift(sent_down, "gy", -1)
    pick_b, pairs_b, count_b, sel_b = local_call(NQ // 2, sb_b, listed, table, tgt)
    lists = (pairs_a, count_a, pairs_b, count_b)

    hidden, up_grad, pre_grad, wg = main_call(
        sb, *lists, row_count, place, listed, flipped, far(features), sel_a, sel_b, sent_up,
        sent_down, got_up, got_down, pick_a, pick_b,
    )
    hidden, up_grad, pre_grad = far(hidden), far(up_grad), far(pre_grad)

    share = 32 * C // devices
    parts = lax.all_to_all(wg.reshape(devices, share, C), AXES, 0, 0, tiled=True)

    to_low, to_high, mid, inner = cycle_call(
        sb, *lists, listed, tgt, pre_grad, hidden, flipped_far
    )
    from_high = shift(to_low, "gx", -1)
    from_low = shift(to_high, "gx", 1)
    parts, from_low, from_high = lax.optimization_barrier((parts, from_low, from_high))
    spread = share_call(parts)
    every = lax.all_to_all(spread, AXES, 0, 0, tiled=True).reshape(32 * C, C)
    weight_grad = every[: KV * C].reshape(KV, C, C).astype(F32) * (1.0 / math.sqrt(VOX * devices))
    to_down, to_up, kept, faces = middle_call(place, mid, inner, from_low, from_high)
    sb_c, to_down, to_up, spread = lax.optimization_barrier((sb, to_down, to_up, spread))
    from_above = shift(to_down, "gy", -1)
    from_below = shift(to_up, "gy", 1)
    grads = table_call(sb_c, listed, pre_grad, flipped_far, up_grad)
    pooled, feature_grad = final_call(
        row_count, place, grads, kept, faces, from_below, from_above
    )
    return (pooled, weight_grad, feature_grad)


def solution(mesh):
    return jax.shard_map(
        shards,
        mesh=mesh,
        in_specs=(
            P(AXES, None),
            P(),
            P(None, AXES),
            P(AXES, None),
            P(AXES),
            P(AXES),
            P(AXES, None),
        ),
        out_specs=(P(AXES, None), P(), P(AXES, None)),
        check_vma=False,
    )
```

```python
import functools
import math

import jax
import jax.numpy as jnp
from jax import lax
from jax.experimental import pallas as pl
from jax.experimental.pallas import tpu as pltpu
from jax.sharding import PartitionSpec as P

BF = jnp.bfloat16
F32 = jnp.float32
AXES = ("gx", "gy")
C = 128
KV = 27
VOX = 2048
BLK = 128
NQ = VOX // BLK
ROWS = 32
FACE = 32
CYC = 16 * FACE
EXT = VOX + CYC
NLOC = VOX // BLK
NTAB = EXT // BLK
COARSE = 256
NT = 9 * COARSE
GROUP = 16
WIDE = 512
SPLIT = 6
SMEM = pl.BlockSpec(memory_space=pltpu.SMEM)
VMEM = pl.BlockSpec(memory_space=pltpu.VMEM)
HBM = pl.BlockSpec(memory_space=pltpu.HBM)
DMA = pltpu.SemaphoreType.DMA


def params():
    return pltpu.CompilerParams(vmem_limit_bytes=24 << 20)


def cost(micros):
    return pl.CostEstimate(flops=0, transcendentals=0, bytes_accessed=int(micros * 3.6e6))


def counting(axis):
    return lax.broadcasted_iota(jnp.int32, (BLK, BLK), axis).astype(F32).astype(BF)


def onehot(row, numbers):
    row = jnp.broadcast_to(row.astype(F32), (BLK, BLK)).astype(BF)
    return jnp.where(row == numbers, jnp.ones((), BF), jnp.zeros((), BF))


def prepare_kernel(
    rows, features_far, rb_far, coarse_far, table, listed, blocks, to_low, to_high,
    features, rb, sems,
):
    half = 2 * FACE
    copies = [
        pltpu.make_async_copy(features_far, features, sems.at[0]),
        pltpu.make_async_copy(rb_far, rb, sems.at[1]),
        pltpu.make_async_copy(coarse_far, to_low.at[pl.ds(half, COARSE), :], sems.at[2]),
        pltpu.make_async_copy(coarse_far, to_high.at[pl.ds(half, COARSE), :], sems.at[3]),
    ]
    for copy in copies:
        copy.start()
    copies[0].wait()
    number = lax.broadcasted_iota(jnp.int32, (BLK, C), 0)
    for q in range(NQ):
        at = slice(q * BLK, (q + 1) * BLK)
        kept = jnp.where(number + q * BLK < rows[0], features[at, :].astype(F32), 0.0).astype(BF)
        table[:, at] = kept.T
        if q == 0:
            to_low[:half, :] = kept[:half]
            to_high[:half, :] = kept[half:]
    copies[1].wait()
    cols = []
    for q in range(NQ):
        part = rb[:, q * BLK : (q + 1) * BLK]
        listed[q * ROWS : q * ROWS + KV, :] = part
        low = jnp.min(part.astype(F32), axis=1, keepdims=True).astype(jnp.int32)
        cols.append(jnp.minimum(low // BLK, NTAB - 1))
    blocks[...] = jnp.concatenate(cols, 1)
    copies[2].wait()
    copies[3].wait()


def prepare_call(*args):
    return pl.pallas_call(
        prepare_kernel,
        in_specs=[SMEM] + [HBM] * 3,
        out_specs=[VMEM] * 5,
        out_shape=[
            pltpu.VMEM((C, VOX), BF),
            pltpu.VMEM((NQ * ROWS, BLK), jnp.int32),
            jax.ShapeDtypeStruct((KV, NQ), jnp.int32),
            pltpu.VMEM((2 * FACE + COARSE, C), BF),
            pltpu.VMEM((2 * FACE + COARSE, C), BF),
        ],
        scratch_shapes=[
            pltpu.VMEM((VOX, C), BF),
            pltpu.VMEM((KV, VOX), jnp.int32),
            DMA((4,)),
        ],
        compiler_params=params(),
        cost_estimate=cost(1),
        name="prepare",
    )(*args)


def strip_kernel(place, to_low, to_high, from_low, from_high, down, up):
    half = 2 * FACE
    low = jnp.where(place[2] > 0, from_low[:half, :].astype(F32), 0.0).astype(BF)
    high = jnp.where(place[2] < place[3] - 1, from_high[:half, :].astype(F32), 0.0).astype(BF)
    for i, part in enumerate((low, to_low[:half, :], to_high[:half, :], high)):
        at = slice(i * FACE, (i + 1) * FACE)
        down[at, :] = part[:FACE]
        up[at, :] = part[FACE:]
    for i, src in enumerate((from_low, to_low, from_high)):
        at = slice(4 * FACE + i * COARSE, 4 * FACE + (i + 1) * COARSE)
        down[at, :] = src[half:, :]
        up[at, :] = src[half:, :]


def strip_call(*args):
    return pl.pallas_call(
        strip_kernel,
        in_specs=[SMEM] + [VMEM] * 4,
        out_specs=[VMEM] * 2,
        out_shape=[pltpu.VMEM((4 * FACE + 3 * COARSE, C), BF)] * 2,
        compiler_params=params(),
        cost_estimate=cost(1),
        name="strip",
    )(*args)


def local_kernel(first, sb, listed, table, tgt, *refs):
    if first:
        pick, pairs, count, sel = refs
    else:
        w_far, pick, pairs, count, sel, flipped, flipped_far, w, sem = refs
        load = pltpu.make_async_copy(w_far, w, sem)
        load.start()
    numbers = counting(0)
    lanes = counting(1)
    zero = jnp.zeros((), BF)

    def body(q, n):
        r0 = pl.multiple_of((q - first) * BLK, BLK)
        for k in range(KV):
            s = sb[k, q]
            pairs[n] = q * ROWS + k
            n = n + jnp.where(s < NLOC, 0, 1)
            t0 = pl.multiple_of(jnp.minimum(s, NLOC - 1) * BLK, BLK)
            row = listed[pl.ds(q * ROWS + k, 1), :] - s * BLK
            got = jnp.dot(
                table[:, pl.ds(t0, BLK)], onehot(row, numbers), preferred_element_type=F32
            )
            pick[k * C : (k + 1) * C, pl.ds(r0, BLK)] = got.astype(BF)
        col = jnp.broadcast_to(tgt[pl.ds(q, 1), :], (BLK, BLK)).T
        tile = jnp.floor(col * (1.0 / BLK))
        hit = jnp.where((col - tile * BLK).astype(BF) == lanes, jnp.ones((), BF), zero)
        tile = tile.astype(BF)
        for t in range(NT // BLK):
            meets = tile == jnp.asarray(t, BF)
            sel[pl.ds(r0, BLK), t * BLK : (t + 1) * BLK] = jnp.where(meets, hit, zero)
        return n

    count[0] = lax.fori_loop(first, first + NQ // 2, body, 0)
    if not first:
        load.wait()
        for k in range(KV):
            flipped[:, k * C : (k + 1) * C] = w[k].T
        store = pltpu.make_async_copy(flipped, flipped_far, sem)
        store.start()
        store.wait()


def local_call(first, *args):
    turns = [pltpu.VMEM((C, KV * C), BF), pltpu.HBM((C, KV * C), BF)]
    return pl.pallas_call(
        functools.partial(local_kernel, first),
        in_specs=[SMEM, VMEM, VMEM, VMEM] + ([] if first else [HBM]),
        out_specs=[VMEM, SMEM, SMEM, VMEM] + ([] if first else [VMEM, HBM]),
        out_shape=[
            pltpu.VMEM((KV * C, VOX // 2), BF),
            jax.ShapeDtypeStruct((KV * NQ // 2 + GROUP,), jnp.int32),
            jax.ShapeDtypeStruct((1,), jnp.int32),
            pltpu.VMEM((VOX // 2, NT), BF),
        ]
        + ([] if first else turns),
        scratch_shapes=[] if first else [pltpu.VMEM((KV, C, C), BF), DMA(())],
        compiler_params=params(),
        cost_estimate=cost(6),
        name="pick_local",
    )(*args)


def main_kernel(
    sb, pairs_a, count_a, pairs_b, count_b, rows, place, listed, flipped, features_far, sel_a,
    sel_b, sent_up, sent_down, got_up, got_down, in_a, in_b, hidden_far, up_far, pre_far, wg_far,
    pick_a, pick_b, cyc, features, hidden, up, pre, wg, sems,
):
    load = pltpu.make_async_copy(features_far, features, sems.at[0])
    load.start()
    numbers = counting(0)
    face = 4 * FACE
    below = jnp.where(place[0] > 0, got_up[:face, :].astype(F32), 0.0).astype(BF)
    above = jnp.where(place[0] < place[1] - 1, got_down[:face, :].astype(F32), 0.0).astype(BF)
    four = (below, sent_down[:face, :], sent_up[:face, :], above)
    for i in range(4):
        part = jnp.concatenate([side[i * FACE : (i + 1) * FACE, :] for side in four], 0)
        cyc[:, i * BLK : (i + 1) * BLK] = part.T

    def group(first, pairs, n, pick, i, carry):
        info, gots = [], []
        for j in range(GROUP):
            e = pairs[jnp.minimum(i * GROUP + j, n - 1)]
            info.append((e, e % ROWS, e // ROWS))
        for e, k, q in info:
            s = sb[k, q]
            t0 = pl.multiple_of((s - NLOC) * BLK, BLK)
            row = listed[pl.ds(e, 1), :] - s * BLK
            got = jnp.dot(cyc[:, pl.ds(t0, BLK)], onehot(row, numbers), preferred_element_type=F32)
            gots.append(got.astype(BF))
        for got, (e, k, q) in zip(gots, info, strict=True):
            r0 = pl.multiple_of((q - first) * BLK, BLK)
            pick[pl.ds(pl.multiple_of(k * C, C), C), pl.ds(r0, BLK)] = got
        return carry

    for first, pairs, count, pick in (
        (0, pairs_a, count_a, pick_a), (NQ // 2, pairs_b, count_b, pick_b)
    ):
        n = count[0]
        fill = functools.partial(group, first, pairs, n, pick)
        lax.fori_loop(0, (n + GROUP - 1) // GROUP, fill, 0)

    def point(first, pick, sel, p, carry):
        at = pl.ds(pl.multiple_of(first + p * WIDE, WIDE), WIDE)
        here = pl.ds(pl.multiple_of(p * WIDE, WIDE), WIDE)
        v = jnp.dot(flipped[...], pick[:, here], preferred_element_type=F32).T
        third = 3 * COARSE
        grad = jnp.zeros((WIDE, C), F32)
        for i, src in enumerate((got_up, sent_up, got_down)):
            part = sel[here, i * third : (i + 1) * third]
            grad += jnp.dot(part, src[face:, :], preferred_element_type=F32)
        sg = 1.0 / (1.0 + jnp.exp(-v))
        up[at, :] = grad.astype(BF)
        pre[at, :] = (grad * (sg * (1.0 + v * (1.0 - sg)))).astype(BF)
        out = features[at, :].astype(F32) + v * sg
        number = lax.broadcasted_iota(jnp.int32, (WIDE, C), 0) + first + p * WIDE
        hidden[at, :] = jnp.where(number < rows[0], out, 0.0).astype(BF)
        return carry

    load.wait()
    for at in ((0, pick_a, sel_a), (VOX // 2, pick_b, sel_b)):
        lax.fori_loop(0, VOX // 2 // WIDE, functools.partial(point, *at), 0)

    stores = [
        pltpu.make_async_copy(pre, pre_far, sems.at[1]),
        pltpu.make_async_copy(hidden, hidden_far, sems.at[2]),
        pltpu.make_async_copy(up, up_far, sems.at[3]),
    ]
    for store in stores:
        store.start()
    wg[KV * C :, :] = jnp.zeros((wg.shape[0] - KV * C, C), BF)
    for i, (low, high) in enumerate(((0, 9 * C), (9 * C, 18 * C), (18 * C, KV * C))):
        at = slice(low, high)
        got = jnp.dot(pick_a[at, :], pre[: VOX // 2, :], preferred_element_type=F32)
        got += jnp.dot(pick_b[at, :], pre[VOX // 2 :, :], preferred_element_type=F32)
        wg[at, :] = got.astype(BF)
        done = pl.ds(low, (high if i < 2 else wg.shape[0]) - low)
        stores.append(pltpu.make_async_copy(wg.at[done, :], wg_far.at[done, :], sems.at[4 + i]))
        stores[-1].start()
    for store in stores:
        store.wait()


def main_call(*args):
    picks = pltpu.VMEM((KV * C, VOX // 2), BF)
    return pl.pallas_call(
        main_kernel,
        in_specs=[SMEM] * 7 + [VMEM] * 2 + [HBM] + [VMEM] * 8,
        out_specs=[HBM] * 4 + [VMEM] * 2,
        out_shape=[pltpu.HBM((VOX, C), BF)] * 3 + [pltpu.HBM((32 * C, C), BF), picks, picks],
        input_output_aliases={16: 4, 17: 5},
        scratch_shapes=[
            pltpu.VMEM((C, CYC), BF),
            pltpu.VMEM((VOX, C), BF),
            pltpu.VMEM((VOX, C), BF),
            pltpu.VMEM((VOX, C), BF),
            pltpu.VMEM((VOX, C), BF),
            pltpu.VMEM((32 * C, C), BF),
            DMA((7,)),
        ],
        compiler_params=params(),
        cost_estimate=cost(15),
        name="conv_main",
    )(*args)[:4]


def table_kernel(first, size, sb, listed, pre_far, flipped_far, *refs):
    if first:
        begun, up_far, out, summed, pre, flipped, sems, up = refs
        begin = pltpu.make_async_copy(up_far, up, sems.at[5])
        begin.start()
    else:
        out, summed, pre, flipped, sems = refs
    load = pltpu.make_async_copy(
        flipped_far.at[:, pl.ds(first * C, size * C)], flipped, sems.at[0]
    )
    chunks = [
        pltpu.make_async_copy(pre_far.at[pl.ds(r, WIDE), :], pre.at[pl.ds(r, WIDE), :], sems.at[i])
        for i, r in enumerate(range(0, VOX, WIDE), 1)
    ]
    for copy in chunks:
        copy.start()
    load.start()
    numbers = counting(0)

    def scatter(q, carry):
        r0 = pl.multiple_of(q * BLK, BLK)
        grads = pre[pl.ds(r0, BLK), :]
        for k in range(size):
            row = listed[pl.ds(q * ROWS + first + k, 1), :] - sb[first + k, q] * BLK
            got = jnp.dot(onehot(row, numbers), grads, preferred_element_type=F32)
            summed[k, pl.ds(r0, BLK), :] = got.astype(BF)
        return carry

    per = WIDE // BLK
    for i, copy in enumerate(chunks):
        copy.wait()
        lax.fori_loop(i * per, (i + 1) * per, scatter, 0)
    load.wait()
    out[VOX:, :] = jnp.zeros((BLK, C), F32)
    if first:
        begin.wait()
        out[:VOX, :] = begun[:VOX, :] + up[...].astype(F32)
    else:
        out[:VOX, :] = jnp.zeros((VOX, C), F32)

    def body(i, carry):
        for j in range(3):
            k = 3 * i + j
            turned = flipped[:, pl.ds(pl.multiple_of(k * C, C), C)]
            got = jnp.dot(summed[k], turned, preferred_element_type=F32)
            for q in range(NQ):
                t0 = pl.multiple_of(jnp.minimum(sb[first + k, q], NLOC) * BLK, BLK)
                out[pl.ds(t0, BLK), :] += got[q * BLK : (q + 1) * BLK, :]
        return carry

    lax.fori_loop(0, size // 3, body, 0)


def table_call(first, last, *args):
    size = last - first
    return pl.pallas_call(
        functools.partial(table_kernel, first, size),
        in_specs=[SMEM, VMEM, HBM, HBM] + ([VMEM, HBM] if first else []),
        out_specs=VMEM,
        out_shape=pltpu.VMEM((VOX + BLK, C), F32),
        scratch_shapes=[
            pltpu.VMEM((size, VOX, C), BF),
            pltpu.VMEM((VOX, C), BF),
            pltpu.VMEM((C, size * C), BF),
            DMA((6,)),
        ]
        + ([pltpu.VMEM((VOX, C), BF)] if first else []),
        compiler_params=params(),
        cost_estimate=cost(0.1 if first else 4),
        name="table_grad",
    )(*args)


def share_kernel(parts, out):
    total = jnp.sum(parts[...].astype(F32), axis=0, keepdims=True).astype(BF)
    out[...] = jnp.broadcast_to(total, out.shape)


def share_call(parts):
    return pl.pallas_call(
        share_kernel,
        in_specs=[VMEM],
        out_specs=VMEM,
        out_shape=jax.ShapeDtypeStruct(parts.shape, BF),
        compiler_params=params(),
        cost_estimate=cost(1),
        name="share_sum",
    )(parts)


def cycle_kernel(
    sb, pairs_a, count_a, pairs_b, count_b, listed, tgt, pre_far, hidden_far, flipped_far,
    to_low, to_high, mid, inner, pre, hidden, flipped, grads, sems,
):
    loads = [
        pltpu.make_async_copy(src, dst, sems.at[i])
        for i, (src, dst) in enumerate(
            ((hidden_far, hidden), (pre_far, pre), (flipped_far, flipped))
        )
    ]
    for load in loads:
        load.start()
    size = 3 * COARSE
    numbers = counting(0)
    grads[...] = jnp.zeros(grads.shape, F32)
    loads[0].wait()
    for t in range(3):
        parts = []
        for q in range(NQ):
            row = tgt[q : q + 1, :] - float(t * size)
            parts.append(
                jnp.concatenate(
                    [onehot(row - float(j * BLK), numbers) for j in range(size // BLK)], 0
                )
            )
        got = jnp.dot(jnp.concatenate(parts, 1), hidden[...], preferred_element_type=F32)
        at = slice(t * COARSE, (t + 1) * COARSE)
        to_low[at, :] = got[:COARSE].astype(BF)
        mid[at, :] = got[COARSE : 2 * COARSE]
        to_high[at, :] = got[2 * COARSE :].astype(BF)
    loads[1].wait()
    loads[2].wait()

    def group(pairs, n, i, carry):
        info, gots = [], []
        for j in range(GROUP):
            e = pairs[jnp.minimum(i * GROUP + j, n - 1)]
            k, q = e % ROWS, e // ROWS
            s = jnp.where(i * GROUP + j < n, sb[k, q] - NLOC, NTAB - NLOC)
            info.append((e, k, q, s))
        for e, k, q, s in info:
            row = listed[pl.ds(e, 1), :] - sb[k, q] * BLK
            rows = pre[pl.ds(pl.multiple_of(q * BLK, BLK), BLK), :]
            got = jnp.dot(onehot(row, numbers), rows, preferred_element_type=F32)
            gots.append(got.astype(BF))
        outs = []
        for got, at in zip(gots, info, strict=True):
            turned = flipped[:, pl.ds(pl.multiple_of(at[1] * C, C), C)]
            outs.append(jnp.dot(got, turned, preferred_element_type=F32))
        for out, at in zip(outs, info, strict=True):
            grads[pl.ds(pl.multiple_of(at[3] * BLK, BLK), BLK), :] += out
        return carry

    for pairs, count in ((pairs_a, count_a), (pairs_b, count_b)):
        n = count[0]
        lax.fori_loop(0, (n + GROUP - 1) // GROUP, functools.partial(group, pairs, n), 0)
    to_low[size:, :] = grads[:BLK, :].astype(BF)
    to_high[size:, :] = grads[CYC - BLK : CYC, :].astype(BF)
    inner[...] = grads[BLK : CYC - BLK, :]


def cycle_call(*args):
    return pl.pallas_call(
        cycle_kernel,
        in_specs=[SMEM] * 5 + [VMEM] * 2 + [HBM] * 3,
        out_specs=[VMEM] * 4,
        out_shape=[pltpu.VMEM((3 * COARSE + BLK, C), BF)] * 2
        + [pltpu.VMEM((3 * COARSE, C), F32), pltpu.VMEM((CYC - 2 * BLK, C), F32)],
        scratch_shapes=[
            pltpu.VMEM((VOX, C), BF),
            pltpu.VMEM((VOX, C), BF),
            pltpu.VMEM((C, KV * C), BF),
            pltpu.VMEM((CYC + BLK, C), F32),
            DMA((3,)),
        ],
        compiler_params=params(),
        cost_estimate=cost(7),
        name="cycle_grad",
    )(*args)


def middle_kernel(place, mid, inner, from_low, from_high, to_down, to_up, kept, faces):
    cut = 3 * COARSE
    sums = mid[...] + from_low[:cut, :].astype(F32) + from_high[:cut, :].astype(F32)
    kept[...] = sums[COARSE : 2 * COARSE]
    to_down[:COARSE, :] = sums[:COARSE].astype(BF)
    to_up[:COARSE, :] = sums[2 * COARSE :].astype(BF)
    low = jnp.where(place[2] > 0, from_low[cut:, :].astype(F32), 0.0)
    high = jnp.where(place[2] < place[3] - 1, from_high[cut:, :].astype(F32), 0.0)
    for i, add in ((0, low), (1, high)):
        wide = inner[i * BLK : (i + 1) * BLK, :] + add
        at = slice(COARSE + i * FACE, COARSE + (i + 1) * FACE)
        to_down[at, :] = wide[:FACE].astype(BF)
        to_up[at, :] = wide[3 * FACE :].astype(BF)
        faces[i * 2 * FACE : (i + 1) * 2 * FACE, :] = wide[FACE : 3 * FACE]


def middle_call(*args):
    return pl.pallas_call(
        middle_kernel,
        in_specs=[SMEM] + [VMEM] * 4,
        out_specs=[VMEM] * 4,
        out_shape=[pltpu.VMEM((COARSE + 2 * FACE, C), BF)] * 2
        + [pltpu.VMEM((COARSE, C), F32), pltpu.VMEM((4 * FACE, C), F32)],
        compiler_params=params(),
        cost_estimate=cost(0.1),
        name="middle",
    )(*args)


def final_kernel(
    rows, place, grads, kept, faces, from_below, from_above, pooled, out
):
    sums = kept[...] + from_below[:COARSE, :].astype(F32) + from_above[:COARSE, :].astype(F32)
    pooled[...] = sums.astype(BF)
    below = jnp.where(place[0] > 0, from_below[COARSE:, :].astype(F32), 0.0)
    above = jnp.where(place[0] < place[1] - 1, from_above[COARSE:, :].astype(F32), 0.0)
    add = jnp.concatenate([below[:FACE], above[:FACE], below[FACE:], above[FACE:]], 0) + faces[...]
    number = lax.broadcasted_iota(jnp.int32, (BLK, C), 0)
    for q in range(NQ):
        at = slice(q * BLK, (q + 1) * BLK)
        total = grads[at, :]
        if q == 0:
            total += add
        out[at, :] = jnp.where(number + q * BLK < rows[0], total, 0.0).astype(BF)


def final_call(*args):
    return pl.pallas_call(
        final_kernel,
        in_specs=[SMEM] * 2 + [VMEM] * 5,
        out_specs=[VMEM] * 2,
        out_shape=[
            jax.ShapeDtypeStruct((COARSE, C), BF), jax.ShapeDtypeStruct((VOX, C), BF)
        ],
        compiler_params=params(),
        cost_estimate=cost(0.1),
        name="final",
    )(*args)


def far(array):
    return pltpu.with_memory_space_constraint(array, pltpu.HBM)


def shift(array, axis, step):
    size = lax.axis_size(axis)
    return lax.ppermute(array, axis, [(i, (i + step) % size) for i in range(size)])


def shards(features, weights, rulebook, owner_map, coarse_slot, row_count, coarse_grad):
    size_x, size_y = lax.axis_size("gx"), lax.axis_size("gy")
    devices = size_x * size_y
    place_x, place_y = lax.axis_index("gx"), lax.axis_index("gy")
    active = lax.iota(jnp.int32, VOX) < row_count[0]
    place = jnp.stack([place_y, jnp.int32(size_y), place_x, jnp.int32(size_x)])

    table, listed, sb, to_low, to_high = prepare_call(
        row_count, far(features), far(rulebook), far(coarse_grad)
    )
    from_low = shift(to_high, "gx", 1)
    from_high = shift(to_low, "gx", -1)

    owner = owner_map[:, 0]
    step_x = (owner // size_y - place_x + 1) % size_x
    step_y = (owner % size_y - place_y + 1) % size_y
    tgt = jnp.where(active, (step_y * 3 + step_x) * COARSE + coarse_slot, -1)
    tgt = tgt.reshape(NQ, BLK).astype(F32)

    first = local_call(0, sb, listed, table, tgt, far(weights))
    pick_a, pairs_a, count_a, sel_a, flipped, flipped_far = first
    flipped_far = far(flipped_far)
    from_low, from_high, pick_a = lax.optimization_barrier((from_low, from_high, pick_a))
    sent_down, sent_up = strip_call(place, to_low, to_high, from_low, from_high)
    sb_b, sent_up, sent_down = lax.optimization_barrier((sb, sent_up, sent_down))
    got_up = shift(sent_up, "gy", 1)
    got_down = shift(sent_down, "gy", -1)
    pick_b, pairs_b, count_b, sel_b = local_call(NQ // 2, sb_b, listed, table, tgt)
    lists = (pairs_a, count_a, pairs_b, count_b)

    hidden, up_grad, pre_grad, wg = main_call(
        sb, *lists, row_count, place, listed, flipped, far(features), sel_a, sel_b, sent_up,
        sent_down, got_up, got_down, pick_a, pick_b,
    )
    hidden, up_grad, pre_grad = far(hidden), far(up_grad), far(pre_grad)

    share = 32 * C // devices
    parts = lax.all_to_all(wg.reshape(devices, share, C), AXES, 0, 0, tiled=True)

    to_low, to_high, mid, inner = cycle_call(
        sb, *lists, listed, tgt, pre_grad, hidden, flipped_far
    )
    from_high = shift(to_low, "gx", -1)
    from_low = shift(to_high, "gx", 1)
    sb_b, to_low = lax.optimization_barrier((sb, to_low))
    begun = table_call(0, SPLIT, sb_b, listed, pre_grad, flipped_far)
    parts, begun, from_low, from_high = lax.optimization_barrier(
        (parts, begun, from_low, from_high)
    )
    spread = share_call(parts)
    every = lax.all_to_all(spread, AXES, 0, 0, tiled=True).reshape(32 * C, C)
    weight_grad = every[: KV * C].reshape(KV, C, C).astype(F32) * (1.0 / math.sqrt(VOX * devices))
    to_down, to_up, kept, faces = middle_call(place, mid, inner, from_low, from_high)
    sb_c, to_down, to_up, spread = lax.optimization_barrier((sb, to_down, to_up, spread))
    from_above = shift(to_down, "gy", -1)
    from_below = shift(to_up, "gy", 1)
    grads = table_call(SPLIT, KV, sb_c, listed, pre_grad, flipped_far, begun, up_grad)
    pooled, feature_grad = final_call(
        row_count, place, grads, kept, faces, from_below, from_above
    )
    return (pooled, weight_grad, feature_grad)


def solution(mesh):
    return jax.shard_map(
        shards,
        mesh=mesh,
        in_specs=(
            P(AXES, None),
            P(),
            P(None, AXES),
            P(AXES, None),
            P(AXES),
            P(AXES),
            P(AXES, None),
        ),
        out_specs=(P(AXES, None), P(), P(AXES, None)),
        check_vma=False,
    )
```

```python
import functools
import math

import jax
import jax.numpy as jnp
from jax import lax
from jax.experimental import pallas as pl
from jax.experimental.pallas import tpu as pltpu
from jax.sharding import PartitionSpec as P

BF = jnp.bfloat16
F32 = jnp.float32
AXES = ("gx", "gy")
C = 128
KV = 27
VOX = 2048
BLK = 128
NQ = VOX // BLK
ROWS = 32
FACE = 32
CYC = 16 * FACE
EXT = VOX + CYC
NLOC = VOX // BLK
NTAB = EXT // BLK
COARSE = 256
NT = 9 * COARSE
GROUP = 16
WIDE = 512
SMEM = pl.BlockSpec(memory_space=pltpu.SMEM)
VMEM = pl.BlockSpec(memory_space=pltpu.VMEM)
HBM = pl.BlockSpec(memory_space=pltpu.HBM)
DMA = pltpu.SemaphoreType.DMA


def params():
    return pltpu.CompilerParams(vmem_limit_bytes=24 << 20)


def cost(micros):
    return pl.CostEstimate(flops=0, transcendentals=0, bytes_accessed=int(micros * 3.6e6))


def counting(axis):
    return lax.broadcasted_iota(jnp.int32, (BLK, BLK), axis).astype(F32).astype(BF)


def onehot(row, numbers):
    row = jnp.broadcast_to(row.astype(F32), (BLK, BLK)).astype(BF)
    return jnp.where(row == numbers, jnp.ones((), BF), jnp.zeros((), BF))


def prepare_kernel(
    rows, features_far, rb_far, coarse_far, table, listed, blocks, to_low, to_high,
    features, rb, sems,
):
    half = 2 * FACE
    copies = [
        pltpu.make_async_copy(features_far, features, sems.at[0]),
        pltpu.make_async_copy(rb_far, rb, sems.at[1]),
        pltpu.make_async_copy(coarse_far, to_low.at[pl.ds(half, COARSE), :], sems.at[2]),
        pltpu.make_async_copy(coarse_far, to_high.at[pl.ds(half, COARSE), :], sems.at[3]),
    ]
    for copy in copies:
        copy.start()
    copies[0].wait()
    number = lax.broadcasted_iota(jnp.int32, (BLK, C), 0)
    for q in range(NQ):
        at = slice(q * BLK, (q + 1) * BLK)
        kept = jnp.where(number + q * BLK < rows[0], features[at, :].astype(F32), 0.0).astype(BF)
        table[:, at] = kept.T
        if q == 0:
            to_low[:half, :] = kept[:half]
            to_high[:half, :] = kept[half:]
    copies[1].wait()
    cols = []
    for q in range(NQ):
        part = rb[:, q * BLK : (q + 1) * BLK]
        listed[q * ROWS : q * ROWS + KV, :] = part
        low = jnp.min(part.astype(F32), axis=1, keepdims=True).astype(jnp.int32)
        cols.append(jnp.minimum(low // BLK, NTAB - 1))
    blocks[...] = jnp.concatenate(cols, 1)
    copies[2].wait()
    copies[3].wait()


def prepare_call(*args):
    return pl.pallas_call(
        prepare_kernel,
        in_specs=[SMEM] + [HBM] * 3,
        out_specs=[VMEM] * 5,
        out_shape=[
            pltpu.VMEM((C, VOX), BF),
            pltpu.VMEM((NQ * ROWS, BLK), jnp.int32),
            jax.ShapeDtypeStruct((KV, NQ), jnp.int32),
            pltpu.VMEM((2 * FACE + COARSE, C), BF),
            pltpu.VMEM((2 * FACE + COARSE, C), BF),
        ],
        scratch_shapes=[
            pltpu.VMEM((VOX, C), BF),
            pltpu.VMEM((KV, VOX), jnp.int32),
            DMA((4,)),
        ],
        compiler_params=params(),
        cost_estimate=cost(1),
        name="prepare",
    )(*args)


def strip_kernel(place, to_low, to_high, from_low, from_high, down, up):
    half = 2 * FACE
    low = jnp.where(place[2] > 0, from_low[:half, :].astype(F32), 0.0).astype(BF)
    high = jnp.where(place[2] < place[3] - 1, from_high[:half, :].astype(F32), 0.0).astype(BF)
    for i, part in enumerate((low, to_low[:half, :], to_high[:half, :], high)):
        at = slice(i * FACE, (i + 1) * FACE)
        down[at, :] = part[:FACE]
        up[at, :] = part[FACE:]
    for i, src in enumerate((from_low, to_low, from_high)):
        at = slice(4 * FACE + i * COARSE, 4 * FACE + (i + 1) * COARSE)
        down[at, :] = src[half:, :]
        up[at, :] = src[half:, :]


def strip_call(*args):
    return pl.pallas_call(
        strip_kernel,
        in_specs=[SMEM] + [VMEM] * 4,
        out_specs=[VMEM] * 2,
        out_shape=[pltpu.VMEM((4 * FACE + 3 * COARSE, C), BF)] * 2,
        compiler_params=params(),
        cost_estimate=cost(1),
        name="strip",
    )(*args)


def local_kernel(first, sb, listed, table, tgt, *refs):
    if first:
        pick, pairs, count, sel = refs
    else:
        w_far, pick, pairs, count, sel, flipped, flipped_far, w, sem = refs
        load = pltpu.make_async_copy(w_far, w, sem)
        load.start()
    numbers = counting(0)
    lanes = counting(1)
    zero = jnp.zeros((), BF)

    def body(q, n):
        r0 = pl.multiple_of((q - first) * BLK, BLK)
        for k in range(KV):
            s = sb[k, q]
            pairs[n] = q * ROWS + k
            n = n + jnp.where(s < NLOC, 0, 1)
            t0 = pl.multiple_of(jnp.minimum(s, NLOC - 1) * BLK, BLK)
            row = listed[pl.ds(q * ROWS + k, 1), :] - s * BLK
            got = jnp.dot(
                table[:, pl.ds(t0, BLK)], onehot(row, numbers), preferred_element_type=F32
            )
            pick[k * C : (k + 1) * C, pl.ds(r0, BLK)] = got.astype(BF)
        col = jnp.broadcast_to(tgt[pl.ds(q, 1), :], (BLK, BLK)).T
        tile = jnp.floor(col * (1.0 / BLK))
        hit = jnp.where((col - tile * BLK).astype(BF) == lanes, jnp.ones((), BF), zero)
        tile = tile.astype(BF)
        for t in range(NT // BLK):
            meets = tile == jnp.asarray(t, BF)
            sel[pl.ds(r0, BLK), t * BLK : (t + 1) * BLK] = jnp.where(meets, hit, zero)
        return n

    count[0] = lax.fori_loop(first, first + NQ // 2, body, 0)
    if not first:
        load.wait()
        for k in range(KV):
            flipped[:, k * C : (k + 1) * C] = w[k].T
        store = pltpu.make_async_copy(flipped, flipped_far, sem)
        store.start()
        store.wait()


def local_call(first, *args):
    turns = [pltpu.VMEM((C, KV * C), BF), pltpu.HBM((C, KV * C), BF)]
    return pl.pallas_call(
        functools.partial(local_kernel, first),
        in_specs=[SMEM, VMEM, VMEM, VMEM] + ([] if first else [HBM]),
        out_specs=[VMEM, SMEM, SMEM, VMEM] + ([] if first else [VMEM, HBM]),
        out_shape=[
            pltpu.VMEM((KV * C, VOX // 2), BF),
            jax.ShapeDtypeStruct((KV * NQ // 2 + GROUP,), jnp.int32),
            jax.ShapeDtypeStruct((1,), jnp.int32),
            pltpu.VMEM((VOX // 2, NT), BF),
        ]
        + ([] if first else turns),
        scratch_shapes=[] if first else [pltpu.VMEM((KV, C, C), BF), DMA(())],
        compiler_params=params(),
        cost_estimate=cost(6),
        name="pick_local",
    )(*args)


def main_kernel(
    sb, pairs_a, count_a, pairs_b, count_b, rows, place, listed, flipped, features_far, sel_a,
    sel_b, sent_up, sent_down, got_up, got_down, in_a, in_b, hidden_far, up_far, pre_far, wg_far,
    pick_a, pick_b, cyc, features, hidden, up, pre, wg, sems,
):
    load = pltpu.make_async_copy(features_far, features, sems.at[0])
    load.start()
    numbers = counting(0)
    face = 4 * FACE
    below = jnp.where(place[0] > 0, got_up[:face, :].astype(F32), 0.0).astype(BF)
    above = jnp.where(place[0] < place[1] - 1, got_down[:face, :].astype(F32), 0.0).astype(BF)
    four = (below, sent_down[:face, :], sent_up[:face, :], above)
    for i in range(4):
        part = jnp.concatenate([side[i * FACE : (i + 1) * FACE, :] for side in four], 0)
        cyc[:, i * BLK : (i + 1) * BLK] = part.T

    def group(first, pairs, n, pick, i, carry):
        info, gots = [], []
        for j in range(GROUP):
            e = pairs[jnp.minimum(i * GROUP + j, n - 1)]
            info.append((e, e % ROWS, e // ROWS))
        for e, k, q in info:
            s = sb[k, q]
            t0 = pl.multiple_of((s - NLOC) * BLK, BLK)
            row = listed[pl.ds(e, 1), :] - s * BLK
            got = jnp.dot(cyc[:, pl.ds(t0, BLK)], onehot(row, numbers), preferred_element_type=F32)
            gots.append(got.astype(BF))
        for got, (e, k, q) in zip(gots, info, strict=True):
            r0 = pl.multiple_of((q - first) * BLK, BLK)
            pick[pl.ds(pl.multiple_of(k * C, C), C), pl.ds(r0, BLK)] = got
        return carry

    for first, pairs, count, pick in (
        (0, pairs_a, count_a, pick_a), (NQ // 2, pairs_b, count_b, pick_b)
    ):
        n = count[0]
        fill = functools.partial(group, first, pairs, n, pick)
        lax.fori_loop(0, (n + GROUP - 1) // GROUP, fill, 0)

    def point(first, pick, sel, p, carry):
        at = pl.ds(pl.multiple_of(first + p * WIDE, WIDE), WIDE)
        here = pl.ds(pl.multiple_of(p * WIDE, WIDE), WIDE)
        v = jnp.dot(flipped[...], pick[:, here], preferred_element_type=F32).T
        third = 3 * COARSE
        grad = jnp.zeros((WIDE, C), F32)
        for i, src in enumerate((got_up, sent_up, got_down)):
            part = sel[here, i * third : (i + 1) * third]
            grad += jnp.dot(part, src[face:, :], preferred_element_type=F32)
        sg = 1.0 / (1.0 + jnp.exp(-v))
        up[at, :] = grad.astype(BF)
        pre[at, :] = (grad * (sg * (1.0 + v * (1.0 - sg)))).astype(BF)
        out = features[at, :].astype(F32) + v * sg
        number = lax.broadcasted_iota(jnp.int32, (WIDE, C), 0) + first + p * WIDE
        hidden[at, :] = jnp.where(number < rows[0], out, 0.0).astype(BF)
        return carry

    load.wait()
    for at in ((0, pick_a, sel_a), (VOX // 2, pick_b, sel_b)):
        lax.fori_loop(0, VOX // 2 // WIDE, functools.partial(point, *at), 0)

    stores = [
        pltpu.make_async_copy(pre, pre_far, sems.at[1]),
        pltpu.make_async_copy(hidden, hidden_far, sems.at[2]),
        pltpu.make_async_copy(up, up_far, sems.at[3]),
    ]
    for store in stores:
        store.start()
    wg[KV * C :, :] = jnp.zeros((wg.shape[0] - KV * C, C), BF)
    for i, (low, high) in enumerate(((0, 9 * C), (9 * C, 18 * C), (18 * C, KV * C))):
        at = slice(low, high)
        got = jnp.dot(pick_a[at, :], pre[: VOX // 2, :], preferred_element_type=F32)
        got += jnp.dot(pick_b[at, :], pre[VOX // 2 :, :], preferred_element_type=F32)
        wg[at, :] = got.astype(BF)
        done = pl.ds(low, (high if i < 2 else wg.shape[0]) - low)
        stores.append(pltpu.make_async_copy(wg.at[done, :], wg_far.at[done, :], sems.at[4 + i]))
        stores[-1].start()
    for store in stores:
        store.wait()


def main_call(*args):
    picks = pltpu.VMEM((KV * C, VOX // 2), BF)
    return pl.pallas_call(
        main_kernel,
        in_specs=[SMEM] * 7 + [VMEM] * 2 + [HBM] + [VMEM] * 8,
        out_specs=[HBM] * 4 + [VMEM] * 2,
        out_shape=[pltpu.HBM((VOX, C), BF)] * 3 + [pltpu.HBM((32 * C, C), BF), picks, picks],
        input_output_aliases={16: 4, 17: 5},
        scratch_shapes=[
            pltpu.VMEM((C, CYC), BF),
            pltpu.VMEM((VOX, C), BF),
            pltpu.VMEM((VOX, C), BF),
            pltpu.VMEM((VOX, C), BF),
            pltpu.VMEM((VOX, C), BF),
            pltpu.VMEM((32 * C, C), BF),
            DMA((7,)),
        ],
        compiler_params=params(),
        cost_estimate=cost(15),
        name="conv_main",
    )(*args)[:4]


def table_kernel(sb, listed, pre_far, flipped_far, up_far, out, summed, pre, flipped, up, sems):
    load = pltpu.make_async_copy(flipped_far, flipped, sems.at[0])
    begin = pltpu.make_async_copy(up_far, up, sems.at[5])
    chunks = [
        pltpu.make_async_copy(pre_far.at[pl.ds(r, WIDE), :], pre.at[pl.ds(r, WIDE), :], sems.at[i])
        for i, r in enumerate(range(0, VOX, WIDE), 1)
    ]
    for copy in chunks:
        copy.start()
    load.start()
    begin.start()
    numbers = counting(0)

    def scatter(q, carry):
        r0 = pl.multiple_of(q * BLK, BLK)
        grads = pre[pl.ds(r0, BLK), :]
        for k in range(KV):
            row = listed[pl.ds(q * ROWS + k, 1), :] - sb[k, q] * BLK
            got = jnp.dot(onehot(row, numbers), grads, preferred_element_type=F32)
            summed[k, pl.ds(r0, BLK), :] = got.astype(BF)
        return carry

    per = WIDE // BLK
    for i, copy in enumerate(chunks):
        copy.wait()
        lax.fori_loop(i * per, (i + 1) * per, scatter, 0)
    load.wait()
    begin.wait()
    out[:VOX, :] = up[...].astype(F32)
    out[VOX:, :] = jnp.zeros((BLK, C), F32)

    def body(i, carry):
        for j in range(3):
            k = 3 * i + j
            turned = flipped[:, pl.ds(pl.multiple_of(k * C, C), C)]
            got = jnp.dot(summed[k], turned, preferred_element_type=F32)
            for q in range(NQ):
                t0 = pl.multiple_of(jnp.minimum(sb[k, q], NLOC) * BLK, BLK)
                out[pl.ds(t0, BLK), :] += got[q * BLK : (q + 1) * BLK, :]
        return carry

    lax.fori_loop(0, KV // 3, body, 0)


def table_call(*args):
    return pl.pallas_call(
        table_kernel,
        in_specs=[SMEM, VMEM] + [HBM] * 3,
        out_specs=VMEM,
        out_shape=pltpu.VMEM((VOX + BLK, C), F32),
        scratch_shapes=[
            pltpu.VMEM((KV, VOX, C), BF),
            pltpu.VMEM((VOX, C), BF),
            pltpu.VMEM((C, KV * C), BF),
            pltpu.VMEM((VOX, C), BF),
            DMA((6,)),
        ],
        compiler_params=params(),
        cost_estimate=cost(0.1),
        name="table_grad",
    )(*args)


def share_kernel(parts, out):
    total = jnp.sum(parts[...].astype(F32), axis=0, keepdims=True).astype(BF)
    out[...] = jnp.broadcast_to(total, out.shape)


def share_call(parts):
    return pl.pallas_call(
        share_kernel,
        in_specs=[VMEM],
        out_specs=VMEM,
        out_shape=jax.ShapeDtypeStruct(parts.shape, BF),
        compiler_params=params(),
        cost_estimate=cost(1),
        name="share_sum",
    )(parts)


def cycle_kernel(
    sb, pairs_a, count_a, pairs_b, count_b, listed, tgt, pre_far, hidden_far, flipped_far,
    to_low, to_high, mid, inner, pre, hidden, flipped, grads, sems,
):
    loads = [
        pltpu.make_async_copy(src, dst, sems.at[i])
        for i, (src, dst) in enumerate(
            ((hidden_far, hidden), (pre_far, pre), (flipped_far, flipped))
        )
    ]
    for load in loads:
        load.start()
    size = 3 * COARSE
    numbers = counting(0)
    grads[...] = jnp.zeros(grads.shape, F32)
    loads[0].wait()
    for t in range(3):
        parts = []
        for q in range(NQ):
            row = tgt[q : q + 1, :] - float(t * size)
            parts.append(
                jnp.concatenate(
                    [onehot(row - float(j * BLK), numbers) for j in range(size // BLK)], 0
                )
            )
        got = jnp.dot(jnp.concatenate(parts, 1), hidden[...], preferred_element_type=F32)
        at = slice(t * COARSE, (t + 1) * COARSE)
        to_low[at, :] = got[:COARSE].astype(BF)
        mid[at, :] = got[COARSE : 2 * COARSE]
        to_high[at, :] = got[2 * COARSE :].astype(BF)
    loads[1].wait()
    loads[2].wait()

    def group(pairs, n, i, carry):
        info, gots = [], []
        for j in range(GROUP):
            e = pairs[jnp.minimum(i * GROUP + j, n - 1)]
            k, q = e % ROWS, e // ROWS
            s = jnp.where(i * GROUP + j < n, sb[k, q] - NLOC, NTAB - NLOC)
            info.append((e, k, q, s))
        for e, k, q, s in info:
            row = listed[pl.ds(e, 1), :] - sb[k, q] * BLK
            rows = pre[pl.ds(pl.multiple_of(q * BLK, BLK), BLK), :]
            got = jnp.dot(onehot(row, numbers), rows, preferred_element_type=F32)
            gots.append(got.astype(BF))
        outs = []
        for got, at in zip(gots, info, strict=True):
            turned = flipped[:, pl.ds(pl.multiple_of(at[1] * C, C), C)]
            outs.append(jnp.dot(got, turned, preferred_element_type=F32))
        for out, at in zip(outs, info, strict=True):
            grads[pl.ds(pl.multiple_of(at[3] * BLK, BLK), BLK), :] += out
        return carry

    for pairs, count in ((pairs_a, count_a), (pairs_b, count_b)):
        n = count[0]
        lax.fori_loop(0, (n + GROUP - 1) // GROUP, functools.partial(group, pairs, n), 0)
    to_low[size:, :] = grads[:BLK, :].astype(BF)
    to_high[size:, :] = grads[CYC - BLK : CYC, :].astype(BF)
    inner[...] = grads[BLK : CYC - BLK, :]


def cycle_call(*args):
    return pl.pallas_call(
        cycle_kernel,
        in_specs=[SMEM] * 5 + [VMEM] * 2 + [HBM] * 3,
        out_specs=[VMEM] * 4,
        out_shape=[pltpu.VMEM((3 * COARSE + BLK, C), BF)] * 2
        + [pltpu.VMEM((3 * COARSE, C), F32), pltpu.VMEM((CYC - 2 * BLK, C), F32)],
        scratch_shapes=[
            pltpu.VMEM((VOX, C), BF),
            pltpu.VMEM((VOX, C), BF),
            pltpu.VMEM((C, KV * C), BF),
            pltpu.VMEM((CYC + BLK, C), F32),
            DMA((3,)),
        ],
        compiler_params=params(),
        cost_estimate=cost(7),
        name="cycle_grad",
    )(*args)


def middle_kernel(place, mid, inner, from_low, from_high, to_down, to_up, kept, faces):
    cut = 3 * COARSE
    sums = mid[...] + from_low[:cut, :].astype(F32) + from_high[:cut, :].astype(F32)
    kept[...] = sums[COARSE : 2 * COARSE]
    to_down[:COARSE, :] = sums[:COARSE].astype(BF)
    to_up[:COARSE, :] = sums[2 * COARSE :].astype(BF)
    low = jnp.where(place[2] > 0, from_low[cut:, :].astype(F32), 0.0)
    high = jnp.where(place[2] < place[3] - 1, from_high[cut:, :].astype(F32), 0.0)
    for i, add in ((0, low), (1, high)):
        wide = inner[i * BLK : (i + 1) * BLK, :] + add
        at = slice(COARSE + i * FACE, COARSE + (i + 1) * FACE)
        to_down[at, :] = wide[:FACE].astype(BF)
        to_up[at, :] = wide[3 * FACE :].astype(BF)
        faces[i * 2 * FACE : (i + 1) * 2 * FACE, :] = wide[FACE : 3 * FACE]


def middle_call(*args):
    return pl.pallas_call(
        middle_kernel,
        in_specs=[SMEM] + [VMEM] * 4,
        out_specs=[VMEM] * 4,
        out_shape=[pltpu.VMEM((COARSE + 2 * FACE, C), BF)] * 2
        + [pltpu.VMEM((COARSE, C), F32), pltpu.VMEM((4 * FACE, C), F32)],
        compiler_params=params(),
        cost_estimate=cost(0.1),
        name="middle",
    )(*args)


def final_kernel(
    rows, place, grads, kept, faces, from_below, from_above, pooled, out
):
    sums = kept[...] + from_below[:COARSE, :].astype(F32) + from_above[:COARSE, :].astype(F32)
    pooled[...] = sums.astype(BF)
    below = jnp.where(place[0] > 0, from_below[COARSE:, :].astype(F32), 0.0)
    above = jnp.where(place[0] < place[1] - 1, from_above[COARSE:, :].astype(F32), 0.0)
    add = jnp.concatenate([below[:FACE], above[:FACE], below[FACE:], above[FACE:]], 0) + faces[...]
    number = lax.broadcasted_iota(jnp.int32, (BLK, C), 0)
    for q in range(NQ):
        at = slice(q * BLK, (q + 1) * BLK)
        total = grads[at, :]
        if q == 0:
            total += add
        out[at, :] = jnp.where(number + q * BLK < rows[0], total, 0.0).astype(BF)


def final_call(*args):
    return pl.pallas_call(
        final_kernel,
        in_specs=[SMEM] * 2 + [VMEM] * 5,
        out_specs=[VMEM] * 2,
        out_shape=[
            jax.ShapeDtypeStruct((COARSE, C), BF), jax.ShapeDtypeStruct((VOX, C), BF)
        ],
        compiler_params=params(),
        cost_estimate=cost(0.1),
        name="final",
    )(*args)


def far(array):
    return pltpu.with_memory_space_constraint(array, pltpu.HBM)


def shift(array, axis, step):
    size = lax.axis_size(axis)
    return lax.ppermute(array, axis, [(i, (i + step) % size) for i in range(size)])


def shards(features, weights, rulebook, owner_map, coarse_slot, row_count, coarse_grad):
    size_x, size_y = lax.axis_size("gx"), lax.axis_size("gy")
    devices = size_x * size_y
    place_x, place_y = lax.axis_index("gx"), lax.axis_index("gy")
    active = lax.iota(jnp.int32, VOX) < row_count[0]
    place = jnp.stack([place_y, jnp.int32(size_y), place_x, jnp.int32(size_x)])

    table, listed, sb, to_low, to_high = prepare_call(
        row_count, far(features), far(rulebook), far(coarse_grad)
    )
    from_low = shift(to_high, "gx", 1)
    from_high = shift(to_low, "gx", -1)

    owner = owner_map[:, 0]
    step_x = (owner // size_y - place_x + 1) % size_x
    step_y = (owner % size_y - place_y + 1) % size_y
    tgt = jnp.where(active, (step_y * 3 + step_x) * COARSE + coarse_slot, -1)
    tgt = tgt.reshape(NQ, BLK).astype(F32)

    first = local_call(0, sb, listed, table, tgt, far(weights))
    pick_a, pairs_a, count_a, sel_a, flipped, flipped_far = first
    flipped_far = far(flipped_far)
    from_low, from_high, pick_a = lax.optimization_barrier((from_low, from_high, pick_a))
    sent_down, sent_up = strip_call(place, to_low, to_high, from_low, from_high)
    sb_b, sent_up, sent_down = lax.optimization_barrier((sb, sent_up, sent_down))
    got_up = shift(sent_up, "gy", 1)
    got_down = shift(sent_down, "gy", -1)
    pick_b, pairs_b, count_b, sel_b = local_call(NQ // 2, sb_b, listed, table, tgt)
    lists = (pairs_a, count_a, pairs_b, count_b)

    hidden, up_grad, pre_grad, wg = main_call(
        sb, *lists, row_count, place, listed, flipped, far(features), sel_a, sel_b, sent_up,
        sent_down, got_up, got_down, pick_a, pick_b,
    )
    hidden, up_grad, pre_grad = far(hidden), far(up_grad), far(pre_grad)

    share = 32 * C // devices
    parts = lax.all_to_all(wg.reshape(devices, share, C), AXES, 0, 0, tiled=True)

    to_low, to_high, mid, inner = cycle_call(
        sb, *lists, listed, tgt, pre_grad, hidden, flipped_far
    )
    from_high = shift(to_low, "gx", -1)
    from_low = shift(to_high, "gx", 1)
    spread = share_call(parts)
    spread, from_low, from_high = lax.optimization_barrier((spread, from_low, from_high))
    every = lax.all_to_all(spread, AXES, 0, 0, tiled=True).reshape(32 * C, C)
    weight_grad = every[: KV * C].reshape(KV, C, C).astype(F32) * (1.0 / math.sqrt(VOX * devices))
    to_down, to_up, kept, faces = middle_call(place, mid, inner, from_low, from_high)
    sb_c, to_down, to_up, spread = lax.optimization_barrier((sb, to_down, to_up, spread))
    from_above = shift(to_down, "gy", -1)
    from_below = shift(to_up, "gy", 1)
    grads = table_call(sb_c, listed, pre_grad, flipped_far, up_grad)
    pooled, feature_grad = final_call(
        row_count, place, grads, kept, faces, from_below, from_above
    )
    return (pooled, weight_grad, feature_grad)


def solution(mesh):
    return jax.shard_map(
        shards,
        mesh=mesh,
        in_specs=(
            P(AXES, None),
            P(),
            P(None, AXES),
            P(AXES, None),
            P(AXES),
            P(AXES),
            P(AXES, None),
        ),
        out_specs=(P(AXES, None), P(), P(AXES, None)),
        check_vma=False,
    )
```
